128 devices in a mesh: dp: 16 (over x, y), expert: 8 (over z, core).
Axes of the slice: x: 4, y: 4, z: 4, core: 2. Of those that a mesh axis runs over, the one named last changes fastest.
Arguments:
- context: bfloat16 [8192, 4096], P('dp'), may hold values from -6 to 6
- out_weight: bfloat16 [4096, 4096], P('dp', 'expert'), may hold values from -0.09375 to 0.09375
- residual: bfloat16 [8192, 4096], P('dp', 'expert'), may hold values from -6 to 6
- gate_weight: bfloat16 [8, 4096, 8192], P('expert', None, 'dp'), may hold values from -0.09375 to 0.09375
- up_weight: bfloat16 [8, 4096, 8192], P('expert', None, 'dp'), may hold values from -0.09375 to 0.09375
- down_weight: bfloat16 [8, 8192, 4096], P('expert', 'dp'), may hold values from -0.0625 to 0.0625
- gate_values: float32 [8, 512], P('expert'), may hold values from 0.2 to 1
- chosen_blocks: int32 [8, 4], replicated, may hold values from 0 to 63, as said below
- block_counts: int32 [8], replicated, may hold values from 1 to 4, as said below
Outputs:
- mixed: bfloat16 [8192, 4096], P('dp', 'expert')
The draws below stay inside these ranges and needn't reach their ends.
Inputs may be any that keep to these rules, and one draw needn't show every extreme that they name: `chosen_blocks`: within one expert the 4 block numbers are distinct; slots from block_counts on are unused but hold valid block numbers. `block_counts`: some expert uses all 4 slots.
All inputs are finite; a program needn't handle non-finite values.
Results may differ from the reference program's by a relative error of at most 0.008.
Values may be sent and summed in bfloat16 or wider, within the bound.
A program may use at most 128 MiB of HBM per device.

```python
import jax
import jax.numpy as jnp
from jax import lax

D = 4096
FF = 8192
BLK = 128
CAP = 4
EXPERTS = 8
NBLK = 64
TOKENS = 8192
N_DP = 16


def draw_chosen_blocks(key, part):
    first, second, third = jax.random.split(key, 3)
    keys = jax.random.split(first, EXPERTS)
    orders = jax.vmap(lambda single: jax.random.permutation(single, NBLK))(keys)[:, :CAP]
    middle = 1 + jax.random.permutation(second, NBLK - 2)[:CAP - 2]
    ends = jnp.concatenate([jnp.array([0, NBLK - 1], jnp.int32), middle.astype(jnp.int32)])
    target = jax.random.randint(third, (), 0, EXPERTS)
    rows = jnp.where(jnp.arange(EXPERTS)[:, None] == target, ends[None, :], orders)
    return rows.astype(jnp.int32)


def draw_block_counts(key, part):
    first, second, third = jax.random.split(key, 3)
    heavy = jax.random.randint(first, (EXPERTS,), 0, 4) == 0
    light = jnp.minimum(jax.random.randint(second, (EXPERTS,), 1, 3), CAP)
    counts = jnp.where(heavy, CAP, light)
    target = jax.random.randint(third, (), 0, EXPERTS)
    counts = jnp.where(jnp.arange(EXPERTS) == target, CAP, counts)
    counts = jnp.where(jnp.arange(EXPERTS) == (target + 1) % EXPERTS, 1, counts)
    return counts.astype(jnp.int32)


def shard_levels(own_key, extent, cuts, low, top_value):
    def one(position, blocks):
        draws = jax.random.uniform(jax.random.fold_in(jax.random.fold_in(own_key, 6), position), (blocks,), jnp.float32, low / len(cuts), top_value / len(cuts))
        return jnp.repeat(jnp.exp(draws), extent[position] // blocks).reshape((-1,) + (1,) * (len(extent) - position - 1))

    level = one(*cuts[0])
    for cut in cuts[1:]:
        level = level * one(*cut)
    return level


def noise(own_key, extent, spread, reach, cuts=(), kind=jnp.bfloat16):
    drawn = jax.random.normal(own_key, extent, jnp.float32) * spread
    if len(cuts) > 0:
        drawn = shard_levels(own_key, extent, cuts, -0.22, 0.18) * drawn
    return jnp.clip(drawn, min=-reach, max=reach).astype(kind)


def setup_inputs(seed: int = 0) -> dict:
    seeds = jax.random.split(jax.random.key(seed), 10)
    return {
        "context": noise(seeds[0], (TOKENS, D), 1.0, 6.0, ((0, 16),)),
        "out_weight": noise(seeds[1], (D, D), D ** -0.5, 0.09375, ((0, 16), (1, 8))),
        "residual": noise(seeds[2], (TOKENS, D), 1.0, 6.0, ((0, 16), (1, 8))),
        "gate_weight": noise(seeds[3], (EXPERTS, D, FF), D ** -0.5, 0.09375, ((0, 8), (2, 16))),
        "up_weight": noise(seeds[4], (EXPERTS, D, FF), D ** -0.5, 0.09375, ((0, 8), (2, 16))),
        "down_weight": noise(seeds[5], (EXPERTS, FF, D), FF ** -0.5, 0.0625, ((0, 8), (1, 16))),
        "gate_values": jnp.clip(0.2 + 0.8 * jax.random.uniform(seeds[6], (EXPERTS, CAP * BLK), jnp.float32) ** shard_levels(seeds[6], (EXPERTS, CAP * BLK), ((0, 8),), -0.2, 0.2), 0.2, 1.0),
        "chosen_blocks": draw_chosen_blocks(jax.random.fold_in(seeds[9], 71), 0),
        "block_counts": draw_block_counts(jax.random.fold_in(seeds[9], 71), 0),
    }


def reference(context, out_weight, residual, gate_weight, up_weight, down_weight, gate_values, chosen_blocks, block_counts):
    attended = (residual.astype(jnp.float32) + jnp.dot(context, out_weight, preferred_element_type=jnp.float32)).astype(jnp.bfloat16)
    blocks = attended.reshape(NBLK, BLK, D)
    width = FF // N_DP

    def one_expert(inputs):
        w_gate, w_up, w_down, gate_row, block_list, count = inputs
        picked = blocks[block_list].reshape(CAP * BLK, D)
        gate = jnp.dot(picked, w_gate, preferred_element_type=jnp.float32)
        upper = jnp.dot(picked, w_up, preferred_element_type=jnp.float32)
        hidden = (jax.nn.silu(gate) * upper).astype(jnp.bfloat16)
        live = (jnp.arange(CAP * BLK) // BLK) < count
        scale = jnp.where(live, gate_row, jnp.zeros_like(gate_row))[:, None]
        total = jnp.zeros((CAP * BLK, D), jnp.float32)
        for slice_index in range(N_DP):
            part = jnp.dot(hidden[:, slice_index * width:(slice_index + 1) * width], w_down[slice_index * width:(slice_index + 1) * width], preferred_element_type=jnp.float32)
            rounded = lax.optimization_barrier((part * scale).astype(jnp.bfloat16))
            total = total + rounded.astype(jnp.float32)
        return total.astype(jnp.bfloat16)

    outputs = lax.map(one_expert, (gate_weight, up_weight, down_weight, gate_values, chosen_blocks, block_counts))
    summed = attended.astype(jnp.float32).reshape(NBLK, BLK, D)
    summed = summed.at[chosen_blocks.reshape(-1)].add(outputs.reshape(EXPERTS * CAP, BLK, D).astype(jnp.float32))
    return summed.reshape(TOKENS, D).astype(jnp.bfloat16)
```

```python
import jax
import jax.numpy as jnp
from jax import lax
from jax.sharding import PartitionSpec as P

BLK = 128
CAP = 4


def body(
    context,
    out_weight,
    residual,
    gate_weight,
    up_weight,
    down_weight,
    gate_values,
    chosen_blocks,
    block_counts,
):
    n_dp = lax.axis_size("dp")
    n_expert = lax.axis_size("expert")
    local_tokens = context.shape[0]
    local_width = residual.shape[1]
    model_width = context.shape[1]
    local_blocks = local_tokens // BLK
    n_blocks = local_blocks * n_dp
    piece = BLK // n_dp
    my_expert = lax.axis_index("expert")

    projected = jnp.dot(
        context,
        lax.all_gather(out_weight, "dp", axis=0, tiled=True),
        preferred_element_type=jnp.float32,
    )
    attended = (residual.astype(jnp.float32) + projected).astype(jnp.bfloat16)

    split = attended.reshape(local_blocks, n_dp, piece, local_width).transpose(1, 0, 2, 3)
    pieces = lax.all_to_all(split, "dp", 0, 0, tiled=True)
    pieces = pieces.reshape(n_blocks, piece, local_width)

    slots = jnp.take(pieces, chosen_blocks.reshape(-1), axis=0)
    slots = slots.reshape(n_expert, CAP, piece, local_width)
    mine = lax.all_to_all(slots, "expert", 0, 3, tiled=True)
    mine = mine.reshape(CAP * piece, model_width)
    picked = lax.all_gather(mine, "dp", axis=0, tiled=True)

    w_gate = gate_weight[0]
    w_up = up_weight[0]
    w_down = down_weight[0]
    gate_row = gate_values[0]
    my_count = lax.dynamic_index_in_dim(block_counts, my_expert, 0, keepdims=False)
    live = jnp.arange(CAP * BLK) // BLK < my_count
    scale = jnp.where(live, gate_row, jnp.zeros_like(gate_row))
    scale = scale.reshape(CAP, n_dp, piece).transpose(1, 0, 2).reshape(-1)

    gate = jnp.dot(picked, w_gate, preferred_element_type=jnp.float32)
    upper = jnp.dot(picked, w_up, preferred_element_type=jnp.float32)
    hidden = (jax.nn.silu(gate) * upper).astype(jnp.bfloat16)
    part = jnp.dot(hidden, w_down, preferred_element_type=jnp.float32)
    part = (part * scale[:, None]).astype(jnp.bfloat16)

    summed = lax.psum_scatter(
        part.reshape(n_dp, CAP * piece, model_width), "dp", scatter_dimension=0, tiled=True
    )
    summed = summed.reshape(CAP * piece, n_expert, local_width).transpose(1, 0, 2)
    outs = lax.all_to_all(summed, "expert", 0, 0, tiled=True)
    outs = outs.reshape(n_expert * CAP, piece * local_width)

    selector = chosen_blocks.reshape(-1)[None, :] == jnp.arange(n_blocks)[:, None]
    added = jnp.dot(selector.astype(jnp.bfloat16), outs, preferred_element_type=jnp.float32)
    added = added.reshape(n_dp, local_blocks, piece, local_width)
    back = lax.all_to_all(added, "dp", 0, 0, tiled=True)
    back = back.transpose(1, 0, 2, 3).reshape(local_tokens, local_width)

    total = attended.astype(jnp.float32) + back
    return total.astype(jnp.bfloat16)


def solution(mesh):
    in_specs = (
        P("dp", None),
        P("dp", "expert"),
        P("dp", "expert"),
        P("expert", None, "dp"),
        P("expert", None, "dp"),
        P("expert", "dp", None),
        P("expert", None),
        P(),
        P(),
    )
    out_specs = P("dp", "expert")
    return jax.shard_map(body, mesh=mesh, in_specs=in_specs, out_specs=out_specs, check_vma=False)
```

```python
import functools

import jax
import jax.numpy as jnp
from jax import lax
from jax.sharding import PartitionSpec as P
from jax.experimental import pallas as pl
from jax.experimental.pallas import tpu as pltpu

BLK = 128
CAP = 4


def _exchange_kernel(n, gather, x_ref, o_ref, local_sem, send_sems, recv_sems):
    me = lax.axis_index("dp")
    mesh_id = pl.DeviceIdType.MESH
    barrier = pltpu.get_barrier_semaphore()
    for k in range(1, n):
        pl.semaphore_signal(barrier, 1, device_id={"dp": lax.rem(me + k, n)}, device_id_type=mesh_id)
    pl.semaphore_wait(barrier, n - 1)
    local = pltpu.make_async_copy(x_ref if gather else x_ref.at[me], o_ref.at[me], local_sem)
    local.start()
    copies = []
    for k in range(1, n):
        target = lax.rem(me + k, n)
        copy = pltpu.make_async_remote_copy(
            src_ref=x_ref if gather else x_ref.at[target],
            dst_ref=o_ref.at[me],
            send_sem=send_sems.at[k - 1],
            recv_sem=recv_sems.at[k - 1],
            device_id={"dp": target},
            device_id_type=mesh_id,
        )
        copy.start()
        copies.append(copy)
    local.wait()
    for copy in copies:
        copy.wait()


def dp_exchange(x, gather, cid):
    n = lax.axis_size("dp")
    shape = (n,) + x.shape if gather else x.shape
    return pl.pallas_call(
        functools.partial(_exchange_kernel, n, gather),
        out_shape=jax.ShapeDtypeStruct(shape, x.dtype),
        in_specs=[pl.BlockSpec(memory_space=pl.ANY)],
        out_specs=pl.BlockSpec(memory_space=pl.ANY),
        scratch_shapes=[
            pltpu.SemaphoreType.DMA(()),
            pltpu.SemaphoreType.DMA((n - 1,)),
            pltpu.SemaphoreType.DMA((n - 1,)),
        ],
        compiler_params=pltpu.CompilerParams(collective_id=cid, has_side_effects=True),
    )(x)


def body(
    context,
    out_weight,
    residual,
    gate_weight,
    up_weight,
    down_weight,
    gate_values,
    chosen_blocks,
    block_counts,
):
    n_dp = lax.axis_size("dp")
    n_expert = lax.axis_size("expert")
    local_tokens = context.shape[0]
    local_width = residual.shape[1]
    model_width = context.shape[1]
    local_blocks = local_tokens // BLK
    n_blocks = local_blocks * n_dp
    piece = BLK // n_dp
    my_expert = lax.axis_index("expert")

    projected = jnp.dot(
        context,
        lax.all_gather(out_weight, "dp", axis=0, tiled=True),
        preferred_element_type=jnp.float32,
    )
    attended = (residual.astype(jnp.float32) + projected).astype(jnp.bfloat16)

    split = attended.reshape(local_blocks, n_dp, piece, local_width).transpose(1, 0, 2, 3)
    pieces = dp_exchange(split, gather=False, cid=0)
    pieces = pieces.reshape(n_blocks, piece, local_width)

    slots = jnp.take(pieces, chosen_blocks.reshape(-1), axis=0)
    slots = slots.reshape(n_expert, CAP, piece, local_width)
    mine = lax.all_to_all(slots, "expert", 0, 3, tiled=True)
    mine = mine.reshape(CAP * piece, model_width)
    picked = lax.all_gather(mine, "dp", axis=0, tiled=True)

    w_gate = gate_weight[0]
    w_up = up_weight[0]
    w_down = down_weight[0]
    gate_row = gate_values[0]
    my_count = lax.dynamic_index_in_dim(block_counts, my_expert, 0, keepdims=False)
    live = jnp.arange(CAP * BLK) // BLK < my_count
    scale = jnp.where(live, gate_row, jnp.zeros_like(gate_row))
    scale = scale.reshape(CAP, n_dp, piece).transpose(1, 0, 2).reshape(-1)

    gate = jnp.dot(picked, w_gate, preferred_element_type=jnp.float32)
    upper = jnp.dot(picked, w_up, preferred_element_type=jnp.float32)
    hidden = (jax.nn.silu(gate) * upper).astype(jnp.bfloat16)
    part = jnp.dot(hidden, w_down, preferred_element_type=jnp.float32)
    part = (part * scale[:, None]).astype(jnp.bfloat16)

    terms = dp_exchange(part.reshape(n_dp, CAP * piece, model_width), gather=False, cid=1)
    summed = terms.astype(jnp.float32).sum(axis=0).astype(jnp.bfloat16)
    summed = summed.reshape(CAP * piece, n_expert, local_width).transpose(1, 0, 2)
    outs = lax.all_to_all(summed, "expert", 0, 0, tiled=True)
    outs = outs.reshape(n_expert * CAP, piece * local_width)

    selector = chosen_blocks.reshape(-1)[None, :] == jnp.arange(n_blocks)[:, None]
    added = jnp.dot(selector.astype(jnp.bfloat16), outs, preferred_element_type=jnp.float32)
    added = added.reshape(n_dp, local_blocks, piece, local_width)
    back = dp_exchange(added, gather=False, cid=2)
    back = back.transpose(1, 0, 2, 3).reshape(local_tokens, local_width)

    total = attended.astype(jnp.float32) + back
    return total.astype(jnp.bfloat16)


def solution(mesh):
    in_specs = (
        P("dp", None),
        P("dp", "expert"),
        P("dp", "expert"),
        P("expert", None, "dp"),
        P("expert", None, "dp"),
        P("expert", "dp", None),
        P("expert", None),
        P(),
        P(),
    )
    out_specs = P("dp", "expert")
    return jax.shard_map(body, mesh=mesh, in_specs=in_specs, out_specs=out_specs, check_vma=False)
```

```python
import functools

import jax
import jax.numpy as jnp
from jax import lax
from jax.sharding import PartitionSpec as P
from jax.experimental import pallas as pl
from jax.experimental.pallas import tpu as pltpu

BLK = 128
CAP = 4


def _exchange_kernel(n, gather, x_ref, o_ref, local_sem, send_sems, recv_sems):
    me = lax.axis_index("dp")
    mesh_id = pl.DeviceIdType.MESH
    barrier = pltpu.get_barrier_semaphore()
    for k in range(1, n):
        pl.semaphore_signal(barrier, 1, device_id={"dp": lax.rem(me + k, n)}, device_id_type=mesh_id)
    pl.semaphore_wait(barrier, n - 1)
    local = pltpu.make_async_copy(x_ref if gather else x_ref.at[me], o_ref.at[me], local_sem)
    local.start()
    copies = []
    for k in range(1, n):
        target = lax.rem(me + k, n)
        copy = pltpu.make_async_remote_copy(
            src_ref=x_ref if gather else x_ref.at[target],
            dst_ref=o_ref.at[me],
            send_sem=send_sems.at[k - 1],
            recv_sem=recv_sems.at[k - 1],
            device_id={"dp": target},
            device_id_type=mesh_id,
        )
        copy.start()
        copies.append(copy)
    local.wait()
    for copy in copies:
        copy.wait()


def dp_exchange(x, gather, cid):
    n = lax.axis_size("dp")
    shape = (n,) + x.shape if gather else x.shape
    return pl.pallas_call(
        functools.partial(_exchange_kernel, n, gather),
        out_shape=jax.ShapeDtypeStruct(shape, x.dtype),
        in_specs=[pl.BlockSpec(memory_space=pl.ANY)],
        out_specs=pl.BlockSpec(memory_space=pl.ANY),
        scratch_shapes=[
            pltpu.SemaphoreType.DMA(()),
            pltpu.SemaphoreType.DMA((n - 1,)),
            pltpu.SemaphoreType.DMA((n - 1,)),
        ],
        compiler_params=pltpu.CompilerParams(collective_id=cid, has_side_effects=True),
    )(x)


def _route_kernel(strides, side, *refs):
    n_in = len(strides)
    ins, outs = refs[:n_in], refs[n_in:2 * n_in]
    local_sems, send_sems, recv_sems = refs[2 * n_in:]
    me = lax.axis_index("dp")
    mesh_id = pl.DeviceIdType.MESH
    routes = []
    for r, stride in enumerate(strides):
        coord = lax.rem(me // stride, side)
        base = me - coord * stride
        for k in range(1, side):
            to = lax.rem(coord + k, side)
            routes.append((r, coord, to, base + to * stride))
    barrier = pltpu.get_barrier_semaphore()
    for _, _, _, target in routes:
        pl.semaphore_signal(barrier, 1, device_id={"dp": target}, device_id_type=mesh_id)
    pl.semaphore_wait(barrier, len(routes))
    locals_ = []
    for r in range(n_in):
        coord = lax.rem(me // strides[r], side)
        local = pltpu.make_async_copy(ins[r].at[coord], outs[r].at[coord], local_sems.at[r])
        local.start()
        locals_.append(local)
    copies = []
    for i, (r, coord, to, target) in enumerate(routes):
        copy = pltpu.make_async_remote_copy(
            src_ref=ins[r].at[to],
            dst_ref=outs[r].at[coord],
            send_sem=send_sems.at[i],
            recv_sem=recv_sems.at[i],
            device_id={"dp": target},
            device_id_type=mesh_id,
        )
        copy.start()
        copies.append(copy)
    for local in locals_:
        local.wait()
    for copy in copies:
        copy.wait()


def dp_route(xs, strides, cid, side=4):
    n_routes = len(strides) * (side - 1)
    return pl.pallas_call(
        functools.partial(_route_kernel, tuple(strides), side),
        out_shape=[jax.ShapeDtypeStruct(x.shape, x.dtype) for x in xs],
        in_specs=[pl.BlockSpec(memory_space=pl.ANY)] * len(xs),
        out_specs=[pl.BlockSpec(memory_space=pl.ANY)] * len(xs),
        scratch_shapes=[
            pltpu.SemaphoreType.DMA((len(xs),)),
            pltpu.SemaphoreType.DMA((n_routes,)),
            pltpu.SemaphoreType.DMA((n_routes,)),
        ],
        compiler_params=pltpu.CompilerParams(collective_id=cid, has_side_effects=True),
    )(*xs)


def reduce_scatter_2d(part, cid):
    side = 4
    n_dp, rows, cols = part.shape
    half = cols // 2
    grid = part.reshape(side, side, rows, cols)
    first_a = grid[..., :half].transpose(1, 0, 2, 3)
    first_b = grid[..., half:]
    got_a, got_b = dp_route([first_a, first_b], (1, side), cid)
    second_a = got_a.astype(jnp.float32).sum(axis=0).astype(jnp.bfloat16)
    second_b = got_b.astype(jnp.float32).sum(axis=0).astype(jnp.bfloat16)
    got_a, got_b = dp_route([second_a, second_b], (side, 1), cid + 1)
    total_a = got_a.astype(jnp.float32).sum(axis=0)
    total_b = got_b.astype(jnp.float32).sum(axis=0)
    return jnp.concatenate([total_a, total_b], axis=-1)


def body(
    context,
    out_weight,
    residual,
    gate_weight,
    up_weight,
    down_weight,
    gate_values,
    chosen_blocks,
    block_counts,
):
    n_dp = lax.axis_size("dp")
    n_expert = lax.axis_size("expert")
    local_tokens = context.shape[0]
    local_width = residual.shape[1]
    model_width = context.shape[1]
    local_blocks = local_tokens // BLK
    n_blocks = local_blocks * n_dp
    piece = BLK // n_dp
    my_expert = lax.axis_index("expert")

    projected = jnp.dot(
        context,
        lax.all_gather(out_weight, "dp", axis=0, tiled=True),
        preferred_element_type=jnp.float32,
    )
    attended = (residual.astype(jnp.float32) + projected).astype(jnp.bfloat16)

    split = attended.reshape(local_blocks, n_dp, piece, local_width).transpose(1, 0, 2, 3)
    pieces = dp_exchange(split, gather=False, cid=0)
    pieces = pieces.reshape(n_blocks, piece, local_width)

    slots = jnp.take(pieces, chosen_blocks.reshape(-1), axis=0)
    slots = slots.reshape(n_expert, CAP, piece, local_width)
    mine = lax.all_to_all(slots, "expert", 0, 3, tiled=True)
    mine = mine.reshape(CAP * piece, model_width)
    picked = lax.all_gather(mine, "dp", axis=0, tiled=True)

    w_gate = gate_weight[0]
    w_up = up_weight[0]
    w_down = down_weight[0]
    gate_row = gate_values[0]
    my_count = lax.dynamic_index_in_dim(block_counts, my_expert, 0, keepdims=False)
    live = jnp.arange(CAP * BLK) // BLK < my_count
    scale = jnp.where(live, gate_row, jnp.zeros_like(gate_row))
    scale = scale.reshape(CAP, n_dp, piece).transpose(1, 0, 2).reshape(-1)

    gate = jnp.dot(picked, w_gate, preferred_element_type=jnp.float32)
    upper = jnp.dot(picked, w_up, preferred_element_type=jnp.float32)
    hidden = (jax.nn.silu(gate) * upper).astype(jnp.bfloat16)
    part = jnp.dot(hidden, w_down, preferred_element_type=jnp.float32)
    part = (part * scale[:, None]).astype(jnp.bfloat16)

    summed = reduce_scatter_2d(part.reshape(n_dp, CAP * piece, model_width), cid=1)
    summed = summed.astype(jnp.bfloat16)
    summed = summed.reshape(CAP * piece, n_expert, local_width).transpose(1, 0, 2)
    outs = lax.all_to_all(summed, "expert", 0, 0, tiled=True)
    outs = outs.reshape(n_expert * CAP, piece * local_width)

    selector = chosen_blocks.reshape(-1)[None, :] == jnp.arange(n_blocks)[:, None]
    added = jnp.dot(selector.astype(jnp.bfloat16), outs, preferred_element_type=jnp.float32)
    added = added.reshape(n_dp, local_blocks, piece, local_width)
    back = lax.all_to_all(added, "dp", 0, 0, tiled=True)
    back = back.transpose(1, 0, 2, 3).reshape(local_tokens, local_width)

    total = attended.astype(jnp.float32) + back
    return total.astype(jnp.bfloat16)


def solution(mesh):
    in_specs = (
        P("dp", None),
        P("dp", "expert"),
        P("dp", "expert"),
        P("expert", None, "dp"),
        P("expert", None, "dp"),
        P("expert", "dp", None),
        P("expert", None),
        P(),
        P(),
    )
    out_specs = P("dp", "expert")
    return jax.shard_map(body, mesh=mesh, in_specs=in_specs, out_specs=out_specs, check_vma=False)
```

```python
import functools

import jax
import jax.numpy as jnp
from jax import lax
from jax.sharding import PartitionSpec as P
from jax.experimental import pallas as pl
from jax.experimental.pallas import tpu as pltpu

BLK = 128
CAP = 4


def _exchange_kernel(n, gather, x_ref, o_ref, local_sem, send_sems, recv_sems):
    me = lax.axis_index("dp")
    mesh_id = pl.DeviceIdType.MESH
    barrier = pltpu.get_barrier_semaphore()
    for k in range(1, n):
        pl.semaphore_signal(barrier, 1, device_id={"dp": lax.rem(me + k, n)}, device_id_type=mesh_id)
    pl.semaphore_wait(barrier, n - 1)
    local = pltpu.make_async_copy(x_ref if gather else x_ref.at[me], o_ref.at[me], local_sem)
    local.start()
    copies = []
    for k in range(1, n):
        target = lax.rem(me + k, n)
        copy = pltpu.make_async_remote_copy(
            src_ref=x_ref if gather else x_ref.at[target],
            dst_ref=o_ref.at[me],
            send_sem=send_sems.at[k - 1],
            recv_sem=recv_sems.at[k - 1],
            device_id={"dp": target},
            device_id_type=mesh_id,
        )
        copy.start()
        copies.append(copy)
    local.wait()
    for copy in copies:
        copy.wait()


def dp_exchange(x, gather, cid):
    n = lax.axis_size("dp")
    shape = (n,) + x.shape if gather else x.shape
    return pl.pallas_call(
        functools.partial(_exchange_kernel, n, gather),
        out_shape=jax.ShapeDtypeStruct(shape, x.dtype),
        in_specs=[pl.BlockSpec(memory_space=pl.ANY)],
        out_specs=pl.BlockSpec(memory_space=pl.ANY),
        scratch_shapes=[
            pltpu.SemaphoreType.DMA(()),
            pltpu.SemaphoreType.DMA((n - 1,)),
            pltpu.SemaphoreType.DMA((n - 1,)),
        ],
        compiler_params=pltpu.CompilerParams(collective_id=cid, has_side_effects=True),
    )(x)


def _route_kernel(strides, side, gather, *refs):
    n_in = len(strides)
    ins, outs = refs[:n_in], refs[n_in:2 * n_in]
    local_sems, send_sems, recv_sems = refs[2 * n_in:]
    me = lax.axis_index("dp")
    mesh_id = pl.DeviceIdType.MESH
    routes = []
    for r, stride in enumerate(strides):
        coord = lax.rem(me // stride, side)
        base = me - coord * stride
        for k in range(1, side):
            to = lax.rem(coord + k, side)
            routes.append((r, coord, to, base + to * stride))
    barrier = pltpu.get_barrier_semaphore()
    for _, _, _, target in routes:
        pl.semaphore_signal(barrier, 1, device_id={"dp": target}, device_id_type=mesh_id)
    pl.semaphore_wait(barrier, len(routes))
    locals_ = []
    for r in range(n_in):
        coord = lax.rem(me // strides[r], side)
        source = ins[r] if gather else ins[r].at[coord]
        local = pltpu.make_async_copy(source, outs[r].at[coord], local_sems.at[r])
        local.start()
        locals_.append(local)
    copies = []
    for i, (r, coord, to, target) in enumerate(routes):
        copy = pltpu.make_async_remote_copy(
            src_ref=ins[r] if gather else ins[r].at[to],
            dst_ref=outs[r].at[coord],
            send_sem=send_sems.at[i],
            recv_sem=recv_sems.at[i],
            device_id={"dp": target},
            device_id_type=mesh_id,
        )
        copy.start()
        copies.append(copy)
    for local in locals_:
        local.wait()
    for copy in copies:
        copy.wait()


def dp_route(xs, strides, cid, side=4, gather=False):
    n_routes = len(strides) * (side - 1)
    shapes = [((side,) + x.shape) if gather else x.shape for x in xs]
    return pl.pallas_call(
        functools.partial(_route_kernel, tuple(strides), side, gather),
        out_shape=[jax.ShapeDtypeStruct(s, x.dtype) for s, x in zip(shapes, xs)],
        in_specs=[pl.BlockSpec(memory_space=pl.ANY)] * len(xs),
        out_specs=[pl.BlockSpec(memory_space=pl.ANY)] * len(xs),
        scratch_shapes=[
            pltpu.SemaphoreType.DMA((len(xs),)),
            pltpu.SemaphoreType.DMA((n_routes,)),
            pltpu.SemaphoreType.DMA((n_routes,)),
        ],
        compiler_params=pltpu.CompilerParams(collective_id=cid, has_side_effects=True),
    )(*xs)


def reduce_scatter_2d(part, cid):
    side = 4
    n_dp, rows, cols = part.shape
    half = cols // 2
    grid = part.reshape(side, side, rows, cols)
    first_a = grid[..., :half].transpose(1, 0, 2, 3)
    first_b = grid[..., half:]
    got_a, got_b = dp_route([first_a, first_b], (1, side), cid)
    second_a = got_a.astype(jnp.float32).sum(axis=0).astype(jnp.bfloat16)
    second_b = got_b.astype(jnp.float32).sum(axis=0).astype(jnp.bfloat16)
    got_a, got_b = dp_route([second_a, second_b], (side, 1), cid + 1)
    total_a = got_a.astype(jnp.float32).sum(axis=0)
    total_b = got_b.astype(jnp.float32).sum(axis=0)
    return jnp.concatenate([total_a, total_b], axis=-1)


def all_gather_2d(x, cid):
    side = 4
    half = x.shape[-1] // 2
    got_a, got_b = dp_route([x[..., :half], x[..., half:]], (1, side), cid, gather=True)
    got_a, got_b = dp_route([got_a, got_b], (side, 1), cid + 1, gather=True)
    n = side * side
    got_a = got_a.reshape((n,) + got_a.shape[2:])
    perm = (1, 0) + tuple(range(2, got_b.ndim))
    got_b = got_b.transpose(perm).reshape((n,) + got_b.shape[2:])
    return got_a, got_b


def body(
    context,
    out_weight,
    residual,
    gate_weight,
    up_weight,
    down_weight,
    gate_values,
    chosen_blocks,
    block_counts,
):
    n_dp = lax.axis_size("dp")
    n_expert = lax.axis_size("expert")
    local_tokens = context.shape[0]
    local_width = residual.shape[1]
    model_width = context.shape[1]
    local_blocks = local_tokens // BLK
    n_blocks = local_blocks * n_dp
    piece = BLK // n_dp
    my_expert = lax.axis_index("expert")

    w_a, w_b = all_gather_2d(out_weight, cid=10)
    w_a = w_a.reshape(model_width, -1)
    w_b = w_b.reshape(model_width, -1)
    projected = jnp.concatenate(
        [
            jnp.dot(context, w_a, preferred_element_type=jnp.float32),
            jnp.dot(context, w_b, preferred_element_type=jnp.float32),
        ],
        axis=1,
    )
    attended = (residual.astype(jnp.float32) + projected).astype(jnp.bfloat16)

    split = attended.reshape(local_blocks, n_dp, piece, local_width).transpose(1, 0, 2, 3)
    pieces = dp_exchange(split, gather=False, cid=0)
    pieces = pieces.reshape(n_blocks, piece, local_width)

    slots = jnp.take(pieces, chosen_blocks.reshape(-1), axis=0)
    slots = slots.reshape(n_expert, CAP, piece, local_width)
    mine = lax.all_to_all(slots, "expert", 0, 3, tiled=True)
    mine = mine.reshape(CAP * piece, model_width)
    picked_a, picked_b = all_gather_2d(mine, cid=20)
    picked_a = picked_a.reshape(n_dp * CAP * piece, -1)
    picked_b = picked_b.reshape(n_dp * CAP * piece, -1)
    half = picked_a.shape[1]

    w_gate = gate_weight[0]
    w_up = up_weight[0]
    w_down = down_weight[0]
    gate_row = gate_values[0]
    my_count = lax.dynamic_index_in_dim(block_counts, my_expert, 0, keepdims=False)
    live = jnp.arange(CAP * BLK) // BLK < my_count
    scale = jnp.where(live, gate_row, jnp.zeros_like(gate_row))
    scale = scale.reshape(CAP, n_dp, piece).transpose(1, 0, 2).reshape(-1)

    gate = jnp.dot(picked_a, w_gate[:half], preferred_element_type=jnp.float32) + jnp.dot(
        picked_b, w_gate[half:], preferred_element_type=jnp.float32
    )
    upper = jnp.dot(picked_a, w_up[:half], preferred_element_type=jnp.float32) + jnp.dot(
        picked_b, w_up[half:], preferred_element_type=jnp.float32
    )
    hidden = (jax.nn.silu(gate) * upper).astype(jnp.bfloat16)
    part = jnp.dot(hidden, w_down, preferred_element_type=jnp.float32)
    part = (part * scale[:, None]).astype(jnp.bfloat16)

    summed = reduce_scatter_2d(part.reshape(n_dp, CAP * piece, model_width), cid=1)
    summed = summed.astype(jnp.bfloat16)
    summed = summed.reshape(CAP * piece, n_expert, local_width).transpose(1, 0, 2)
    outs = lax.all_to_all(summed, "expert", 0, 0, tiled=True)
    outs = outs.reshape(n_expert * CAP, piece * local_width)

    selector = chosen_blocks.reshape(-1)[None, :] == jnp.arange(n_blocks)[:, None]
    added = jnp.dot(selector.astype(jnp.bfloat16), outs, preferred_element_type=jnp.float32)
    mixed = pieces.reshape(n_blocks, piece * local_width).astype(jnp.float32) + added
    mixed = mixed.astype(jnp.bfloat16).reshape(n_dp, local_blocks, piece, local_width)
    back = dp_exchange(mixed, gather=False, cid=3)
    return back.transpose(1, 0, 2, 3).reshape(local_tokens, local_width)


def solution(mesh):
    in_specs = (
        P("dp", None),
        P("dp", "expert"),
        P("dp", "expert"),
        P("expert", None, "dp"),
        P("expert", None, "dp"),
        P("expert", "dp", None),
        P("expert", None),
        P(),
        P(),
    )
    out_specs = P("dp", "expert")
    return jax.shard_map(body, mesh=mesh, in_specs=in_specs, out_specs=out_specs, check_vma=False)
```

```python
import functools

import jax
import jax.numpy as jnp
from jax import lax
from jax.sharding import PartitionSpec as P
from jax.experimental import pallas as pl
from jax.experimental.pallas import tpu as pltpu

BLK = 128
CAP = 4


def _exchange_kernel(n, gather, x_ref, o_ref, local_sem, send_sems, recv_sems):
    me = lax.axis_index("dp")
    mesh_id = pl.DeviceIdType.MESH
    barrier = pltpu.get_barrier_semaphore()
    for k in range(1, n):
        pl.semaphore_signal(barrier, 1, device_id={"dp": lax.rem(me + k, n)}, device_id_type=mesh_id)
    pl.semaphore_wait(barrier, n - 1)
    local = pltpu.make_async_copy(x_ref if gather else x_ref.at[me], o_ref.at[me], local_sem)
    local.start()
    copies = []
    for k in range(1, n):
        target = lax.rem(me + k, n)
        copy = pltpu.make_async_remote_copy(
            src_ref=x_ref if gather else x_ref.at[target],
            dst_ref=o_ref.at[me],
            send_sem=send_sems.at[k - 1],
            recv_sem=recv_sems.at[k - 1],
            device_id={"dp": target},
            device_id_type=mesh_id,
        )
        copy.start()
        copies.append(copy)
    local.wait()
    for copy in copies:
        copy.wait()


def dp_exchange(x, gather, cid):
    n = lax.axis_size("dp")
    shape = (n,) + x.shape if gather else x.shape
    return pl.pallas_call(
        functools.partial(_exchange_kernel, n, gather),
        out_shape=jax.ShapeDtypeStruct(shape, x.dtype),
        in_specs=[pl.BlockSpec(memory_space=pl.ANY)],
        out_specs=pl.BlockSpec(memory_space=pl.ANY),
        scratch_shapes=[
            pltpu.SemaphoreType.DMA(()),
            pltpu.SemaphoreType.DMA((n - 1,)),
            pltpu.SemaphoreType.DMA((n - 1,)),
        ],
        compiler_params=pltpu.CompilerParams(collective_id=cid, has_side_effects=True),
    )(x)


def _route_kernel(strides, side, gather, *refs):
    n_in = len(strides)
    ins, outs = refs[:n_in], refs[n_in:2 * n_in]
    local_sems, send_sems, recv_sems = refs[2 * n_in:]
    me = lax.axis_index("dp")
    mesh_id = pl.DeviceIdType.MESH
    routes = []
    for r, stride in enumerate(strides):
        coord = lax.rem(me // stride, side)
        base = me - coord * stride
        for k in range(1, side):
            to = lax.rem(coord + k, side)
            routes.append((r, coord, to, base + to * stride))
    barrier = pltpu.get_barrier_semaphore()
    for _, _, _, target in routes:
        pl.semaphore_signal(barrier, 1, device_id={"dp": target}, device_id_type=mesh_id)
    pl.semaphore_wait(barrier, len(routes))
    locals_ = []
    for r in range(n_in):
        coord = lax.rem(me // strides[r], side)
        source = ins[r] if gather else ins[r].at[coord]
        local = pltpu.make_async_copy(source, outs[r].at[coord], local_sems.at[r])
        local.start()
        locals_.append(local)
    copies = []
    for i, (r, coord, to, target) in enumerate(routes):
        copy = pltpu.make_async_remote_copy(
            src_ref=ins[r] if gather else ins[r].at[to],
            dst_ref=outs[r].at[coord],
            send_sem=send_sems.at[i],
            recv_sem=recv_sems.at[i],
            device_id={"dp": target},
            device_id_type=mesh_id,
        )
        copy.start()
        copies.append(copy)
    for local in locals_:
        local.wait()
    for copy in copies:
        copy.wait()


def dp_route(xs, strides, cid, side=4, gather=False):
    n_routes = len(strides) * (side - 1)
    shapes = [((side,) + x.shape) if gather else x.shape for x in xs]
    return pl.pallas_call(
        functools.partial(_route_kernel, tuple(strides), side, gather),
        out_shape=[jax.ShapeDtypeStruct(s, x.dtype) for s, x in zip(shapes, xs)],
        in_specs=[pl.BlockSpec(memory_space=pl.ANY)] * len(xs),
        out_specs=[pl.BlockSpec(memory_space=pl.ANY)] * len(xs),
        scratch_shapes=[
            pltpu.SemaphoreType.DMA((len(xs),)),
            pltpu.SemaphoreType.DMA((n_routes,)),
            pltpu.SemaphoreType.DMA((n_routes,)),
        ],
        compiler_params=pltpu.CompilerParams(collective_id=cid, has_side_effects=True),
    )(*xs)


def reduce_scatter_2d(part, cid):
    side = 4
    n_dp, rows, cols = part.shape
    half = cols // 2
    grid = part.reshape(side, side, rows, cols)
    first_a = grid[..., :half].transpose(1, 0, 2, 3)
    first_b = grid[..., half:]
    got_a, got_b = dp_route([first_a, first_b], (1, side), cid)
    second_a = got_a.astype(jnp.float32).sum(axis=0).astype(jnp.bfloat16)
    second_b = got_b.astype(jnp.float32).sum(axis=0).astype(jnp.bfloat16)
    got_a, got_b = dp_route([second_a, second_b], (side, 1), cid + 1)
    total_a = got_a.astype(jnp.float32).sum(axis=0)
    total_b = got_b.astype(jnp.float32).sum(axis=0)
    return jnp.concatenate([total_a, total_b], axis=-1)


def all_gather_2d(x, cid):
    side = 4
    half = x.shape[-1] // 2
    got_a, got_b = dp_route([x[..., :half], x[..., half:]], (1, side), cid, gather=True)
    got_a, got_b = dp_route([got_a, got_b], (side, 1), cid + 1, gather=True)
    n = side * side
    got_a = got_a.reshape((n,) + got_a.shape[2:])
    perm = (1, 0) + tuple(range(2, got_b.ndim))
    got_b = got_b.transpose(perm).reshape((n,) + got_b.shape[2:])
    return got_a, got_b


def body(
    context,
    out_weight,
    residual,
    gate_weight,
    up_weight,
    down_weight,
    gate_values,
    chosen_blocks,
    block_counts,
):
    n_dp = lax.axis_size("dp")
    n_expert = lax.axis_size("expert")
    local_tokens = context.shape[0]
    local_width = residual.shape[1]
    model_width = context.shape[1]
    local_blocks = local_tokens // BLK
    n_blocks = local_blocks * n_dp
    piece = BLK // n_dp
    my_expert = lax.axis_index("expert")

    split_w = local_width // 2
    w_s = lax.all_gather(out_weight[:, :split_w], "dp", axis=0, tiled=True)
    w_a, w_b = all_gather_2d(out_weight[:, split_w:], cid=10)
    w_a = w_a.reshape(model_width, -1)
    w_b = w_b.reshape(model_width, -1)
    projected = jnp.concatenate(
        [
            jnp.dot(context, w_s, preferred_element_type=jnp.float32),
            jnp.dot(context, w_a, preferred_element_type=jnp.float32),
            jnp.dot(context, w_b, preferred_element_type=jnp.float32),
        ],
        axis=1,
    )
    attended = (residual.astype(jnp.float32) + projected).astype(jnp.bfloat16)

    split = attended.reshape(local_blocks, n_dp, piece, local_width).transpose(1, 0, 2, 3)
    pieces = dp_exchange(split, gather=False, cid=0)
    pieces = pieces.reshape(n_blocks, piece, local_width)

    slots = jnp.take(pieces, chosen_blocks.reshape(-1), axis=0)
    slots = slots.reshape(n_expert, CAP, piece, local_width)
    mine = lax.all_to_all(slots, "expert", 0, 3, tiled=True)
    mine = mine.reshape(CAP * piece, model_width)
    split_m = model_width // 2
    picked_s = lax.all_gather(mine[:, :split_m], "dp", axis=0, tiled=True)
    picked_a, picked_b = all_gather_2d(mine[:, split_m:], cid=20)
    picked_a = picked_a.reshape(n_dp * CAP * piece, -1)
    picked_b = picked_b.reshape(n_dp * CAP * piece, -1)
    quarter = picked_a.shape[1]

    w_gate = gate_weight[0]
    w_up = up_weight[0]
    w_down = down_weight[0]
    gate_row = gate_values[0]
    my_count = lax.dynamic_index_in_dim(block_counts, my_expert, 0, keepdims=False)
    live = jnp.arange(CAP * BLK) // BLK < my_count
    scale = jnp.where(live, gate_row, jnp.zeros_like(gate_row))
    scale = scale.reshape(CAP, n_dp, piece).transpose(1, 0, 2).reshape(-1)

    def contract(w):
        return (
            jnp.dot(picked_s, w[:split_m], preferred_element_type=jnp.float32)
            + jnp.dot(picked_a, w[split_m:split_m + quarter], preferred_element_type=jnp.float32)
            + jnp.dot(picked_b, w[split_m + quarter:], preferred_element_type=jnp.float32)
        )

    gate = contract(w_gate)
    upper = contract(w_up)
    hidden = (jax.nn.silu(gate) * upper).astype(jnp.bfloat16)
    part = jnp.dot(hidden, w_down, preferred_element_type=jnp.float32)
    part = (part * scale[:, None]).astype(jnp.bfloat16)

    part = part.reshape(n_dp, CAP * piece, model_width)
    summed_s = lax.psum_scatter(part[..., :split_m], "dp", scatter_dimension=0, tiled=True)
    summed_k = reduce_scatter_2d(part[..., split_m:], cid=1).astype(jnp.bfloat16)
    summed = jnp.concatenate([summed_s[0], summed_k], axis=-1)
    summed = summed.reshape(CAP * piece, n_expert, local_width).transpose(1, 0, 2)
    outs = lax.all_to_all(summed, "expert", 0, 0, tiled=True)
    outs = outs.reshape(n_expert * CAP, piece * local_width)

    selector = chosen_blocks.reshape(-1)[None, :] == jnp.arange(n_blocks)[:, None]
    added = jnp.dot(selector.astype(jnp.bfloat16), outs, preferred_element_type=jnp.float32)
    mixed = pieces.reshape(n_blocks, piece * local_width).astype(jnp.float32) + added
    mixed = mixed.astype(jnp.bfloat16).reshape(n_dp, local_blocks, piece, local_width)
    back = dp_exchange(mixed, gather=False, cid=3)
    return back.transpose(1, 0, 2, 3).reshape(local_tokens, local_width)


def solution(mesh):
    in_specs = (
        P("dp", None),
        P("dp", "expert"),
        P("dp", "expert"),
        P("expert", None, "dp"),
        P("expert", None, "dp"),
        P("expert", "dp", None),
        P("expert", None),
        P(),
        P(),
    )
    out_specs = P("dp", "expert")
    return jax.shard_map(body, mesh=mesh, in_specs=in_specs, out_specs=out_specs, check_vma=False)
```

```python
import functools

import jax
import jax.numpy as jnp
from jax import lax
from jax.sharding import PartitionSpec as P
from jax.experimental import pallas as pl
from jax.experimental.pallas import tpu as pltpu

BLK = 128
CAP = 4


def _exchange_kernel(n, gather, axis, x_ref, o_ref, local_sem, send_sems, recv_sems):
    me = lax.axis_index(axis)
    mesh_id = pl.DeviceIdType.MESH
    barrier = pltpu.get_barrier_semaphore()
    for k in range(1, n):
        pl.semaphore_signal(barrier, 1, device_id={axis: lax.rem(me + k, n)}, device_id_type=mesh_id)
    pl.semaphore_wait(barrier, n - 1)
    local = pltpu.make_async_copy(x_ref if gather else x_ref.at[me], o_ref.at[me], local_sem)
    local.start()
    copies = []
    for k in range(1, n):
        target = lax.rem(me + k, n)
        copy = pltpu.make_async_remote_copy(
            src_ref=x_ref if gather else x_ref.at[target],
            dst_ref=o_ref.at[me],
            send_sem=send_sems.at[k - 1],
            recv_sem=recv_sems.at[k - 1],
            device_id={axis: target},
            device_id_type=mesh_id,
        )
        copy.start()
        copies.append(copy)
    local.wait()
    for copy in copies:
        copy.wait()


def dp_exchange(x, gather, cid, axis="dp"):
    n = lax.axis_size(axis)
    shape = (n,) + x.shape if gather else x.shape
    return pl.pallas_call(
        functools.partial(_exchange_kernel, n, gather, axis),
        out_shape=jax.ShapeDtypeStruct(shape, x.dtype),
        in_specs=[pl.BlockSpec(memory_space=pl.ANY)],
        out_specs=pl.BlockSpec(memory_space=pl.ANY),
        scratch_shapes=[
            pltpu.SemaphoreType.DMA(()),
            pltpu.SemaphoreType.DMA((n - 1,)),
            pltpu.SemaphoreType.DMA((n - 1,)),
        ],
        compiler_params=pltpu.CompilerParams(collective_id=cid, has_side_effects=True),
    )(x)


def _route_kernel(strides, side, gather, *refs):
    n_in = len(strides)
    ins, outs = refs[:n_in], refs[n_in:2 * n_in]
    local_sems, send_sems, recv_sems = refs[2 * n_in:]
    me = lax.axis_index("dp")
    mesh_id = pl.DeviceIdType.MESH
    routes = []
    for r, stride in enumerate(strides):
        coord = lax.rem(me // stride, side)
        base = me - coord * stride
        for k in range(1, side):
            to = lax.rem(coord + k, side)
            routes.append((r, coord, to, base + to * stride))
    barrier = pltpu.get_barrier_semaphore()
    for _, _, _, target in routes:
        pl.semaphore_signal(barrier, 1, device_id={"dp": target}, device_id_type=mesh_id)
    pl.semaphore_wait(barrier, len(routes))
    locals_ = []
    for r in range(n_in):
        coord = lax.rem(me // strides[r], side)
        source = ins[r] if gather else ins[r].at[coord]
        local = pltpu.make_async_copy(source, outs[r].at[coord], local_sems.at[r])
        local.start()
        locals_.append(local)
    copies = []
    for i, (r, coord, to, target) in enumerate(routes):
        copy = pltpu.make_async_remote_copy(
            src_ref=ins[r] if gather else ins[r].at[to],
            dst_ref=outs[r].at[coord],
            send_sem=send_sems.at[i],
            recv_sem=recv_sems.at[i],
            device_id={"dp": target},
            device_id_type=mesh_id,
        )
        copy.start()
        copies.append(copy)
    for local in locals_:
        local.wait()
    for copy in copies:
        copy.wait()


def dp_route(xs, strides, cid, side=4, gather=False):
    n_routes = len(strides) * (side - 1)
    shapes = [((side,) + x.shape) if gather else x.shape for x in xs]
    return pl.pallas_call(
        functools.partial(_route_kernel, tuple(strides), side, gather),
        out_shape=[jax.ShapeDtypeStruct(s, x.dtype) for s, x in zip(shapes, xs)],
        in_specs=[pl.BlockSpec(memory_space=pl.ANY)] * len(xs),
        out_specs=[pl.BlockSpec(memory_space=pl.ANY)] * len(xs),
        scratch_shapes=[
            pltpu.SemaphoreType.DMA((len(xs),)),
            pltpu.SemaphoreType.DMA((n_routes,)),
            pltpu.SemaphoreType.DMA((n_routes,)),
        ],
        compiler_params=pltpu.CompilerParams(collective_id=cid, has_side_effects=True),
    )(*xs)


def reduce_scatter_2d(part, cid):
    side = 4
    n_dp, rows, cols = part.shape
    half = cols // 2
    grid = part.reshape(side, side, rows, cols)
    first_a = grid[..., :half].transpose(1, 0, 2, 3)
    first_b = grid[..., half:]
    got_a, got_b = dp_route([first_a, first_b], (1, side), cid)
    second_a = got_a.astype(jnp.float32).sum(axis=0).astype(jnp.bfloat16)
    second_b = got_b.astype(jnp.float32).sum(axis=0).astype(jnp.bfloat16)
    got_a, got_b = dp_route([second_a, second_b], (side, 1), cid + 1)
    total_a = got_a.astype(jnp.float32).sum(axis=0)
    total_b = got_b.astype(jnp.float32).sum(axis=0)
    return jnp.concatenate([total_a, total_b], axis=-1)


def all_gather_2d(x, cid):
    side = 4
    half = x.shape[-1] // 2
    got_a, got_b = dp_route([x[..., :half], x[..., half:]], (1, side), cid, gather=True)
    got_a, got_b = dp_route([got_a, got_b], (side, 1), cid + 1, gather=True)
    n = side * side
    got_a = got_a.reshape((n,) + got_a.shape[2:])
    perm = (1, 0) + tuple(range(2, got_b.ndim))
    got_b = got_b.transpose(perm).reshape((n,) + got_b.shape[2:])
    return got_a, got_b


def body(
    context,
    out_weight,
    residual,
    gate_weight,
    up_weight,
    down_weight,
    gate_values,
    chosen_blocks,
    block_counts,
):
    n_dp = lax.axis_size("dp")
    n_expert = lax.axis_size("expert")
    local_tokens = context.shape[0]
    local_width = residual.shape[1]
    model_width = context.shape[1]
    local_blocks = local_tokens // BLK
    n_blocks = local_blocks * n_dp
    piece = BLK // n_dp
    my_expert = lax.axis_index("expert")

    w_a, w_b = all_gather_2d(out_weight, cid=10)
    w_a = w_a.reshape(model_width, -1)
    w_b = w_b.reshape(model_width, -1)
    projected = jnp.concatenate(
        [
            jnp.dot(context, w_a, preferred_element_type=jnp.float32),
            jnp.dot(context, w_b, preferred_element_type=jnp.float32),
        ],
        axis=1,
    )
    attended = (residual.astype(jnp.float32) + projected).astype(jnp.bfloat16)

    split = attended.reshape(local_blocks, n_dp, piece, local_width).transpose(1, 0, 2, 3)
    pieces = dp_exchange(split, gather=False, cid=0)
    pieces = pieces.reshape(n_blocks, piece, local_width)

    slots = jnp.take(pieces, chosen_blocks.reshape(-1), axis=0)
    slots = slots.reshape(n_expert, CAP, piece, local_width)
    mine = dp_exchange(slots, gather=False, cid=4, axis="expert")
    mine = mine.transpose(1, 2, 0, 3).reshape(CAP * piece, model_width)
    picked_a, picked_b = all_gather_2d(mine, cid=20)
    picked_a = picked_a.reshape(n_dp * CAP * piece, -1)
    picked_b = picked_b.reshape(n_dp * CAP * piece, -1)
    half = picked_a.shape[1]

    w_gate = gate_weight[0]
    w_up = up_weight[0]
    w_down = down_weight[0]
    gate_row = gate_values[0]
    my_count = lax.dynamic_index_in_dim(block_counts, my_expert, 0, keepdims=False)
    live = jnp.arange(CAP * BLK) // BLK < my_count
    scale = jnp.where(live, gate_row, jnp.zeros_like(gate_row))
    scale = scale.reshape(CAP, n_dp, piece).transpose(1, 0, 2).reshape(-1)

    gate = jnp.dot(picked_a, w_gate[:half], preferred_element_type=jnp.float32) + jnp.dot(
        picked_b, w_gate[half:], preferred_element_type=jnp.float32
    )
    upper = jnp.dot(picked_a, w_up[:half], preferred_element_type=jnp.float32) + jnp.dot(
        picked_b, w_up[half:], preferred_element_type=jnp.float32
    )
    hidden = (jax.nn.silu(gate) * upper).astype(jnp.bfloat16)
    part = jnp.dot(hidden, w_down, preferred_element_type=jnp.float32)
    part = (part * scale[:, None]).astype(jnp.bfloat16)

    summed = reduce_scatter_2d(part.reshape(n_dp, CAP * piece, model_width), cid=1)
    summed = summed.astype(jnp.bfloat16)
    summed = summed.reshape(CAP * piece, n_expert, local_width).transpose(1, 0, 2)
    outs = dp_exchange(summed, gather=False, cid=5, axis="expert")
    outs = outs.reshape(n_expert * CAP, piece * local_width)

    selector = chosen_blocks.reshape(-1)[None, :] == jnp.arange(n_blocks)[:, None]
    added = jnp.dot(selector.astype(jnp.bfloat16), outs, preferred_element_type=jnp.float32)
    mixed = pieces.reshape(n_blocks, piece * local_width).astype(jnp.float32) + added
    mixed = mixed.astype(jnp.bfloat16).reshape(n_dp, local_blocks, piece, local_width)
    back = dp_exchange(mixed, gather=False, cid=3)
    return back.transpose(1, 0, 2, 3).reshape(local_tokens, local_width)


def solution(mesh):
    in_specs = (
        P("dp", None),
        P("dp", "expert"),
        P("dp", "expert"),
        P("expert", None, "dp"),
        P("expert", None, "dp"),
        P("expert", "dp", None),
        P("expert", None),
        P(),
        P(),
    )
    out_specs = P("dp", "expert")
    return jax.shard_map(body, mesh=mesh, in_specs=in_specs, out_specs=out_specs, check_vma=False)
```

```python
import functools

import jax
import jax.numpy as jnp
from jax import lax
from jax.sharding import PartitionSpec as P
from jax.experimental import pallas as pl
from jax.experimental.pallas import tpu as pltpu

BLK = 128
CAP = 4


def _exchange_kernel(n, gather, axis, x_ref, o_ref, local_sem, send_sems, recv_sems):
    me = lax.axis_index(axis)
    mesh_id = pl.DeviceIdType.MESH
    barrier = pltpu.get_barrier_semaphore()
    for k in range(1, n):
        pl.semaphore_signal(barrier, 1, device_id={axis: lax.rem(me + k, n)}, device_id_type=mesh_id)
    pl.semaphore_wait(barrier, n - 1)
    local = pltpu.make_async_copy(x_ref if gather else x_ref.at[me], o_ref.at[me], local_sem)
    local.start()
    copies = []
    for k in range(1, n):
        target = lax.rem(me + k, n)
        copy = pltpu.make_async_remote_copy(
            src_ref=x_ref if gather else x_ref.at[target],
            dst_ref=o_ref.at[me],
            send_sem=send_sems.at[k - 1],
            recv_sem=recv_sems.at[k - 1],
            device_id={axis: target},
            device_id_type=mesh_id,
        )
        copy.start()
        copies.append(copy)
    local.wait()
    for copy in copies:
        copy.wait()


def dp_exchange(x, gather, cid, axis="dp"):
    n = lax.axis_size(axis)
    shape = (n,) + x.shape if gather else x.shape
    return pl.pallas_call(
        functools.partial(_exchange_kernel, n, gather, axis),
        out_shape=jax.ShapeDtypeStruct(shape, x.dtype),
        in_specs=[pl.BlockSpec(memory_space=pl.ANY)],
        out_specs=pl.BlockSpec(memory_space=pl.ANY),
        scratch_shapes=[
            pltpu.SemaphoreType.DMA(()),
            pltpu.SemaphoreType.DMA((n - 1,)),
            pltpu.SemaphoreType.DMA((n - 1,)),
        ],
        compiler_params=pltpu.CompilerParams(collective_id=cid, has_side_effects=True),
    )(x)


def _route_kernel(strides, side, gather, *refs):
    n_in = len(strides)
    ins, outs = refs[:n_in], refs[n_in:2 * n_in]
    local_sems, send_sems, recv_sems = refs[2 * n_in:]
    me = lax.axis_index("dp")
    mesh_id = pl.DeviceIdType.MESH
    routes = []
    for r, stride in enumerate(strides):
        coord = lax.rem(me // stride, side)
        base = me - coord * stride
        for k in range(1, side):
            to = lax.rem(coord + k, side)
            routes.append((r, coord, to, base + to * stride))
    barrier = pltpu.get_barrier_semaphore()
    for _, _, _, target in routes:
        pl.semaphore_signal(barrier, 1, device_id={"dp": target}, device_id_type=mesh_id)
    pl.semaphore_wait(barrier, len(routes))
    locals_ = []
    for r in range(n_in):
        coord = lax.rem(me // strides[r], side)
        source = ins[r] if gather else ins[r].at[coord]
        local = pltpu.make_async_copy(source, outs[r].at[coord], local_sems.at[r])
        local.start()
        locals_.append(local)
    copies = []
    for i, (r, coord, to, target) in enumerate(routes):
        copy = pltpu.make_async_remote_copy(
            src_ref=ins[r] if gather else ins[r].at[to],
            dst_ref=outs[r].at[coord],
            send_sem=send_sems.at[i],
            recv_sem=recv_sems.at[i],
            device_id={"dp": target},
            device_id_type=mesh_id,
        )
        copy.start()
        copies.append(copy)
    for local in locals_:
        local.wait()
    for copy in copies:
        copy.wait()


def dp_route(xs, strides, cid, side=4, gather=False):
    n_routes = len(strides) * (side - 1)
    shapes = [((side,) + x.shape) if gather else x.shape for x in xs]
    return pl.pallas_call(
        functools.partial(_route_kernel, tuple(strides), side, gather),
        out_shape=[jax.ShapeDtypeStruct(s, x.dtype) for s, x in zip(shapes, xs)],
        in_specs=[pl.BlockSpec(memory_space=pl.ANY)] * len(xs),
        out_specs=[pl.BlockSpec(memory_space=pl.ANY)] * len(xs),
        scratch_shapes=[
            pltpu.SemaphoreType.DMA((len(xs),)),
            pltpu.SemaphoreType.DMA((n_routes,)),
            pltpu.SemaphoreType.DMA((n_routes,)),
        ],
        compiler_params=pltpu.CompilerParams(collective_id=cid, has_side_effects=True),
    )(*xs)


def reduce_scatter_2d(part, cid):
    side = 4
    n_dp, rows, cols = part.shape
    half = cols // 2
    grid = part.reshape(side, side, rows, cols)
    first_a = grid[..., :half].transpose(1, 0, 2, 3)
    first_b = grid[..., half:]
    got_a, got_b = dp_route([first_a, first_b], (1, side), cid)
    second_a = got_a.astype(jnp.float32).sum(axis=0).astype(jnp.bfloat16)
    second_b = got_b.astype(jnp.float32).sum(axis=0).astype(jnp.bfloat16)
    got_a, got_b = dp_route([second_a, second_b], (side, 1), cid + 1)
    total_a = got_a.astype(jnp.float32).sum(axis=0)
    total_b = got_b.astype(jnp.float32).sum(axis=0)
    return jnp.concatenate([total_a, total_b], axis=-1)


def _ring_gather_kernel(strides, side, *refs):
    n_in = len(strides)
    ins, outs = refs[:n_in], refs[n_in:2 * n_in]
    local_sems, send_sems, recv_sems = refs[2 * n_in:]
    me = lax.axis_index("dp")
    mesh_id = pl.DeviceIdType.MESH
    geo = []
    for r, stride in enumerate(strides):
        coord = lax.rem(me // stride, side)
        base = me - coord * stride
        plus = lax.rem(coord + 1, side)
        minus = lax.rem(coord + side - 1, side)
        far = lax.rem(coord + 2, side)
        geo.append((coord, plus, minus, far, base + plus * stride, base + minus * stride))
    barrier = pltpu.get_barrier_semaphore()
    for _, _, _, _, to_plus, to_minus in geo:
        pl.semaphore_signal(barrier, 1, device_id={"dp": to_plus}, device_id_type=mesh_id)
        pl.semaphore_signal(barrier, 1, device_id={"dp": to_minus}, device_id_type=mesh_id)
    pl.semaphore_wait(barrier, 2 * n_in)

    def remote(r, src, dst, slot, target):
        return pltpu.make_async_remote_copy(
            src_ref=src,
            dst_ref=dst,
            send_sem=send_sems.at[r, slot],
            recv_sem=recv_sems.at[r, slot],
            device_id={"dp": target},
            device_id_type=mesh_id,
        )

    started, locals_ = [], []
    for r, (coord, plus, minus, far, to_plus, to_minus) in enumerate(geo):
        local = pltpu.make_async_copy(ins[r], outs[r].at[coord], local_sems.at[r])
        local.start()
        locals_.append(local)
        for slot, target in ((0, to_plus), (1, to_minus)):
            copy = remote(r, ins[r], outs[r].at[coord], slot, target)
            copy.start()
            started.append(copy)
    finals = []
    for r, (coord, plus, minus, far, to_plus, to_minus) in enumerate(geo):
        half = outs[r].shape[1] // 2
        rest = outs[r].shape[1] - half
        first = pl.ds(0, half)
        second = pl.ds(half, rest)
        remote(r, ins[r], outs[r].at[minus], 0, to_minus).wait_recv()
        onward = remote(r, outs[r].at[minus, first], outs[r].at[minus, first], 2, to_plus)
        onward.start()
        started.append(onward)
        remote(r, ins[r], outs[r].at[plus], 1, to_plus).wait_recv()
        onward = remote(r, outs[r].at[plus, second], outs[r].at[plus, second], 3, to_minus)
        onward.start()
        started.append(onward)
        finals.append(remote(r, outs[r].at[far, first], outs[r].at[far, first], 2, to_minus))
        finals.append(remote(r, outs[r].at[far, second], outs[r].at[far, second], 3, to_plus))
    for copy in finals:
        copy.wait_recv()
    for local in locals_:
        local.wait()
    for copy in started:
        copy.wait_send()


def ring_gather(xs, strides, cid, side=4):
    return pl.pallas_call(
        functools.partial(_ring_gather_kernel, tuple(strides), side),
        out_shape=[jax.ShapeDtypeStruct((side,) + x.shape, x.dtype) for x in xs],
        in_specs=[pl.BlockSpec(memory_space=pl.ANY)] * len(xs),
        out_specs=[pl.BlockSpec(memory_space=pl.ANY)] * len(xs),
        scratch_shapes=[
            pltpu.SemaphoreType.DMA((len(xs),)),
            pltpu.SemaphoreType.DMA((len(xs), 4)),
            pltpu.SemaphoreType.DMA((len(xs), 4)),
        ],
        compiler_params=pltpu.CompilerParams(collective_id=cid, has_side_effects=True),
    )(*xs)


def all_gather_2d(x, cid):
    side = 4
    half = x.shape[-1] // 2
    got_a, got_b = ring_gather([x[..., :half], x[..., half:]], (1, side), cid)
    got_a, got_b = ring_gather([got_a, got_b], (side, 1), cid + 1)
    n = side * side
    got_a = got_a.reshape((n,) + got_a.shape[2:])
    perm = (1, 0) + tuple(range(2, got_b.ndim))
    got_b = got_b.transpose(perm).reshape((n,) + got_b.shape[2:])
    return got_a, got_b


def body(
    context,
    out_weight,
    residual,
    gate_weight,
    up_weight,
    down_weight,
    gate_values,
    chosen_blocks,
    block_counts,
):
    n_dp = lax.axis_size("dp")
    n_expert = lax.axis_size("expert")
    local_tokens = context.shape[0]
    local_width = residual.shape[1]
    model_width = context.shape[1]
    local_blocks = local_tokens // BLK
    n_blocks = local_blocks * n_dp
    piece = BLK // n_dp
    my_expert = lax.axis_index("expert")

    w_a, w_b = all_gather_2d(out_weight, cid=10)
    w_a = w_a.reshape(model_width, -1)
    w_b = w_b.reshape(model_width, -1)
    projected = jnp.concatenate(
        [
            jnp.dot(context, w_a, preferred_element_type=jnp.float32),
            jnp.dot(context, w_b, preferred_element_type=jnp.float32),
        ],
        axis=1,
    )
    attended = (residual.astype(jnp.float32) + projected).astype(jnp.bfloat16)

    split = attended.reshape(local_blocks, n_dp, piece, local_width).transpose(1, 0, 2, 3)
    pieces = dp_exchange(split, gather=False, cid=0)
    pieces = pieces.reshape(n_blocks, piece, local_width)

    slots = jnp.take(pieces, chosen_blocks.reshape(-1), axis=0)
    slots = slots.reshape(n_expert, CAP, piece, local_width)
    mine = dp_exchange(slots, gather=False, cid=4, axis="expert")
    mine = mine.transpose(1, 2, 0, 3).reshape(CAP * piece, model_width)
    picked_a, picked_b = all_gather_2d(mine, cid=20)
    picked_a = picked_a.reshape(n_dp * CAP * piece, -1)
    picked_b = picked_b.reshape(n_dp * CAP * piece, -1)
    half = picked_a.shape[1]

    w_gate = gate_weight[0]
    w_up = up_weight[0]
    w_down = down_weight[0]
    gate_row = gate_values[0]
    my_count = lax.dynamic_index_in_dim(block_counts, my_expert, 0, keepdims=False)
    live = jnp.arange(CAP * BLK) // BLK < my_count
    scale = jnp.where(live, gate_row, jnp.zeros_like(gate_row))
    scale = scale.reshape(CAP, n_dp, piece).transpose(1, 0, 2).reshape(-1)

    gate = jnp.dot(picked_a, w_gate[:half], preferred_element_type=jnp.float32) + jnp.dot(
        picked_b, w_gate[half:], preferred_element_type=jnp.float32
    )
    upper = jnp.dot(picked_a, w_up[:half], preferred_element_type=jnp.float32) + jnp.dot(
        picked_b, w_up[half:], preferred_element_type=jnp.float32
    )
    hidden = (jax.nn.silu(gate) * upper).astype(jnp.bfloat16)
    part = jnp.dot(hidden, w_down, preferred_element_type=jnp.float32)
    part = (part * scale[:, None]).astype(jnp.bfloat16)

    summed = reduce_scatter_2d(part.reshape(n_dp, CAP * piece, model_width), cid=1)
    summed = summed.astype(jnp.bfloat16)
    summed = summed.reshape(CAP * piece, n_expert, local_width).transpose(1, 0, 2)
    outs = dp_exchange(summed, gather=False, cid=5, axis="expert")
    outs = outs.reshape(n_expert * CAP, piece * local_width)

    selector = chosen_blocks.reshape(-1)[None, :] == jnp.arange(n_blocks)[:, None]
    added = jnp.dot(selector.astype(jnp.bfloat16), outs, preferred_element_type=jnp.float32)
    mixed = pieces.reshape(n_blocks, piece * local_width).astype(jnp.float32) + added
    mixed = mixed.astype(jnp.bfloat16).reshape(n_dp, local_blocks, piece, local_width)
    back = dp_exchange(mixed, gather=False, cid=3)
    return back.transpose(1, 0, 2, 3).reshape(local_tokens, local_width)


def solution(mesh):
    in_specs = (
        P("dp", None),
        P("dp", "expert"),
        P("dp", "expert"),
        P("expert", None, "dp"),
        P("expert", None, "dp"),
        P("expert", "dp", None),
        P("expert", None),
        P(),
        P(),
    )
    out_specs = P("dp", "expert")
    return jax.shard_map(body, mesh=mesh, in_specs=in_specs, out_specs=out_specs, check_vma=False)
```

```python
import functools

import jax
import jax.numpy as jnp
from jax import lax
from jax.sharding import PartitionSpec as P
from jax.experimental import pallas as pl
from jax.experimental.pallas import tpu as pltpu

BLK = 128
CAP = 4


def _exchange_kernel(n, gather, axis, x_ref, o_ref, local_sem, send_sems, recv_sems):
    me = lax.axis_index(axis)
    mesh_id = pl.DeviceIdType.MESH
    barrier = pltpu.get_barrier_semaphore()
    for k in range(1, n):
        pl.semaphore_signal(barrier, 1, device_id={axis: lax.rem(me + k, n)}, device_id_type=mesh_id)
    pl.semaphore_wait(barrier, n - 1)
    local = pltpu.make_async_copy(x_ref if gather else x_ref.at[me], o_ref.at[me], local_sem)
    local.start()
    copies = []
    for k in range(1, n):
        target = lax.rem(me + k, n)
        copy = pltpu.make_async_remote_copy(
            src_ref=x_ref if gather else x_ref.at[target],
            dst_ref=o_ref.at[me],
            send_sem=send_sems.at[k - 1],
            recv_sem=recv_sems.at[k - 1],
            device_id={axis: target},
            device_id_type=mesh_id,
        )
        copy.start()
        copies.append(copy)
    local.wait()
    for copy in copies:
        copy.wait()


def dp_exchange(x, gather, cid, axis="dp"):
    n = lax.axis_size(axis)
    shape = (n,) + x.shape if gather else x.shape
    return pl.pallas_call(
        functools.partial(_exchange_kernel, n, gather, axis),
        out_shape=jax.ShapeDtypeStruct(shape, x.dtype),
        in_specs=[pl.BlockSpec(memory_space=pl.ANY)],
        out_specs=pl.BlockSpec(memory_space=pl.ANY),
        scratch_shapes=[
            pltpu.SemaphoreType.DMA(()),
            pltpu.SemaphoreType.DMA((n - 1,)),
            pltpu.SemaphoreType.DMA((n - 1,)),
        ],
        compiler_params=pltpu.CompilerParams(collective_id=cid, has_side_effects=True),
    )(x)


def _route_kernel(strides, side, gather, *refs):
    n_in = len(strides)
    ins, outs = refs[:n_in], refs[n_in:2 * n_in]
    local_sems, send_sems, recv_sems = refs[2 * n_in:]
    me = lax.axis_index("dp")
    mesh_id = pl.DeviceIdType.MESH
    routes = []
    for r, stride in enumerate(strides):
        coord = lax.rem(me // stride, side)
        base = me - coord * stride
        for k in range(1, side):
            to = lax.rem(coord + k, side)
            routes.append((r, coord, to, base + to * stride))
    barrier = pltpu.get_barrier_semaphore()
    for _, _, _, target in routes:
        pl.semaphore_signal(barrier, 1, device_id={"dp": target}, device_id_type=mesh_id)
    pl.semaphore_wait(barrier, len(routes))
    locals_ = []
    for r in range(n_in):
        coord = lax.rem(me // strides[r], side)
        source = ins[r] if gather else ins[r].at[coord]
        local = pltpu.make_async_copy(source, outs[r].at[coord], local_sems.at[r])
        local.start()
        locals_.append(local)
    copies = []
    for i, (r, coord, to, target) in enumerate(routes):
        copy = pltpu.make_async_remote_copy(
            src_ref=ins[r] if gather else ins[r].at[to],
            dst_ref=outs[r].at[coord],
            send_sem=send_sems.at[i],
            recv_sem=recv_sems.at[i],
            device_id={"dp": target},
            device_id_type=mesh_id,
        )
        copy.start()
        copies.append(copy)
    for local in locals_:
        local.wait()
    for copy in copies:
        copy.wait()


def dp_route(xs, strides, cid, side=4, gather=False):
    n_routes = len(strides) * (side - 1)
    shapes = [((side,) + x.shape) if gather else x.shape for x in xs]
    return pl.pallas_call(
        functools.partial(_route_kernel, tuple(strides), side, gather),
        out_shape=[jax.ShapeDtypeStruct(s, x.dtype) for s, x in zip(shapes, xs)],
        in_specs=[pl.BlockSpec(memory_space=pl.ANY)] * len(xs),
        out_specs=[pl.BlockSpec(memory_space=pl.ANY)] * len(xs),
        scratch_shapes=[
            pltpu.SemaphoreType.DMA((len(xs),)),
            pltpu.SemaphoreType.DMA((n_routes,)),
            pltpu.SemaphoreType.DMA((n_routes,)),
        ],
        compiler_params=pltpu.CompilerParams(collective_id=cid, has_side_effects=True),
    )(*xs)


def reduce_scatter_2d(part, cid):
    side = 4
    n_dp, rows, cols = part.shape
    half = cols // 2
    grid = part.reshape(side, side, rows, cols)
    first_a = grid[..., :half].transpose(1, 0, 2, 3)
    first_b = grid[..., half:]
    got_a, got_b = dp_route([first_a, first_b], (1, side), cid)
    second_a = got_a.astype(jnp.float32).sum(axis=0).astype(jnp.bfloat16)
    second_b = got_b.astype(jnp.float32).sum(axis=0).astype(jnp.bfloat16)
    got_a, got_b = dp_route([second_a, second_b], (side, 1), cid + 1)
    total_a = got_a.astype(jnp.float32).sum(axis=0)
    total_b = got_b.astype(jnp.float32).sum(axis=0)
    return jnp.concatenate([total_a, total_b], axis=-1)


def _ring_gather_kernel(strides, side, *refs):
    n_in = len(strides)
    ins, outs = refs[:n_in], refs[n_in:2 * n_in]
    local_sems, send_sems, recv_sems = refs[2 * n_in:]
    me = lax.axis_index("dp")
    mesh_id = pl.DeviceIdType.MESH
    geo = []
    for r, stride in enumerate(strides):
        coord = lax.rem(me // stride, side)
        base = me - coord * stride
        plus = lax.rem(coord + 1, side)
        minus = lax.rem(coord + side - 1, side)
        far = lax.rem(coord + 2, side)
        geo.append((coord, plus, minus, far, base + plus * stride, base + minus * stride))
    barrier = pltpu.get_barrier_semaphore()
    for _, _, _, _, to_plus, to_minus in geo:
        pl.semaphore_signal(barrier, 1, device_id={"dp": to_plus}, device_id_type=mesh_id)
        pl.semaphore_signal(barrier, 1, device_id={"dp": to_minus}, device_id_type=mesh_id)
    pl.semaphore_wait(barrier, 2 * n_in)

    def remote(r, src, dst, slot, target):
        return pltpu.make_async_remote_copy(
            src_ref=src,
            dst_ref=dst,
            send_sem=send_sems.at[r, slot],
            recv_sem=recv_sems.at[r, slot],
            device_id={"dp": target},
            device_id_type=mesh_id,
        )

    started, locals_ = [], []
    for r, (coord, plus, minus, far, to_plus, to_minus) in enumerate(geo):
        local = pltpu.make_async_copy(ins[r], outs[r].at[coord], local_sems.at[r])
        local.start()
        locals_.append(local)
        for slot, target in ((0, to_plus), (1, to_minus)):
            copy = remote(r, ins[r], outs[r].at[coord], slot, target)
            copy.start()
            started.append(copy)
    finals = []
    for r, (coord, plus, minus, far, to_plus, to_minus) in enumerate(geo):
        half = outs[r].shape[1] // 2
        rest = outs[r].shape[1] - half
        first = pl.ds(0, half)
        second = pl.ds(half, rest)
        remote(r, ins[r], outs[r].at[minus], 0, to_minus).wait_recv()
        onward = remote(r, outs[r].at[minus, first], outs[r].at[minus, first], 2, to_plus)
        onward.start()
        started.append(onward)
        remote(r, ins[r], outs[r].at[plus], 1, to_plus).wait_recv()
        onward = remote(r, outs[r].at[plus, second], outs[r].at[plus, second], 3, to_minus)
        onward.start()
        started.append(onward)
        finals.append(remote(r, outs[r].at[far, first], outs[r].at[far, first], 2, to_minus))
        finals.append(remote(r, outs[r].at[far, second], outs[r].at[far, second], 3, to_plus))
    for copy in finals:
        copy.wait_recv()
    for local in locals_:
        local.wait()
    for copy in started:
        copy.wait_send()


def ring_gather(xs, strides, cid, side=4):
    return pl.pallas_call(
        functools.partial(_ring_gather_kernel, tuple(strides), side),
        out_shape=[jax.ShapeDtypeStruct((side,) + x.shape, x.dtype) for x in xs],
        in_specs=[pl.BlockSpec(memory_space=pl.ANY)] * len(xs),
        out_specs=[pl.BlockSpec(memory_space=pl.ANY)] * len(xs),
        scratch_shapes=[
            pltpu.SemaphoreType.DMA((len(xs),)),
            pltpu.SemaphoreType.DMA((len(xs), 4)),
            pltpu.SemaphoreType.DMA((len(xs), 4)),
        ],
        compiler_params=pltpu.CompilerParams(collective_id=cid, has_side_effects=True),
    )(*xs)


def _gather_2d_kernel(side, *refs):
    routes = ((1, side), (side, 1))
    ins, outs = refs[:2], refs[2:4]
    local_sems, send_sems, recv_sems = refs[4:]
    me = lax.axis_index("dp")
    mesh_id = pl.DeviceIdType.MESH

    def coords(stride):
        coord = lax.rem(me // stride, side)
        return coord, me - coord * stride

    barrier = pltpu.get_barrier_semaphore()
    for stride in (1, side):
        coord, base = coords(stride)
        for k in range(1, side):
            peer = base + lax.rem(coord + k, side) * stride
            pl.semaphore_signal(barrier, 1, device_id={"dp": peer}, device_id_type=mesh_id)
    pl.semaphore_wait(barrier, 2 * (side - 1))

    def remote(r, src, dst, slot, target):
        return pltpu.make_async_remote_copy(
            src_ref=src,
            dst_ref=dst,
            send_sem=send_sems.at[r, slot],
            recv_sem=recv_sems.at[r, slot],
            device_id={"dp": target},
            device_id_type=mesh_id,
        )

    started, locals_, waits = [], [], []
    for r, (first, second) in enumerate(routes):
        c1, base1 = coords(first)
        c2, base2 = coords(second)
        out = outs[r]
        local = pltpu.make_async_copy(ins[r], out.at[c2, c1], local_sems.at[r])
        local.start()
        locals_.append(local)
        for k in range(1, side):
            copy = remote(r, ins[r], out.at[c2, c1], k - 1, base1 + lax.rem(c1 + k, side) * first)
            copy.start()
            started.append(copy)
        for k in range(1, side):
            slot = (side - 1) + (k - 1) * side
            target = base2 + lax.rem(c2 + k, side) * second
            copy = remote(r, ins[r], out.at[c2, c1], slot + 0, target)
            copy.start()
            started.append(copy)
        for j in range(1, side):
            held = lax.rem(c1 + side - j, side)
            remote(r, ins[r], out.at[c2, held], j - 1, base1 + held * first).wait_recv()
            for k in range(1, side):
                slot = (side - 1) + (k - 1) * side + j
                target = base2 + lax.rem(c2 + k, side) * second
                copy = remote(r, out.at[c2, held], out.at[c2, held], slot, target)
                copy.start()
                started.append(copy)
        for k in range(1, side):
            source = lax.rem(c2 + side - k, side)
            for j in range(side):
                slot = (side - 1) + (k - 1) * side + j
                held = lax.rem(c1 + side - j, side)
                waits.append(remote(r, out.at[source, held], out.at[source, held], slot, base2 + source * second))
    for copy in waits:
        copy.wait_recv()
    for local in locals_:
        local.wait()
    for copy in started:
        copy.wait_send()


def all_gather_2d(x, cid):
    side = 4
    half = x.shape[-1] // 2
    parts = [x[..., :half], x[..., half:]]
    n_slots = (side - 1) * (side + 1)
    got_a, got_b = pl.pallas_call(
        functools.partial(_gather_2d_kernel, side),
        out_shape=[jax.ShapeDtypeStruct((side, side) + p.shape, p.dtype) for p in parts],
        in_specs=[pl.BlockSpec(memory_space=pl.ANY)] * 2,
        out_specs=[pl.BlockSpec(memory_space=pl.ANY)] * 2,
        scratch_shapes=[
            pltpu.SemaphoreType.DMA((2,)),
            pltpu.SemaphoreType.DMA((2, n_slots)),
            pltpu.SemaphoreType.DMA((2, n_slots)),
        ],
        compiler_params=pltpu.CompilerParams(collective_id=cid, has_side_effects=True),
    )(*parts)
    n = side * side
    got_a = got_a.reshape((n,) + got_a.shape[2:])
    perm = (1, 0) + tuple(range(2, got_b.ndim))
    got_b = got_b.transpose(perm).reshape((n,) + got_b.shape[2:])
    return got_a, got_b


def body(
    context,
    out_weight,
    residual,
    gate_weight,
    up_weight,
    down_weight,
    gate_values,
    chosen_blocks,
    block_counts,
):
    n_dp = lax.axis_size("dp")
    n_expert = lax.axis_size("expert")
    local_tokens = context.shape[0]
    local_width = residual.shape[1]
    model_width = context.shape[1]
    local_blocks = local_tokens // BLK
    n_blocks = local_blocks * n_dp
    piece = BLK // n_dp
    my_expert = lax.axis_index("expert")

    w_a, w_b = all_gather_2d(out_weight, cid=10)
    w_a = w_a.reshape(model_width, -1)
    w_b = w_b.reshape(model_width, -1)
    projected = jnp.concatenate(
        [
            jnp.dot(context, w_a, preferred_element_type=jnp.float32),
            jnp.dot(context, w_b, preferred_element_type=jnp.float32),
        ],
        axis=1,
    )
    attended = (residual.astype(jnp.float32) + projected).astype(jnp.bfloat16)

    split = attended.reshape(local_blocks, n_dp, piece, local_width).transpose(1, 0, 2, 3)
    pieces = dp_exchange(split, gather=False, cid=0)
    pieces = pieces.reshape(n_blocks, piece, local_width)

    slots = jnp.take(pieces, chosen_blocks.reshape(-1), axis=0)
    slots = slots.reshape(n_expert, CAP, piece, local_width)
    mine = dp_exchange(slots, gather=False, cid=4, axis="expert")
    mine = mine.transpose(1, 2, 0, 3).reshape(CAP * piece, model_width)
    picked_a, picked_b = all_gather_2d(mine, cid=20)
    picked_a = picked_a.reshape(n_dp * CAP * piece, -1)
    picked_b = picked_b.reshape(n_dp * CAP * piece, -1)
    half = picked_a.shape[1]

    w_gate = gate_weight[0]
    w_up = up_weight[0]
    w_down = down_weight[0]
    gate_row = gate_values[0]
    my_count = lax.dynamic_index_in_dim(block_counts, my_expert, 0, keepdims=False)
    live = jnp.arange(CAP * BLK) // BLK < my_count
    scale = jnp.where(live, gate_row, jnp.zeros_like(gate_row))
    scale = scale.reshape(CAP, n_dp, piece).transpose(1, 0, 2).reshape(-1)

    gate = jnp.dot(picked_a, w_gate[:half], preferred_element_type=jnp.float32) + jnp.dot(
        picked_b, w_gate[half:], preferred_element_type=jnp.float32
    )
    upper = jnp.dot(picked_a, w_up[:half], preferred_element_type=jnp.float32) + jnp.dot(
        picked_b, w_up[half:], preferred_element_type=jnp.float32
    )
    hidden = (jax.nn.silu(gate) * upper).astype(jnp.bfloat16)
    part = jnp.dot(hidden, w_down, preferred_element_type=jnp.float32)
    part = (part * scale[:, None]).astype(jnp.bfloat16)

    summed = reduce_scatter_2d(part.reshape(n_dp, CAP * piece, model_width), cid=1)
    summed = summed.astype(jnp.bfloat16)
    summed = summed.reshape(CAP * piece, n_expert, local_width).transpose(1, 0, 2)
    outs = dp_exchange(summed, gather=False, cid=5, axis="expert")
    outs = outs.reshape(n_expert * CAP, piece * local_width)

    selector = chosen_blocks.reshape(-1)[None, :] == jnp.arange(n_blocks)[:, None]
    added = jnp.dot(selector.astype(jnp.bfloat16), outs, preferred_element_type=jnp.float32)
    mixed = pieces.reshape(n_blocks, piece * local_width).astype(jnp.float32) + added
    mixed = mixed.astype(jnp.bfloat16).reshape(n_dp, local_blocks, piece, local_width)
    back = dp_exchange(mixed, gather=False, cid=3)
    return back.transpose(1, 0, 2, 3).reshape(local_tokens, local_width)


def solution(mesh):
    in_specs = (
        P("dp", None),
        P("dp", "expert"),
        P("dp", "expert"),
        P("expert", None, "dp"),
        P("expert", None, "dp"),
        P("expert", "dp", None),
        P("expert", None),
        P(),
        P(),
    )
    out_specs = P("dp", "expert")
    return jax.shard_map(body, mesh=mesh, in_specs=in_specs, out_specs=out_specs, check_vma=False)
```

```python
import functools

import jax
import jax.numpy as jnp
from jax import lax
from jax.sharding import PartitionSpec as P
from jax.experimental import pallas as pl
from jax.experimental.pallas import tpu as pltpu

BLK = 128
CAP = 4


def _exchange_kernel(n, gather, axis, x_ref, o_ref, local_sem, send_sems, recv_sems):
    me = lax.axis_index(axis)
    mesh_id = pl.DeviceIdType.MESH
    barrier = pltpu.get_barrier_semaphore()
    for k in range(1, n):
        pl.semaphore_signal(barrier, 1, device_id={axis: lax.rem(me + k, n)}, device_id_type=mesh_id)
    pl.semaphore_wait(barrier, n - 1)
    local = pltpu.make_async_copy(x_ref if gather else x_ref.at[me], o_ref.at[me], local_sem)
    local.start()
    copies = []
    for k in range(1, n):
        target = lax.rem(me + k, n)
        copy = pltpu.make_async_remote_copy(
            src_ref=x_ref if gather else x_ref.at[target],
            dst_ref=o_ref.at[me],
            send_sem=send_sems.at[k - 1],
            recv_sem=recv_sems.at[k - 1],
            device_id={axis: target},
            device_id_type=mesh_id,
        )
        copy.start()
        copies.append(copy)
    local.wait()
    for copy in copies:
        copy.wait()


def dp_exchange(x, gather, cid, axis="dp"):
    n = lax.axis_size(axis)
    shape = (n,) + x.shape if gather else x.shape
    return pl.pallas_call(
        functools.partial(_exchange_kernel, n, gather, axis),
        out_shape=jax.ShapeDtypeStruct(shape, x.dtype),
        in_specs=[pl.BlockSpec(memory_space=pl.ANY)],
        out_specs=pl.BlockSpec(memory_space=pl.ANY),
        scratch_shapes=[
            pltpu.SemaphoreType.DMA(()),
            pltpu.SemaphoreType.DMA((n - 1,)),
            pltpu.SemaphoreType.DMA((n - 1,)),
        ],
        compiler_params=pltpu.CompilerParams(collective_id=cid, has_side_effects=True),
    )(x)


def _route_kernel(strides, side, gather, *refs):
    n_in = len(strides)
    ins, outs = refs[:n_in], refs[n_in:2 * n_in]
    local_sems, send_sems, recv_sems = refs[2 * n_in:]
    me = lax.axis_index("dp")
    mesh_id = pl.DeviceIdType.MESH
    routes = []
    for r, stride in enumerate(strides):
        coord = lax.rem(me // stride, side)
        base = me - coord * stride
        for k in range(1, side):
            to = lax.rem(coord + k, side)
            routes.append((r, coord, to, base + to * stride))
    barrier = pltpu.get_barrier_semaphore()
    for _, _, _, target in routes:
        pl.semaphore_signal(barrier, 1, device_id={"dp": target}, device_id_type=mesh_id)
    pl.semaphore_wait(barrier, len(routes))
    locals_ = []
    for r in range(n_in):
        coord = lax.rem(me // strides[r], side)
        source = ins[r] if gather else ins[r].at[coord]
        local = pltpu.make_async_copy(source, outs[r].at[coord], local_sems.at[r])
        local.start()
        locals_.append(local)
    copies = []
    for i, (r, coord, to, target) in enumerate(routes):
        copy = pltpu.make_async_remote_copy(
            src_ref=ins[r] if gather else ins[r].at[to],
            dst_ref=outs[r].at[coord],
            send_sem=send_sems.at[i],
            recv_sem=recv_sems.at[i],
            device_id={"dp": target},
            device_id_type=mesh_id,
        )
        copy.start()
        copies.append(copy)
    for local in locals_:
        local.wait()
    for copy in copies:
        copy.wait()


def dp_route(xs, strides, cid, side=4, gather=False):
    n_routes = len(strides) * (side - 1)
    shapes = [((side,) + x.shape) if gather else x.shape for x in xs]
    return pl.pallas_call(
        functools.partial(_route_kernel, tuple(strides), side, gather),
        out_shape=[jax.ShapeDtypeStruct(s, x.dtype) for s, x in zip(shapes, xs)],
        in_specs=[pl.BlockSpec(memory_space=pl.ANY)] * len(xs),
        out_specs=[pl.BlockSpec(memory_space=pl.ANY)] * len(xs),
        scratch_shapes=[
            pltpu.SemaphoreType.DMA((len(xs),)),
            pltpu.SemaphoreType.DMA((n_routes,)),
            pltpu.SemaphoreType.DMA((n_routes,)),
        ],
        compiler_params=pltpu.CompilerParams(collective_id=cid, has_side_effects=True),
    )(*xs)


def reduce_scatter_2d(part, cid):
    side = 4
    n_dp, rows, cols = part.shape
    half = cols // 2
    grid = part.reshape(side, side, rows, cols)
    first_a = grid[..., :half].transpose(1, 0, 2, 3)
    first_b = grid[..., half:]
    got_a, got_b = dp_route([first_a, first_b], (1, side), cid)
    second_a = got_a.astype(jnp.float32).sum(axis=0).astype(jnp.bfloat16)
    second_b = got_b.astype(jnp.float32).sum(axis=0).astype(jnp.bfloat16)
    got_a, got_b = dp_route([second_a, second_b], (side, 1), cid + 1)
    total_a = got_a.astype(jnp.float32).sum(axis=0)
    total_b = got_b.astype(jnp.float32).sum(axis=0)
    return jnp.concatenate([total_a, total_b], axis=-1)


def all_gather_2d(x, cid):
    side = 4
    half = x.shape[-1] // 2
    got_a, got_b = dp_route([x[..., :half], x[..., half:]], (1, side), cid, gather=True)
    got_a, got_b = dp_route([got_a, got_b], (side, 1), cid + 1, gather=True)
    n = side * side
    got_a = got_a.reshape((n,) + got_a.shape[2:])
    perm = (1, 0) + tuple(range(2, got_b.ndim))
    got_b = got_b.transpose(perm).reshape((n,) + got_b.shape[2:])
    return got_a, got_b


def _spread_kernel(n_dp, n_expert, chosen_ref, split_ref, pieces_ref, mine_ref,
                   held, outgoing, local_sems, dp_send, dp_recv, ex_send, ex_recv):
    me = lax.axis_index("dp")
    mine_e = lax.axis_index("expert")
    mesh_id = pl.DeviceIdType.MESH
    group = split_ref.shape[1]
    barrier = pltpu.get_barrier_semaphore()
    for k in range(1, n_dp):
        pl.semaphore_signal(barrier, 1, device_id={"dp": lax.rem(me + k, n_dp)}, device_id_type=mesh_id)
    for k in range(1, n_expert):
        pl.semaphore_signal(
            barrier, 1, device_id={"expert": lax.rem(mine_e + k, n_expert)}, device_id_type=mesh_id
        )
    pl.semaphore_wait(barrier, n_dp + n_expert - 2)

    def at_source(src):
        return held.at[pl.ds(pl.multiple_of(src * group, group), group)]

    local = pltpu.make_async_copy(split_ref.at[me], at_source(me), local_sems.at[0])
    local.start()
    copies = []
    for k in range(1, n_dp):
        target = lax.rem(me + k, n_dp)
        copy = pltpu.make_async_remote_copy(
            src_ref=split_ref.at[target],
            dst_ref=at_source(me),
            send_sem=dp_send.at[k - 1],
            recv_sem=dp_recv.at[k - 1],
            device_id={"dp": target},
            device_id_type=mesh_id,
        )
        copy.start()
        copies.append(copy)
    local.wait()
    for copy in copies:
        copy.wait()
    keep = pltpu.make_async_copy(held, pieces_ref, local_sems.at[1])
    keep.start()
    for e in range(n_expert):
        for s in range(CAP):
            outgoing[e, s] = held[chosen_ref[e * CAP + s]]
    local = pltpu.make_async_copy(outgoing.at[mine_e], mine_ref.at[mine_e], local_sems.at[2])
    local.start()
    copies = []
    for k in range(1, n_expert):
        target = lax.rem(mine_e + k, n_expert)
        copy = pltpu.make_async_remote_copy(
            src_ref=outgoing.at[target],
            dst_ref=mine_ref.at[mine_e],
            send_sem=ex_send.at[k - 1],
            recv_sem=ex_recv.at[k - 1],
            device_id={"expert": target},
            device_id_type=mesh_id,
        )
        copy.start()
        copies.append(copy)
    local.wait()
    for copy in copies:
        copy.wait()
    keep.wait()


def spread_select(chosen, split, cid):
    n_dp = lax.axis_size("dp")
    n_expert = lax.axis_size("expert")
    _, group, rows, width = split.shape
    n_blocks = n_dp * group
    return pl.pallas_call(
        functools.partial(_spread_kernel, n_dp, n_expert),
        out_shape=[
            jax.ShapeDtypeStruct((n_blocks, rows, width), split.dtype),
            jax.ShapeDtypeStruct((n_expert, CAP, rows, width), split.dtype),
        ],
        in_specs=[pl.BlockSpec(memory_space=pltpu.SMEM), pl.BlockSpec(memory_space=pl.ANY)],
        out_specs=[pl.BlockSpec(memory_space=pl.ANY)] * 2,
        scratch_shapes=[
            pltpu.VMEM((n_blocks, rows, width), split.dtype),
            pltpu.VMEM((n_expert, CAP, rows, width), split.dtype),
            pltpu.SemaphoreType.DMA((3,)),
            pltpu.SemaphoreType.DMA((n_dp - 1,)),
            pltpu.SemaphoreType.DMA((n_dp - 1,)),
            pltpu.SemaphoreType.DMA((n_expert - 1,)),
            pltpu.SemaphoreType.DMA((n_expert - 1,)),
        ],
        compiler_params=pltpu.CompilerParams(collective_id=cid, has_side_effects=True),
    )(chosen, split)


def body(
    context,
    out_weight,
    residual,
    gate_weight,
    up_weight,
    down_weight,
    gate_values,
    chosen_blocks,
    block_counts,
):
    n_dp = lax.axis_size("dp")
    n_expert = lax.axis_size("expert")
    local_tokens = context.shape[0]
    local_width = residual.shape[1]
    model_width = context.shape[1]
    local_blocks = local_tokens // BLK
    n_blocks = local_blocks * n_dp
    piece = BLK // n_dp
    my_expert = lax.axis_index("expert")

    w_a, w_b = all_gather_2d(out_weight, cid=10)
    w_a = w_a.reshape(model_width, -1)
    w_b = w_b.reshape(model_width, -1)
    projected = jnp.concatenate(
        [
            jnp.dot(context, w_a, preferred_element_type=jnp.float32),
            jnp.dot(context, w_b, preferred_element_type=jnp.float32),
        ],
        axis=1,
    )
    attended = (residual.astype(jnp.float32) + projected).astype(jnp.bfloat16)

    split = attended.reshape(local_blocks, n_dp, piece, local_width).transpose(1, 0, 2, 3)
    pieces, mine = spread_select(chosen_blocks.reshape(-1), split, cid=0)
    mine = mine.transpose(1, 2, 0, 3).reshape(CAP * piece, model_width)
    picked_a, picked_b = all_gather_2d(mine, cid=20)
    picked_a = picked_a.reshape(n_dp * CAP * piece, -1)
    picked_b = picked_b.reshape(n_dp * CAP * piece, -1)
    half = picked_a.shape[1]

    w_gate = gate_weight[0]
    w_up = up_weight[0]
    w_down = down_weight[0]
    gate_row = gate_values[0]
    my_count = lax.dynamic_index_in_dim(block_counts, my_expert, 0, keepdims=False)
    live = jnp.arange(CAP * BLK) // BLK < my_count
    scale = jnp.where(live, gate_row, jnp.zeros_like(gate_row))
    scale = scale.reshape(CAP, n_dp, piece).transpose(1, 0, 2).reshape(-1)

    gate = jnp.dot(picked_a, w_gate[:half], preferred_element_type=jnp.float32) + jnp.dot(
        picked_b, w_gate[half:], preferred_element_type=jnp.float32
    )
    upper = jnp.dot(picked_a, w_up[:half], preferred_element_type=jnp.float32) + jnp.dot(
        picked_b, w_up[half:], preferred_element_type=jnp.float32
    )
    hidden = (jax.nn.silu(gate) * upper).astype(jnp.bfloat16)
    part = jnp.dot(hidden, w_down, preferred_element_type=jnp.float32)
    part = (part * scale[:, None]).astype(jnp.bfloat16)

    summed = reduce_scatter_2d(part.reshape(n_dp, CAP * piece, model_width), cid=1)
    summed = summed.astype(jnp.bfloat16)
    summed = summed.reshape(CAP * piece, n_expert, local_width).transpose(1, 0, 2)
    outs = dp_exchange(summed, gather=False, cid=5, axis="expert")
    outs = outs.reshape(n_expert * CAP, piece * local_width)

    selector = chosen_blocks.reshape(-1)[None, :] == jnp.arange(n_blocks)[:, None]
    added = jnp.dot(selector.astype(jnp.bfloat16), outs, preferred_element_type=jnp.float32)
    mixed = pieces.reshape(n_blocks, piece * local_width).astype(jnp.float32) + added
    mixed = mixed.astype(jnp.bfloat16).reshape(n_dp, local_blocks, piece, local_width)
    back = dp_exchange(mixed, gather=False, cid=3)
    return back.transpose(1, 0, 2, 3).reshape(local_tokens, local_width)


def solution(mesh):
    in_specs = (
        P("dp", None),
        P("dp", "expert"),
        P("dp", "expert"),
        P("expert", None, "dp"),
        P("expert", None, "dp"),
        P("expert", "dp", None),
        P("expert", None),
        P(),
        P(),
    )
    out_specs = P("dp", "expert")
    return jax.shard_map(body, mesh=mesh, in_specs=in_specs, out_specs=out_specs, check_vma=False)
```

```python
import functools

import jax
import jax.numpy as jnp
from jax import lax
from jax.sharding import PartitionSpec as P
from jax.experimental import pallas as pl
from jax.experimental.pallas import tpu as pltpu

BLK = 128
CAP = 4


def _exchange_kernel(n, gather, axis, x_ref, o_ref, local_sem, send_sems, recv_sems):
    me = lax.axis_index(axis)
    mesh_id = pl.DeviceIdType.MESH
    barrier = pltpu.get_barrier_semaphore()
    for k in range(1, n):
        pl.semaphore_signal(barrier, 1, device_id={axis: lax.rem(me + k, n)}, device_id_type=mesh_id)
    pl.semaphore_wait(barrier, n - 1)
    local = pltpu.make_async_copy(x_ref if gather else x_ref.at[me], o_ref.at[me], local_sem)
    local.start()
    copies = []
    for k in range(1, n):
        target = lax.rem(me + k, n)
        copy = pltpu.make_async_remote_copy(
            src_ref=x_ref if gather else x_ref.at[target],
            dst_ref=o_ref.at[me],
            send_sem=send_sems.at[k - 1],
            recv_sem=recv_sems.at[k - 1],
            device_id={axis: target},
            device_id_type=mesh_id,
        )
        copy.start()
        copies.append(copy)
    local.wait()
    for copy in copies:
        copy.wait()


def dp_exchange(x, gather, cid, axis="dp"):
    n = lax.axis_size(axis)
    shape = (n,) + x.shape if gather else x.shape
    return pl.pallas_call(
        functools.partial(_exchange_kernel, n, gather, axis),
        out_shape=jax.ShapeDtypeStruct(shape, x.dtype),
        in_specs=[pl.BlockSpec(memory_space=pl.ANY)],
        out_specs=pl.BlockSpec(memory_space=pl.ANY),
        scratch_shapes=[
            pltpu.SemaphoreType.DMA(()),
            pltpu.SemaphoreType.DMA((n - 1,)),
            pltpu.SemaphoreType.DMA((n - 1,)),
        ],
        compiler_params=pltpu.CompilerParams(collective_id=cid, has_side_effects=True),
    )(x)


def _route_kernel(strides, side, gather, *refs):
    n_in = len(strides)
    ins, outs = refs[:n_in], refs[n_in:2 * n_in]
    local_sems, send_sems, recv_sems = refs[2 * n_in:]
    me = lax.axis_index("dp")
    mesh_id = pl.DeviceIdType.MESH
    routes = []
    for r, stride in enumerate(strides):
        coord = lax.rem(me // stride, side)
        base = me - coord * stride
        for k in range(1, side):
            to = lax.rem(coord + k, side)
            routes.append((r, coord, to, base + to * stride))
    barrier = pltpu.get_barrier_semaphore()
    for _, _, _, target in routes:
        pl.semaphore_signal(barrier, 1, device_id={"dp": target}, device_id_type=mesh_id)
    pl.semaphore_wait(barrier, len(routes))
    locals_ = []
    for r in range(n_in):
        coord = lax.rem(me // strides[r], side)
        source = ins[r] if gather else ins[r].at[coord]
        local = pltpu.make_async_copy(source, outs[r].at[coord], local_sems.at[r])
        local.start()
        locals_.append(local)
    copies = []
    for i, (r, coord, to, target) in enumerate(routes):
        copy = pltpu.make_async_remote_copy(
            src_ref=ins[r] if gather else ins[r].at[to],
            dst_ref=outs[r].at[coord],
            send_sem=send_sems.at[i],
            recv_sem=recv_sems.at[i],
            device_id={"dp": target},
            device_id_type=mesh_id,
        )
        copy.start()
        copies.append(copy)
    for local in locals_:
        local.wait()
    for copy in copies:
        copy.wait()


def dp_route(xs, strides, cid, side=4, gather=False):
    n_routes = len(strides) * (side - 1)
    shapes = [((side,) + x.shape) if gather else x.shape for x in xs]
    return pl.pallas_call(
        functools.partial(_route_kernel, tuple(strides), side, gather),
        out_shape=[jax.ShapeDtypeStruct(s, x.dtype) for s, x in zip(shapes, xs)],
        in_specs=[pl.BlockSpec(memory_space=pl.ANY)] * len(xs),
        out_specs=[pl.BlockSpec(memory_space=pl.ANY)] * len(xs),
        scratch_shapes=[
            pltpu.SemaphoreType.DMA((len(xs),)),
            pltpu.SemaphoreType.DMA((n_routes,)),
            pltpu.SemaphoreType.DMA((n_routes,)),
        ],
        compiler_params=pltpu.CompilerParams(collective_id=cid, has_side_effects=True),
    )(*xs)


def _finish_kernel(side, n_expert, a_ref, b_ref, out_ref, got_a, got_b, outgoing,
                   local_sems, send_sems, recv_sems, ex_send, ex_recv):
    me = lax.axis_index("dp")
    mine_e = lax.axis_index("expert")
    mesh_id = pl.DeviceIdType.MESH
    routes = ((a_ref, got_a, side), (b_ref, got_b, 1))
    barrier = pltpu.get_barrier_semaphore()
    for _, _, stride in routes:
        coord = lax.rem(me // stride, side)
        base = me - coord * stride
        for k in range(1, side):
            peer = base + lax.rem(coord + k, side) * stride
            pl.semaphore_signal(barrier, 1, device_id={"dp": peer}, device_id_type=mesh_id)
    for k in range(1, n_expert):
        pl.semaphore_signal(
            barrier, 1, device_id={"expert": lax.rem(mine_e + k, n_expert)}, device_id_type=mesh_id
        )
    pl.semaphore_wait(barrier, 2 * (side - 1) + n_expert - 1)
    locals_, copies = [], []
    for r, (src, dst, stride) in enumerate(routes):
        coord = lax.rem(me // stride, side)
        base = me - coord * stride
        local = pltpu.make_async_copy(src.at[coord], dst.at[coord], local_sems.at[r])
        local.start()
        locals_.append(local)
        for k in range(1, side):
            to = lax.rem(coord + k, side)
            copy = pltpu.make_async_remote_copy(
                src_ref=src.at[to],
                dst_ref=dst.at[coord],
                send_sem=send_sems.at[r, k - 1],
                recv_sem=recv_sems.at[r, k - 1],
                device_id={"dp": base + to * stride},
                device_id_type=mesh_id,
            )
            copy.start()
            copies.append(copy)
    for local in locals_:
        local.wait()
    for copy in copies:
        copy.wait()
    width = outgoing.shape[-1]
    per_half = got_a.shape[-1] // width
    for h, got in enumerate((got_a, got_b)):
        total = got[0].astype(jnp.float32)
        for j in range(1, side):
            total = total + got[j].astype(jnp.float32)
        total = total.astype(outgoing.dtype)
        for j in range(per_half):
            outgoing[h * per_half + j] = total[:, j * width:(j + 1) * width]
    local = pltpu.make_async_copy(outgoing.at[mine_e], out_ref.at[mine_e], local_sems.at[2])
    local.start()
    copies = []
    for k in range(1, n_expert):
        target = lax.rem(mine_e + k, n_expert)
        copy = pltpu.make_async_remote_copy(
            src_ref=outgoing.at[target],
            dst_ref=out_ref.at[mine_e],
            send_sem=ex_send.at[k - 1],
            recv_sem=ex_recv.at[k - 1],
            device_id={"expert": target},
            device_id_type=mesh_id,
        )
        copy.start()
        copies.append(copy)
    local.wait()
    for copy in copies:
        copy.wait()


def reduce_scatter_2d(part, cid):
    side = 4
    n_expert = lax.axis_size("expert")
    n_dp, rows, cols = part.shape
    half = cols // 2
    width = cols // n_expert
    grid = part.reshape(side, side, rows, cols)
    first_a = grid[..., :half].transpose(1, 0, 2, 3)
    first_b = grid[..., half:]
    got_a, got_b = dp_route([first_a, first_b], (1, side), cid)
    second_a = got_a.astype(jnp.float32).sum(axis=0).astype(jnp.bfloat16)
    second_b = got_b.astype(jnp.float32).sum(axis=0).astype(jnp.bfloat16)
    return pl.pallas_call(
        functools.partial(_finish_kernel, side, n_expert),
        out_shape=jax.ShapeDtypeStruct((n_expert, rows, width), part.dtype),
        in_specs=[pl.BlockSpec(memory_space=pl.ANY)] * 2,
        out_specs=pl.BlockSpec(memory_space=pl.ANY),
        scratch_shapes=[
            pltpu.VMEM(second_a.shape, second_a.dtype),
            pltpu.VMEM(second_b.shape, second_b.dtype),
            pltpu.VMEM((n_expert, rows, width), part.dtype),
            pltpu.SemaphoreType.DMA((3,)),
            pltpu.SemaphoreType.DMA((2, side - 1)),
            pltpu.SemaphoreType.DMA((2, side - 1)),
            pltpu.SemaphoreType.DMA((n_expert - 1,)),
            pltpu.SemaphoreType.DMA((n_expert - 1,)),
        ],
        compiler_params=pltpu.CompilerParams(collective_id=cid + 1, has_side_effects=True),
    )(second_a, second_b)


def all_gather_2d(x, cid):
    side = 4
    half = x.shape[-1] // 2
    got_a, got_b = dp_route([x[..., :half], x[..., half:]], (1, side), cid, gather=True)
    got_a, got_b = dp_route([got_a, got_b], (side, 1), cid + 1, gather=True)
    n = side * side
    got_a = got_a.reshape((n,) + got_a.shape[2:])
    perm = (1, 0) + tuple(range(2, got_b.ndim))
    got_b = got_b.transpose(perm).reshape((n,) + got_b.shape[2:])
    return got_a, got_b


def _spread_kernel(n_dp, n_expert, chosen_ref, split_ref, pieces_ref, mine_ref,
                   held, outgoing, local_sems, dp_send, dp_recv, ex_send, ex_recv):
    me = lax.axis_index("dp")
    mine_e = lax.axis_index("expert")
    mesh_id = pl.DeviceIdType.MESH
    group = split_ref.shape[1]
    barrier = pltpu.get_barrier_semaphore()
    for k in range(1, n_dp):
        pl.semaphore_signal(barrier, 1, device_id={"dp": lax.rem(me + k, n_dp)}, device_id_type=mesh_id)
    for k in range(1, n_expert):
        pl.semaphore_signal(
            barrier, 1, device_id={"expert": lax.rem(mine_e + k, n_expert)}, device_id_type=mesh_id
        )
    pl.semaphore_wait(barrier, n_dp + n_expert - 2)

    def at_source(src):
        return held.at[pl.ds(pl.multiple_of(src * group, group), group)]

    local = pltpu.make_async_copy(split_ref.at[me], at_source(me), local_sems.at[0])
    local.start()
    copies = []
    for k in range(1, n_dp):
        target = lax.rem(me + k, n_dp)
        copy = pltpu.make_async_remote_copy(
            src_ref=split_ref.at[target],
            dst_ref=at_source(me),
            send_sem=dp_send.at[k - 1],
            recv_sem=dp_recv.at[k - 1],
            device_id={"dp": target},
            device_id_type=mesh_id,
        )
        copy.start()
        copies.append(copy)
    local.wait()
    for copy in copies:
        copy.wait()
    keep = pltpu.make_async_copy(held, pieces_ref, local_sems.at[1])
    keep.start()
    for e in range(n_expert):
        for s in range(CAP):
            outgoing[e, s] = held[chosen_ref[e * CAP + s]]
    local = pltpu.make_async_copy(outgoing.at[mine_e], mine_ref.at[mine_e], local_sems.at[2])
    local.start()
    copies = []
    for k in range(1, n_expert):
        target = lax.rem(mine_e + k, n_expert)
        copy = pltpu.make_async_remote_copy(
            src_ref=outgoing.at[target],
            dst_ref=mine_ref.at[mine_e],
            send_sem=ex_send.at[k - 1],
            recv_sem=ex_recv.at[k - 1],
            device_id={"expert": target},
            device_id_type=mesh_id,
        )
        copy.start()
        copies.append(copy)
    local.wait()
    for copy in copies:
        copy.wait()
    keep.wait()


def spread_select(chosen, split, cid):
    n_dp = lax.axis_size("dp")
    n_expert = lax.axis_size("expert")
    _, group, rows, width = split.shape
    n_blocks = n_dp * group
    return pl.pallas_call(
        functools.partial(_spread_kernel, n_dp, n_expert),
        out_shape=[
            jax.ShapeDtypeStruct((n_blocks, rows, width), split.dtype),
            jax.ShapeDtypeStruct((n_expert, CAP, rows, width), split.dtype),
        ],
        in_specs=[pl.BlockSpec(memory_space=pltpu.SMEM), pl.BlockSpec(memory_space=pl.ANY)],
        out_specs=[pl.BlockSpec(memory_space=pl.ANY)] * 2,
        scratch_shapes=[
            pltpu.VMEM((n_blocks, rows, width), split.dtype),
            pltpu.VMEM((n_expert, CAP, rows, width), split.dtype),
            pltpu.SemaphoreType.DMA((3,)),
            pltpu.SemaphoreType.DMA((n_dp - 1,)),
            pltpu.SemaphoreType.DMA((n_dp - 1,)),
            pltpu.SemaphoreType.DMA((n_expert - 1,)),
            pltpu.SemaphoreType.DMA((n_expert - 1,)),
        ],
        compiler_params=pltpu.CompilerParams(collective_id=cid, has_side_effects=True),
    )(chosen, split)


def body(
    context,
    out_weight,
    residual,
    gate_weight,
    up_weight,
    down_weight,
    gate_values,
    chosen_blocks,
    block_counts,
):
    n_dp = lax.axis_size("dp")
    n_expert = lax.axis_size("expert")
    local_tokens = context.shape[0]
    local_width = residual.shape[1]
    model_width = context.shape[1]
    local_blocks = local_tokens // BLK
    n_blocks = local_blocks * n_dp
    piece = BLK // n_dp
    my_expert = lax.axis_index("expert")

    w_a, w_b = all_gather_2d(out_weight, cid=10)
    w_a = w_a.reshape(model_width, -1)
    w_b = w_b.reshape(model_width, -1)
    projected = jnp.concatenate(
        [
            jnp.dot(context, w_a, preferred_element_type=jnp.float32),
            jnp.dot(context, w_b, preferred_element_type=jnp.float32),
        ],
        axis=1,
    )
    attended = (residual.astype(jnp.float32) + projected).astype(jnp.bfloat16)

    split = attended.reshape(local_blocks, n_dp, piece, local_width).transpose(1, 0, 2, 3)
    pieces, mine = spread_select(chosen_blocks.reshape(-1), split, cid=0)
    mine = mine.transpose(1, 2, 0, 3).reshape(CAP * piece, model_width)
    picked_a, picked_b = all_gather_2d(mine, cid=20)
    picked_a = picked_a.reshape(n_dp * CAP * piece, -1)
    picked_b = picked_b.reshape(n_dp * CAP * piece, -1)
    half = picked_a.shape[1]

    w_gate = gate_weight[0]
    w_up = up_weight[0]
    w_down = down_weight[0]
    gate_row = gate_values[0]
    my_count = lax.dynamic_index_in_dim(block_counts, my_expert, 0, keepdims=False)
    live = jnp.arange(CAP * BLK) // BLK < my_count
    scale = jnp.where(live, gate_row, jnp.zeros_like(gate_row))
    scale = scale.reshape(CAP, n_dp, piece).transpose(1, 0, 2).reshape(-1)

    gate = jnp.dot(picked_a, w_gate[:half], preferred_element_type=jnp.float32) + jnp.dot(
        picked_b, w_gate[half:], preferred_element_type=jnp.float32
    )
    upper = jnp.dot(picked_a, w_up[:half], preferred_element_type=jnp.float32) + jnp.dot(
        picked_b, w_up[half:], preferred_element_type=jnp.float32
    )
    hidden = (jax.nn.silu(gate) * upper).astype(jnp.bfloat16)
    part = jnp.dot(hidden, w_down, preferred_element_type=jnp.float32)
    part = (part * scale[:, None]).astype(jnp.bfloat16)

    outs = reduce_scatter_2d(part.reshape(n_dp, CAP * piece, model_width), cid=1)
    outs = outs.reshape(n_expert * CAP, piece * local_width)

    selector = chosen_blocks.reshape(-1)[None, :] == jnp.arange(n_blocks)[:, None]
    added = jnp.dot(selector.astype(jnp.bfloat16), outs, preferred_element_type=jnp.float32)
    mixed = pieces.reshape(n_blocks, piece * local_width).astype(jnp.float32) + added
    mixed = mixed.astype(jnp.bfloat16).reshape(n_dp, local_blocks, piece, local_width)
    back = dp_exchange(mixed, gather=False, cid=3)
    return back.transpose(1, 0, 2, 3).reshape(local_tokens, local_width)


def solution(mesh):
    in_specs = (
        P("dp", None),
        P("dp", "expert"),
        P("dp", "expert"),
        P("expert", None, "dp"),
        P("expert", None, "dp"),
        P("expert", "dp", None),
        P("expert", None),
        P(),
        P(),
    )
    out_specs = P("dp", "expert")
    return jax.shard_map(body, mesh=mesh, in_specs=in_specs, out_specs=out_specs, check_vma=False)
```

```python
import functools

import jax
import jax.numpy as jnp
from jax import lax
from jax.sharding import PartitionSpec as P
from jax.experimental import pallas as pl
from jax.experimental.pallas import tpu as pltpu

BLK = 128
CAP = 4


def _exchange_kernel(n, gather, axis, x_ref, o_ref, local_sem, send_sems, recv_sems):
    me = lax.axis_index(axis)
    mesh_id = pl.DeviceIdType.MESH
    barrier = pltpu.get_barrier_semaphore()
    for k in range(1, n):
        pl.semaphore_signal(barrier, 1, device_id={axis: lax.rem(me + k, n)}, device_id_type=mesh_id)
    pl.semaphore_wait(barrier, n - 1)
    local = pltpu.make_async_copy(x_ref if gather else x_ref.at[me], o_ref.at[me], local_sem)
    local.start()
    copies = []
    for k in range(1, n):
        target = lax.rem(me + k, n)
        copy = pltpu.make_async_remote_copy(
            src_ref=x_ref if gather else x_ref.at[target],
            dst_ref=o_ref.at[me],
            send_sem=send_sems.at[k - 1],
            recv_sem=recv_sems.at[k - 1],
            device_id={axis: target},
            device_id_type=mesh_id,
        )
        copy.start()
        copies.append(copy)
    local.wait()
    for copy in copies:
        copy.wait()


def dp_exchange(x, gather, cid, axis="dp"):
    n = lax.axis_size(axis)
    shape = (n,) + x.shape if gather else x.shape
    return pl.pallas_call(
        functools.partial(_exchange_kernel, n, gather, axis),
        out_shape=jax.ShapeDtypeStruct(shape, x.dtype),
        in_specs=[pl.BlockSpec(memory_space=pl.ANY)],
        out_specs=pl.BlockSpec(memory_space=pl.ANY),
        scratch_shapes=[
            pltpu.SemaphoreType.DMA(()),
            pltpu.SemaphoreType.DMA((n - 1,)),
            pltpu.SemaphoreType.DMA((n - 1,)),
        ],
        compiler_params=pltpu.CompilerParams(collective_id=cid, has_side_effects=True),
    )(x)


def _route_kernel(strides, side, gather, *refs):
    n_in = len(strides)
    ins, outs = refs[:n_in], refs[n_in:2 * n_in]
    local_sems, send_sems, recv_sems = refs[2 * n_in:]
    me = lax.axis_index("dp")
    mesh_id = pl.DeviceIdType.MESH
    routes = []
    for r, stride in enumerate(strides):
        coord = lax.rem(me // stride, side)
        base = me - coord * stride
        for k in range(1, side):
            to = lax.rem(coord + k, side)
            routes.append((r, coord, to, base + to * stride))
    barrier = pltpu.get_barrier_semaphore()
    for _, _, _, target in routes:
        pl.semaphore_signal(barrier, 1, device_id={"dp": target}, device_id_type=mesh_id)
    pl.semaphore_wait(barrier, len(routes))
    locals_ = []
    for r in range(n_in):
        coord = lax.rem(me // strides[r], side)
        source = ins[r] if gather else ins[r].at[coord]
        local = pltpu.make_async_copy(source, outs[r].at[coord], local_sems.at[r])
        local.start()
        locals_.append(local)
    copies = []
    for i, (r, coord, to, target) in enumerate(routes):
        copy = pltpu.make_async_remote_copy(
            src_ref=ins[r] if gather else ins[r].at[to],
            dst_ref=outs[r].at[coord],
            send_sem=send_sems.at[i],
            recv_sem=recv_sems.at[i],
            device_id={"dp": target},
            device_id_type=mesh_id,
        )
        copy.start()
        copies.append(copy)
    for local in locals_:
        local.wait()
    for copy in copies:
        copy.wait()


def dp_route(xs, strides, cid, side=4, gather=False):
    n_routes = len(strides) * (side - 1)
    shapes = [((side,) + x.shape) if gather else x.shape for x in xs]
    return pl.pallas_call(
        functools.partial(_route_kernel, tuple(strides), side, gather),
        out_shape=[jax.ShapeDtypeStruct(s, x.dtype) for s, x in zip(shapes, xs)],
        in_specs=[pl.BlockSpec(memory_space=pl.ANY)] * len(xs),
        out_specs=[pl.BlockSpec(memory_space=pl.ANY)] * len(xs),
        scratch_shapes=[
            pltpu.SemaphoreType.DMA((len(xs),)),
            pltpu.SemaphoreType.DMA((n_routes,)),
            pltpu.SemaphoreType.DMA((n_routes,)),
        ],
        compiler_params=pltpu.CompilerParams(collective_id=cid, has_side_effects=True),
    )(*xs)


def _finish_kernel(side, n_expert, a_ref, b_ref, out_ref, got_a, got_b, outgoing,
                   local_sems, send_sems, recv_sems, ex_send, ex_recv):
    me = lax.axis_index("dp")
    mine_e = lax.axis_index("expert")
    mesh_id = pl.DeviceIdType.MESH
    routes = ((a_ref, got_a, side), (b_ref, got_b, 1))
    barrier = pltpu.get_barrier_semaphore()
    for _, _, stride in routes:
        coord = lax.rem(me // stride, side)
        base = me - coord * stride
        for k in range(1, side):
            peer = base + lax.rem(coord + k, side) * stride
            pl.semaphore_signal(barrier, 1, device_id={"dp": peer}, device_id_type=mesh_id)
    for k in range(1, n_expert):
        pl.semaphore_signal(
            barrier, 1, device_id={"expert": lax.rem(mine_e + k, n_expert)}, device_id_type=mesh_id
        )
    pl.semaphore_wait(barrier, 2 * (side - 1) + n_expert - 1)
    locals_, copies = [], []
    for r, (src, dst, stride) in enumerate(routes):
        coord = lax.rem(me // stride, side)
        base = me - coord * stride
        local = pltpu.make_async_copy(src.at[coord], dst.at[coord], local_sems.at[r])
        local.start()
        locals_.append(local)
        for k in range(1, side):
            to = lax.rem(coord + k, side)
            copy = pltpu.make_async_remote_copy(
                src_ref=src.at[to],
                dst_ref=dst.at[coord],
                send_sem=send_sems.at[r, k - 1],
                recv_sem=recv_sems.at[r, k - 1],
                device_id={"dp": base + to * stride},
                device_id_type=mesh_id,
            )
            copy.start()
            copies.append(copy)
    for local in locals_:
        local.wait()
    for copy in copies:
        copy.wait()
    width = outgoing.shape[-1]
    per_half = got_a.shape[-1] // width
    for h, got in enumerate((got_a, got_b)):
        total = got[0].astype(jnp.float32)
        for j in range(1, side):
            total = total + got[j].astype(jnp.float32)
        total = total.astype(outgoing.dtype)
        for j in range(per_half):
            outgoing[h * per_half + j] = total[:, j * width:(j + 1) * width]
    local = pltpu.make_async_copy(outgoing.at[mine_e], out_ref.at[mine_e], local_sems.at[2])
    local.start()
    copies = []
    for k in range(1, n_expert):
        target = lax.rem(mine_e + k, n_expert)
        copy = pltpu.make_async_remote_copy(
            src_ref=outgoing.at[target],
            dst_ref=out_ref.at[mine_e],
            send_sem=ex_send.at[k - 1],
            recv_sem=ex_recv.at[k - 1],
            device_id={"expert": target},
            device_id_type=mesh_id,
        )
        copy.start()
        copies.append(copy)
    local.wait()
    for copy in copies:
        copy.wait()


def reduce_scatter_2d(part, cid):
    side = 4
    n_expert = lax.axis_size("expert")
    n_dp, rows, cols = part.shape
    half = cols // 2
    width = cols // n_expert
    grid = part.reshape(side, side, rows, cols)
    first_a = grid[..., :half].transpose(1, 0, 2, 3)
    first_b = grid[..., half:]
    got_a, got_b = dp_route([first_a, first_b], (1, side), cid)
    second_a = got_a.astype(jnp.float32).sum(axis=0).astype(jnp.bfloat16)
    second_b = got_b.astype(jnp.float32).sum(axis=0).astype(jnp.bfloat16)
    return pl.pallas_call(
        functools.partial(_finish_kernel, side, n_expert),
        out_shape=jax.ShapeDtypeStruct((n_expert, rows, width), part.dtype),
        in_specs=[pl.BlockSpec(memory_space=pl.ANY)] * 2,
        out_specs=pl.BlockSpec(memory_space=pl.ANY),
        scratch_shapes=[
            pltpu.VMEM(second_a.shape, second_a.dtype),
            pltpu.VMEM(second_b.shape, second_b.dtype),
            pltpu.VMEM((n_expert, rows, width), part.dtype),
            pltpu.SemaphoreType.DMA((3,)),
            pltpu.SemaphoreType.DMA((2, side - 1)),
            pltpu.SemaphoreType.DMA((2, side - 1)),
            pltpu.SemaphoreType.DMA((n_expert - 1,)),
            pltpu.SemaphoreType.DMA((n_expert - 1,)),
        ],
        compiler_params=pltpu.CompilerParams(collective_id=cid + 1, has_side_effects=True),
    )(second_a, second_b)


def all_gather_2d(x, cid):
    side = 4
    half = x.shape[-1] // 2
    got_a, got_b = dp_route([x[..., :half], x[..., half:]], (1, side), cid, gather=True)
    got_a, got_b = dp_route([got_a, got_b], (side, 1), cid + 1, gather=True)
    n = side * side
    got_a = got_a.reshape((n,) + got_a.shape[2:])
    perm = (1, 0) + tuple(range(2, got_b.ndim))
    got_b = got_b.transpose(perm).reshape((n,) + got_b.shape[2:])
    return got_a, got_b


def _gather_gate_kernel(side, a_ref, b_ref, wg_ref, wu_ref, hidden_ref,
                        got_a, got_b, acc_g, acc_u, local_sems, send_sems, recv_sems):
    me = lax.axis_index("dp")
    mesh_id = pl.DeviceIdType.MESH
    half = a_ref.shape[-1]
    group = got_a.shape[1] * got_a.shape[2]
    rows = got_a.shape[2]
    routes = ((a_ref, got_a, side), (b_ref, got_b, 1))
    geo = []
    for _, _, stride in routes:
        coord = lax.rem(me // stride, side)
        geo.append((coord, me - coord * stride))
    barrier = pltpu.get_barrier_semaphore()
    for (coord, base), (_, _, stride) in zip(geo, routes):
        for k in range(1, side):
            peer = base + lax.rem(coord + k, side) * stride
            pl.semaphore_signal(barrier, 1, device_id={"dp": peer}, device_id_type=mesh_id)
    pl.semaphore_wait(barrier, 2 * (side - 1))

    def remote(r, k, source, to):
        src, dst, stride = routes[r]
        coord, base = geo[r]
        return pltpu.make_async_remote_copy(
            src_ref=src,
            dst_ref=dst.at[source],
            send_sem=send_sems.at[r, k - 1],
            recv_sem=recv_sems.at[r, k - 1],
            device_id={"dp": base + to * stride},
            device_id_type=mesh_id,
        )

    locals_, sends = [], []
    for r, (src, dst, stride) in enumerate(routes):
        coord, base = geo[r]
        local = pltpu.make_async_copy(src, dst.at[coord], local_sems.at[r])
        local.start()
        locals_.append(local)
        for k in range(1, side):
            copy = remote(r, k, coord, lax.rem(coord + k, side))
            copy.start()
            sends.append(copy)
    acc_g[...] = jnp.zeros_like(acc_g)
    acc_u[...] = jnp.zeros_like(acc_u)

    def add_a(source):
        block = got_a[source].reshape(group, half)
        at = pl.ds(pl.multiple_of(source * group, group), group)
        acc_g[at] += jnp.dot(block, wg_ref[:half], preferred_element_type=jnp.float32)
        acc_u[at] += jnp.dot(block, wu_ref[:half], preferred_element_type=jnp.float32)

    def add_b(source):
        block = got_b[source].reshape(group, half)
        g = jnp.dot(block, wg_ref[half:], preferred_element_type=jnp.float32)
        u = jnp.dot(block, wu_ref[half:], preferred_element_type=jnp.float32)
        for x in range(side):
            at = pl.ds(pl.multiple_of((x * side + source) * rows, rows), rows)
            acc_g[at] += g[x * rows:(x + 1) * rows]
            acc_u[at] += u[x * rows:(x + 1) * rows]

    for local in locals_:
        local.wait()
    add_a(geo[0][0])
    add_b(geo[1][0])
    for k in range(1, side):
        for r, add in ((0, add_a), (1, add_b)):
            coord, _ = geo[r]
            source = lax.rem(coord + side - k, side)
            remote(r, k, source, source).wait_recv()
            add(source)
    g = acc_g[...]
    hidden_ref[...] = (g / (1.0 + jnp.exp(-g)) * acc_u[...]).astype(hidden_ref.dtype)
    for copy in sends:
        copy.wait_send()


def gather_gate(x, w_gate, w_up, cid):
    side = 4
    n = side * side
    half = x.shape[-1] // 2
    first_a, first_b = dp_route([x[..., :half], x[..., half:]], (1, side), cid, gather=True)
    return pl.pallas_call(
        functools.partial(_gather_gate_kernel, side),
        out_shape=jax.ShapeDtypeStruct((n * x.shape[0], w_gate.shape[1]), jnp.bfloat16),
        in_specs=[pl.BlockSpec(memory_space=pl.ANY)] * 2 + [pl.BlockSpec(memory_space=pltpu.VMEM)] * 2,
        out_specs=pl.BlockSpec(memory_space=pltpu.VMEM),
        scratch_shapes=[
            pltpu.VMEM((side,) + first_a.shape, first_a.dtype),
            pltpu.VMEM((side,) + first_b.shape, first_b.dtype),
            pltpu.VMEM((n * x.shape[0], w_gate.shape[1]), jnp.float32),
            pltpu.VMEM((n * x.shape[0], w_gate.shape[1]), jnp.float32),
            pltpu.SemaphoreType.DMA((2,)),
            pltpu.SemaphoreType.DMA((2, side - 1)),
            pltpu.SemaphoreType.DMA((2, side - 1)),
        ],
        compiler_params=pltpu.CompilerParams(collective_id=cid + 1, has_side_effects=True),
    )(first_a, first_b, w_gate, w_up)


def _spread_kernel(n_dp, n_expert, chosen_ref, split_ref, pieces_ref, mine_ref,
                   held, outgoing, local_sems, dp_send, dp_recv, ex_send, ex_recv):
    me = lax.axis_index("dp")
    mine_e = lax.axis_index("expert")
    mesh_id = pl.DeviceIdType.MESH
    group = split_ref.shape[1]
    barrier = pltpu.get_barrier_semaphore()
    for k in range(1, n_dp):
        pl.semaphore_signal(barrier, 1, device_id={"dp": lax.rem(me + k, n_dp)}, device_id_type=mesh_id)
    for k in range(1, n_expert):
        pl.semaphore_signal(
            barrier, 1, device_id={"expert": lax.rem(mine_e + k, n_expert)}, device_id_type=mesh_id
        )
    pl.semaphore_wait(barrier, n_dp + n_expert - 2)

    def at_source(src):
        return held.at[pl.ds(pl.multiple_of(src * group, group), group)]

    local = pltpu.make_async_copy(split_ref.at[me], at_source(me), local_sems.at[0])
    local.start()
    copies = []
    for k in range(1, n_dp):
        target = lax.rem(me + k, n_dp)
        copy = pltpu.make_async_remote_copy(
            src_ref=split_ref.at[target],
            dst_ref=at_source(me),
            send_sem=dp_send.at[k - 1],
            recv_sem=dp_recv.at[k - 1],
            device_id={"dp": target},
            device_id_type=mesh_id,
        )
        copy.start()
        copies.append(copy)
    local.wait()
    for copy in copies:
        copy.wait()
    keep = pltpu.make_async_copy(held, pieces_ref, local_sems.at[1])
    keep.start()
    for e in range(n_expert):
        for s in range(CAP):
            outgoing[e, s] = held[chosen_ref[e * CAP + s]]
    local = pltpu.make_async_copy(outgoing.at[mine_e], mine_ref.at[mine_e], local_sems.at[2])
    local.start()
    copies = []
    for k in range(1, n_expert):
        target = lax.rem(mine_e + k, n_expert)
        copy = pltpu.make_async_remote_copy(
            src_ref=outgoing.at[target],
            dst_ref=mine_ref.at[mine_e],
            send_sem=ex_send.at[k - 1],
            recv_sem=ex_recv.at[k - 1],
            device_id={"expert": target},
            device_id_type=mesh_id,
        )
        copy.start()
        copies.append(copy)
    local.wait()
    for copy in copies:
        copy.wait()
    keep.wait()


def spread_select(chosen, split, cid):
    n_dp = lax.axis_size("dp")
    n_expert = lax.axis_size("expert")
    _, group, rows, width = split.shape
    n_blocks = n_dp * group
    return pl.pallas_call(
        functools.partial(_spread_kernel, n_dp, n_expert),
        out_shape=[
            jax.ShapeDtypeStruct((n_blocks, rows, width), split.dtype),
            jax.ShapeDtypeStruct((n_expert, CAP, rows, width), split.dtype),
        ],
        in_specs=[pl.BlockSpec(memory_space=pltpu.SMEM), pl.BlockSpec(memory_space=pl.ANY)],
        out_specs=[pl.BlockSpec(memory_space=pl.ANY)] * 2,
        scratch_shapes=[
            pltpu.VMEM((n_blocks, rows, width), split.dtype),
            pltpu.VMEM((n_expert, CAP, rows, width), split.dtype),
            pltpu.SemaphoreType.DMA((3,)),
            pltpu.SemaphoreType.DMA((n_dp - 1,)),
            pltpu.SemaphoreType.DMA((n_dp - 1,)),
            pltpu.SemaphoreType.DMA((n_expert - 1,)),
            pltpu.SemaphoreType.DMA((n_expert - 1,)),
        ],
        compiler_params=pltpu.CompilerParams(collective_id=cid, has_side_effects=True),
    )(chosen, split)


def body(
    context,
    out_weight,
    residual,
    gate_weight,
    up_weight,
    down_weight,
    gate_values,
    chosen_blocks,
    block_counts,
):
    n_dp = lax.axis_size("dp")
    n_expert = lax.axis_size("expert")
    local_tokens = context.shape[0]
    local_width = residual.shape[1]
    model_width = context.shape[1]
    local_blocks = local_tokens // BLK
    n_blocks = local_blocks * n_dp
    piece = BLK // n_dp
    my_expert = lax.axis_index("expert")

    w_a, w_b = all_gather_2d(out_weight, cid=10)
    w_a = w_a.reshape(model_width, -1)
    w_b = w_b.reshape(model_width, -1)
    projected = jnp.concatenate(
        [
            jnp.dot(context, w_a, preferred_element_type=jnp.float32),
            jnp.dot(context, w_b, preferred_element_type=jnp.float32),
        ],
        axis=1,
    )
    attended = (residual.astype(jnp.float32) + projected).astype(jnp.bfloat16)

    split = attended.reshape(local_blocks, n_dp, piece, local_width).transpose(1, 0, 2, 3)
    pieces, mine = spread_select(chosen_blocks.reshape(-1), split, cid=0)
    mine = mine.transpose(1, 2, 0, 3).reshape(CAP * piece, model_width)
    w_gate = gate_weight[0]
    w_up = up_weight[0]
    w_down = down_weight[0]
    gate_row = gate_values[0]
    my_count = lax.dynamic_index_in_dim(block_counts, my_expert, 0, keepdims=False)
    live = jnp.arange(CAP * BLK) // BLK < my_count
    scale = jnp.where(live, gate_row, jnp.zeros_like(gate_row))
    scale = scale.reshape(CAP, n_dp, piece).transpose(1, 0, 2).reshape(-1)

    hidden = gather_gate(mine, w_gate, w_up, cid=20)
    part = jnp.dot(hidden, w_down, preferred_element_type=jnp.float32)
    part = (part * scale[:, None]).astype(jnp.bfloat16)

    outs = reduce_scatter_2d(part.reshape(n_dp, CAP * piece, model_width), cid=1)
    outs = outs.reshape(n_expert * CAP, piece * local_width)

    selector = chosen_blocks.reshape(-1)[None, :] == jnp.arange(n_blocks)[:, None]
    added = jnp.dot(selector.astype(jnp.bfloat16), outs, preferred_element_type=jnp.float32)
    mixed = pieces.reshape(n_blocks, piece * local_width).astype(jnp.float32) + added
    mixed = mixed.astype(jnp.bfloat16).reshape(n_dp, local_blocks, piece, local_width)
    back = dp_exchange(mixed, gather=False, cid=3)
    return back.transpose(1, 0, 2, 3).reshape(local_tokens, local_width)


def solution(mesh):
    in_specs = (
        P("dp", None),
        P("dp", "expert"),
        P("dp", "expert"),
        P("expert", None, "dp"),
        P("expert", None, "dp"),
        P("expert", "dp", None),
        P("expert", None),
        P(),
        P(),
    )
    out_specs = P("dp", "expert")
    return jax.shard_map(body, mesh=mesh, in_specs=in_specs, out_specs=out_specs, check_vma=False)
```

```python
import functools

import jax
import jax.numpy as jnp
from jax import lax
from jax.sharding import PartitionSpec as P
from jax.experimental import pallas as pl
from jax.experimental.pallas import tpu as pltpu

BLK = 128
CAP = 4


def _exchange_kernel(n, gather, axis, x_ref, o_ref, local_sem, send_sems, recv_sems):
    me = lax.axis_index(axis)
    mesh_id = pl.DeviceIdType.MESH
    barrier = pltpu.get_barrier_semaphore()
    for k in range(1, n):
        pl.semaphore_signal(barrier, 1, device_id={axis: lax.rem(me + k, n)}, device_id_type=mesh_id)
    pl.semaphore_wait(barrier, n - 1)
    local = pltpu.make_async_copy(x_ref if gather else x_ref.at[me], o_ref.at[me], local_sem)
    local.start()
    copies = []
    for k in range(1, n):
        target = lax.rem(me + k, n)
        copy = pltpu.make_async_remote_copy(
            src_ref=x_ref if gather else x_ref.at[target],
            dst_ref=o_ref.at[me],
            send_sem=send_sems.at[k - 1],
            recv_sem=recv_sems.at[k - 1],
            device_id={axis: target},
            device_id_type=mesh_id,
        )
        copy.start()
        copies.append(copy)
    local.wait()
    for copy in copies:
        copy.wait()


def dp_exchange(x, gather, cid, axis="dp"):
    n = lax.axis_size(axis)
    shape = (n,) + x.shape if gather else x.shape
    return pl.pallas_call(
        functools.partial(_exchange_kernel, n, gather, axis),
        out_shape=jax.ShapeDtypeStruct(shape, x.dtype),
        in_specs=[pl.BlockSpec(memory_space=pl.ANY)],
        out_specs=pl.BlockSpec(memory_space=pl.ANY),
        scratch_shapes=[
            pltpu.SemaphoreType.DMA(()),
            pltpu.SemaphoreType.DMA((n - 1,)),
            pltpu.SemaphoreType.DMA((n - 1,)),
        ],
        compiler_params=pltpu.CompilerParams(collective_id=cid, has_side_effects=True),
    )(x)


def _route_kernel(strides, side, gather, *refs):
    n_in = len(strides)
    ins, outs = refs[:n_in], refs[n_in:2 * n_in]
    local_sems, send_sems, recv_sems = refs[2 * n_in:]
    me = lax.axis_index("dp")
    mesh_id = pl.DeviceIdType.MESH
    routes = []
    for r, stride in enumerate(strides):
        coord = lax.rem(me // stride, side)
        base = me - coord * stride
        for k in range(1, side):
            to = lax.rem(coord + k, side)
            routes.append((r, coord, to, base + to * stride))
    barrier = pltpu.get_barrier_semaphore()
    for _, _, _, target in routes:
        pl.semaphore_signal(barrier, 1, device_id={"dp": target}, device_id_type=mesh_id)
    pl.semaphore_wait(barrier, len(routes))
    locals_ = []
    for r in range(n_in):
        coord = lax.rem(me // strides[r], side)
        source = ins[r] if gather else ins[r].at[coord]
        local = pltpu.make_async_copy(source, outs[r].at[coord], local_sems.at[r])
        local.start()
        locals_.append(local)
    copies = []
    for i, (r, coord, to, target) in enumerate(routes):
        copy = pltpu.make_async_remote_copy(
            src_ref=ins[r] if gather else ins[r].at[to],
            dst_ref=outs[r].at[coord],
            send_sem=send_sems.at[i],
            recv_sem=recv_sems.at[i],
            device_id={"dp": target},
            device_id_type=mesh_id,
        )
        copy.start()
        copies.append(copy)
    for local in locals_:
        local.wait()
    for copy in copies:
        copy.wait()


def dp_route(xs, strides, cid, side=4, gather=False):
    n_routes = len(strides) * (side - 1)
    shapes = [((side,) + x.shape) if gather else x.shape for x in xs]
    return pl.pallas_call(
        functools.partial(_route_kernel, tuple(strides), side, gather),
        out_shape=[jax.ShapeDtypeStruct(s, x.dtype) for s, x in zip(shapes, xs)],
        in_specs=[pl.BlockSpec(memory_space=pl.ANY)] * len(xs),
        out_specs=[pl.BlockSpec(memory_space=pl.ANY)] * len(xs),
        scratch_shapes=[
            pltpu.SemaphoreType.DMA((len(xs),)),
            pltpu.SemaphoreType.DMA((n_routes,)),
            pltpu.SemaphoreType.DMA((n_routes,)),
        ],
        compiler_params=pltpu.CompilerParams(collective_id=cid, has_side_effects=True),
    )(*xs)


def _finish_kernel(side, n_expert, a_ref, b_ref, out_ref, got_a, got_b, outgoing,
                   local_sems, send_sems, recv_sems, ex_send, ex_recv):
    me = lax.axis_index("dp")
    mine_e = lax.axis_index("expert")
    mesh_id = pl.DeviceIdType.MESH
    routes = ((a_ref, got_a, side), (b_ref, got_b, 1))
    barrier = pltpu.get_barrier_semaphore()
    for _, _, stride in routes:
        coord = lax.rem(me // stride, side)
        base = me - coord * stride
        for k in range(1, side):
            peer = base + lax.rem(coord + k, side) * stride
            pl.semaphore_signal(barrier, 1, device_id={"dp": peer}, device_id_type=mesh_id)
    for k in range(1, n_expert):
        pl.semaphore_signal(
            barrier, 1, device_id={"expert": lax.rem(mine_e + k, n_expert)}, device_id_type=mesh_id
        )
    pl.semaphore_wait(barrier, 2 * (side - 1) + n_expert - 1)
    locals_, copies = [], []
    for r, (src, dst, stride) in enumerate(routes):
        coord = lax.rem(me // stride, side)
        base = me - coord * stride
        local = pltpu.make_async_copy(src.at[coord], dst.at[coord], local_sems.at[r])
        local.start()
        locals_.append(local)
        for k in range(1, side):
            to = lax.rem(coord + k, side)
            copy = pltpu.make_async_remote_copy(
                src_ref=src.at[to],
                dst_ref=dst.at[coord],
                send_sem=send_sems.at[r, k - 1],
                recv_sem=recv_sems.at[r, k - 1],
                device_id={"dp": base + to * stride},
                device_id_type=mesh_id,
            )
            copy.start()
            copies.append(copy)
    for local in locals_:
        local.wait()
    for copy in copies:
        copy.wait()
    width = outgoing.shape[-1]
    per_half = got_a.shape[-1] // width
    for h, got in enumerate((got_a, got_b)):
        total = got[0].astype(jnp.float32)
        for j in range(1, side):
            total = total + got[j].astype(jnp.float32)
        total = total.astype(outgoing.dtype)
        for j in range(per_half):
            outgoing[h * per_half + j] = total[:, j * width:(j + 1) * width]
    local = pltpu.make_async_copy(outgoing.at[mine_e], out_ref.at[mine_e], local_sems.at[2])
    local.start()
    copies = []
    for k in range(1, n_expert):
        target = lax.rem(mine_e + k, n_expert)
        copy = pltpu.make_async_remote_copy(
            src_ref=outgoing.at[target],
            dst_ref=out_ref.at[mine_e],
            send_sem=ex_send.at[k - 1],
            recv_sem=ex_recv.at[k - 1],
            device_id={"expert": target},
            device_id_type=mesh_id,
        )
        copy.start()
        copies.append(copy)
    local.wait()
    for copy in copies:
        copy.wait()


def _down_scatter_kernel(side, hidden_ref, wd_ref, scale_ref, sum_a, sum_b,
                         send_a, send_b, got_a, got_b, send_sems, recv_sems):
    me = lax.axis_index("dp")
    mesh_id = pl.DeviceIdType.MESH
    half = send_a.shape[-1]
    rows = send_a.shape[2]
    chunk = side * rows
    my_y = lax.rem(me, side)
    my_x = lax.rem(me // side, side)
    base_y = me - my_y
    base_x = me - my_x * side
    barrier = pltpu.get_barrier_semaphore()
    for k in range(1, side):
        pl.semaphore_signal(barrier, 1, device_id={"dp": base_y + lax.rem(my_y + k, side)}, device_id_type=mesh_id)
        pl.semaphore_signal(
            barrier, 1, device_id={"dp": base_x + lax.rem(my_x + k, side) * side}, device_id_type=mesh_id
        )
    pl.semaphore_wait(barrier, 2 * (side - 1))

    def to_a(k, y):
        return pltpu.make_async_remote_copy(
            src_ref=send_a.at[y], dst_ref=got_a.at[my_y], send_sem=send_sems.at[0, k - 1],
            recv_sem=recv_sems.at[0, k - 1], device_id={"dp": base_y + y}, device_id_type=mesh_id,
        )

    def to_b(k, x):
        return pltpu.make_async_remote_copy(
            src_ref=send_b.at[x], dst_ref=got_b.at[my_x], send_sem=send_sems.at[1, k - 1],
            recv_sem=recv_sems.at[1, k - 1], device_id={"dp": base_x + x * side}, device_id_type=mesh_id,
        )

    sends = []
    for k in list(range(1, side)) + [0]:
        x = lax.rem(my_x + k, side)
        at = pl.ds(pl.multiple_of(x * chunk, chunk), chunk)
        part = jnp.dot(hidden_ref[at], wd_ref[...], preferred_element_type=jnp.float32)
        part = (part * scale_ref[at]).astype(send_a.dtype)
        for y in range(side):
            send_a[y, x] = part[y * rows:(y + 1) * rows, :half]
            send_b[x, y] = part[y * rows:(y + 1) * rows, half:]
        if k:
            copy = to_b(k, x)
            copy.start()
            sends.append(copy)
    for k in range(1, side):
        copy = to_a(k, lax.rem(my_y + k, side))
        copy.start()
        sends.append(copy)
    for k in range(1, side):
        to_a(k, lax.rem(my_y + side - k, side)).wait_recv()
        to_b(k, lax.rem(my_x + side - k, side)).wait_recv()
    for x in range(side):
        total = send_a[my_y, x].astype(jnp.float32)
        for k in range(1, side):
            total = total + got_a[lax.rem(my_y + side - k, side), x].astype(jnp.float32)
        sum_a[x] = total.astype(sum_a.dtype)
    for y in range(side):
        total = send_b[my_x, y].astype(jnp.float32)
        for k in range(1, side):
            total = total + got_b[lax.rem(my_x + side - k, side), y].astype(jnp.float32)
        sum_b[y] = total.astype(sum_b.dtype)
    for copy in sends:
        copy.wait_send()


def down_scatter(hidden, w_down, scale, cid):
    side = 4
    rows = hidden.shape[0] // (side * side)
    half = w_down.shape[1] // 2
    slab = (side, side, rows, half)
    vmem = pl.BlockSpec(memory_space=pltpu.VMEM)
    return pl.pallas_call(
        functools.partial(_down_scatter_kernel, side),
        out_shape=[jax.ShapeDtypeStruct((side, rows, half), jnp.bfloat16)] * 2,
        in_specs=[vmem] * 3,
        out_specs=[vmem] * 2,
        scratch_shapes=[
            pltpu.VMEM(slab, jnp.bfloat16),
            pltpu.VMEM(slab, jnp.bfloat16),
            pltpu.VMEM(slab, jnp.bfloat16),
            pltpu.VMEM(slab, jnp.bfloat16),
            pltpu.SemaphoreType.DMA((2, side - 1)),
            pltpu.SemaphoreType.DMA((2, side - 1)),
        ],
        compiler_params=pltpu.CompilerParams(collective_id=cid, has_side_effects=True),
    )(hidden, w_down, scale)


def reduce_scatter_2d(part, cid):
    side = 4
    n_expert = lax.axis_size("expert")
    second_a, second_b = part
    rows = second_a.shape[1]
    cols = 2 * second_a.shape[2]
    width = cols // n_expert
    return pl.pallas_call(
        functools.partial(_finish_kernel, side, n_expert),
        out_shape=jax.ShapeDtypeStruct((n_expert, rows, width), second_a.dtype),
        in_specs=[pl.BlockSpec(memory_space=pl.ANY)] * 2,
        out_specs=pl.BlockSpec(memory_space=pl.ANY),
        scratch_shapes=[
            pltpu.VMEM(second_a.shape, second_a.dtype),
            pltpu.VMEM(second_b.shape, second_b.dtype),
            pltpu.VMEM((n_expert, rows, width), second_a.dtype),
            pltpu.SemaphoreType.DMA((3,)),
            pltpu.SemaphoreType.DMA((2, side - 1)),
            pltpu.SemaphoreType.DMA((2, side - 1)),
            pltpu.SemaphoreType.DMA((n_expert - 1,)),
            pltpu.SemaphoreType.DMA((n_expert - 1,)),
        ],
        compiler_params=pltpu.CompilerParams(collective_id=cid, has_side_effects=True),
    )(second_a, second_b)


def all_gather_2d(x, cid):
    side = 4
    half = x.shape[-1] // 2
    got_a, got_b = dp_route([x[..., :half], x[..., half:]], (1, side), cid, gather=True)
    got_a, got_b = dp_route([got_a, got_b], (side, 1), cid + 1, gather=True)
    n = side * side
    got_a = got_a.reshape((n,) + got_a.shape[2:])
    perm = (1, 0) + tuple(range(2, got_b.ndim))
    got_b = got_b.transpose(perm).reshape((n,) + got_b.shape[2:])
    return got_a, got_b


def _gather_gate_kernel(side, a_ref, b_ref, wg_ref, wu_ref, hidden_ref,
                        got_a, got_b, acc_g, acc_u, local_sems, send_sems, recv_sems):
    me = lax.axis_index("dp")
    mesh_id = pl.DeviceIdType.MESH
    half = a_ref.shape[-1]
    group = got_a.shape[1] * got_a.shape[2]
    rows = got_a.shape[2]
    routes = ((a_ref, got_a, side), (b_ref, got_b, 1))
    geo = []
    for _, _, stride in routes:
        coord = lax.rem(me // stride, side)
        geo.append((coord, me - coord * stride))
    barrier = pltpu.get_barrier_semaphore()
    for (coord, base), (_, _, stride) in zip(geo, routes):
        for k in range(1, side):
            peer = base + lax.rem(coord + k, side) * stride
            pl.semaphore_signal(barrier, 1, device_id={"dp": peer}, device_id_type=mesh_id)
    pl.semaphore_wait(barrier, 2 * (side - 1))

    def remote(r, k, source, to):
        src, dst, stride = routes[r]
        coord, base = geo[r]
        return pltpu.make_async_remote_copy(
            src_ref=src,
            dst_ref=dst.at[source],
            send_sem=send_sems.at[r, k - 1],
            recv_sem=recv_sems.at[r, k - 1],
            device_id={"dp": base + to * stride},
            device_id_type=mesh_id,
        )

    locals_, sends = [], []
    for r, (src, dst, stride) in enumerate(routes):
        coord, base = geo[r]
        local = pltpu.make_async_copy(src, dst.at[coord], local_sems.at[r])
        local.start()
        locals_.append(local)
        for k in range(1, side):
            copy = remote(r, k, coord, lax.rem(coord + k, side))
            copy.start()
            sends.append(copy)
    acc_g[...] = jnp.zeros_like(acc_g)
    acc_u[...] = jnp.zeros_like(acc_u)

    def add_a(source):
        block = got_a[source].reshape(group, half)
        at = pl.ds(pl.multiple_of(source * group, group), group)
        acc_g[at] += jnp.dot(block, wg_ref[:half], preferred_element_type=jnp.float32)
        acc_u[at] += jnp.dot(block, wu_ref[:half], preferred_element_type=jnp.float32)

    def add_b(source):
        block = got_b[source].reshape(group, half)
        g = jnp.dot(block, wg_ref[half:], preferred_element_type=jnp.float32)
        u = jnp.dot(block, wu_ref[half:], preferred_element_type=jnp.float32)
        for x in range(side):
            at = pl.ds(pl.multiple_of((x * side + source) * rows, rows), rows)
            acc_g[at] += g[x * rows:(x + 1) * rows]
            acc_u[at] += u[x * rows:(x + 1) * rows]

    for local in locals_:
        local.wait()
    add_a(geo[0][0])
    add_b(geo[1][0])
    for k in range(1, side):
        for r, add in ((0, add_a), (1, add_b)):
            coord, _ = geo[r]
            source = lax.rem(coord + side - k, side)
            remote(r, k, source, source).wait_recv()
            add(source)
    g = acc_g[...]
    hidden_ref[...] = (g / (1.0 + jnp.exp(-g)) * acc_u[...]).astype(hidden_ref.dtype)
    for copy in sends:
        copy.wait_send()


def gather_gate(x, w_gate, w_up, cid):
    side = 4
    n = side * side
    half = x.shape[-1] // 2
    first_a, first_b = dp_route([x[..., :half], x[..., half:]], (1, side), cid, gather=True)
    return pl.pallas_call(
        functools.partial(_gather_gate_kernel, side),
        out_shape=jax.ShapeDtypeStruct((n * x.shape[0], w_gate.shape[1]), jnp.bfloat16),
        in_specs=[pl.BlockSpec(memory_space=pl.ANY)] * 2 + [pl.BlockSpec(memory_space=pltpu.VMEM)] * 2,
        out_specs=pl.BlockSpec(memory_space=pltpu.VMEM),
        scratch_shapes=[
            pltpu.VMEM((side,) + first_a.shape, first_a.dtype),
            pltpu.VMEM((side,) + first_b.shape, first_b.dtype),
            pltpu.VMEM((n * x.shape[0], w_gate.shape[1]), jnp.float32),
            pltpu.VMEM((n * x.shape[0], w_gate.shape[1]), jnp.float32),
            pltpu.SemaphoreType.DMA((2,)),
            pltpu.SemaphoreType.DMA((2, side - 1)),
            pltpu.SemaphoreType.DMA((2, side - 1)),
        ],
        compiler_params=pltpu.CompilerParams(collective_id=cid + 1, has_side_effects=True),
    )(first_a, first_b, w_gate, w_up)


def _spread_kernel(n_dp, n_expert, chosen_ref, split_ref, pieces_ref, mine_ref,
                   held, outgoing, local_sems, dp_send, dp_recv, ex_send, ex_recv):
    me = lax.axis_index("dp")
    mine_e = lax.axis_index("expert")
    mesh_id = pl.DeviceIdType.MESH
    group = split_ref.shape[1]
    barrier = pltpu.get_barrier_semaphore()
    for k in range(1, n_dp):
        pl.semaphore_signal(barrier, 1, device_id={"dp": lax.rem(me + k, n_dp)}, device_id_type=mesh_id)
    for k in range(1, n_expert):
        pl.semaphore_signal(
            barrier, 1, device_id={"expert": lax.rem(mine_e + k, n_expert)}, device_id_type=mesh_id
        )
    pl.semaphore_wait(barrier, n_dp + n_expert - 2)

    def at_source(src):
        return held.at[pl.ds(pl.multiple_of(src * group, group), group)]

    local = pltpu.make_async_copy(split_ref.at[me], at_source(me), local_sems.at[0])
    local.start()
    copies = []
    for k in range(1, n_dp):
        target = lax.rem(me + k, n_dp)
        copy = pltpu.make_async_remote_copy(
            src_ref=split_ref.at[target],
            dst_ref=at_source(me),
            send_sem=dp_send.at[k - 1],
            recv_sem=dp_recv.at[k - 1],
            device_id={"dp": target},
            device_id_type=mesh_id,
        )
        copy.start()
        copies.append(copy)
    local.wait()
    for copy in copies:
        copy.wait()
    keep = pltpu.make_async_copy(held, pieces_ref, local_sems.at[1])
    keep.start()
    for e in range(n_expert):
        for s in range(CAP):
            outgoing[e, s] = held[chosen_ref[e * CAP + s]]
    local = pltpu.make_async_copy(outgoing.at[mine_e], mine_ref.at[mine_e], local_sems.at[2])
    local.start()
    copies = []
    for k in range(1, n_expert):
        target = lax.rem(mine_e + k, n_expert)
        copy = pltpu.make_async_remote_copy(
            src_ref=outgoing.at[target],
            dst_ref=mine_ref.at[mine_e],
            send_sem=ex_send.at[k - 1],
            recv_sem=ex_recv.at[k - 1],
            device_id={"expert": target},
            device_id_type=mesh_id,
        )
        copy.start()
        copies.append(copy)
    local.wait()
    for copy in copies:
        copy.wait()
    keep.wait()


def spread_select(chosen, split, cid):
    n_dp = lax.axis_size("dp")
    n_expert = lax.axis_size("expert")
    _, group, rows, width = split.shape
    n_blocks = n_dp * group
    return pl.pallas_call(
        functools.partial(_spread_kernel, n_dp, n_expert),
        out_shape=[
            jax.ShapeDtypeStruct((n_blocks, rows, width), split.dtype),
            jax.ShapeDtypeStruct((n_expert, CAP, rows, width), split.dtype),
        ],
        in_specs=[pl.BlockSpec(memory_space=pltpu.SMEM), pl.BlockSpec(memory_space=pl.ANY)],
        out_specs=[pl.BlockSpec(memory_space=pl.ANY)] * 2,
        scratch_shapes=[
            pltpu.VMEM((n_blocks, rows, width), split.dtype),
            pltpu.VMEM((n_expert, CAP, rows, width), split.dtype),
            pltpu.SemaphoreType.DMA((3,)),
            pltpu.SemaphoreType.DMA((n_dp - 1,)),
            pltpu.SemaphoreType.DMA((n_dp - 1,)),
            pltpu.SemaphoreType.DMA((n_expert - 1,)),
            pltpu.SemaphoreType.DMA((n_expert - 1,)),
        ],
        compiler_params=pltpu.CompilerParams(collective_id=cid, has_side_effects=True),
    )(chosen, split)


def body(
    context,
    out_weight,
    residual,
    gate_weight,
    up_weight,
    down_weight,
    gate_values,
    chosen_blocks,
    block_counts,
):
    n_dp = lax.axis_size("dp")
    n_expert = lax.axis_size("expert")
    local_tokens = context.shape[0]
    local_width = residual.shape[1]
    model_width = context.shape[1]
    local_blocks = local_tokens // BLK
    n_blocks = local_blocks * n_dp
    piece = BLK // n_dp
    my_expert = lax.axis_index("expert")

    w_a, w_b = all_gather_2d(out_weight, cid=10)
    w_a = w_a.reshape(model_width, -1)
    w_b = w_b.reshape(model_width, -1)
    projected = jnp.concatenate(
        [
            jnp.dot(context, w_a, preferred_element_type=jnp.float32),
            jnp.dot(context, w_b, preferred_element_type=jnp.float32),
        ],
        axis=1,
    )
    attended = (residual.astype(jnp.float32) + projected).astype(jnp.bfloat16)

    split = attended.reshape(local_blocks, n_dp, piece, local_width).transpose(1, 0, 2, 3)
    pieces, mine = spread_select(chosen_blocks.reshape(-1), split, cid=0)
    mine = mine.transpose(1, 2, 0, 3).reshape(CAP * piece, model_width)
    w_gate = gate_weight[0]
    w_up = up_weight[0]
    w_down = down_weight[0]
    gate_row = gate_values[0]
    my_count = lax.dynamic_index_in_dim(block_counts, my_expert, 0, keepdims=False)
    live = jnp.arange(CAP * BLK) // BLK < my_count
    scale = jnp.where(live, gate_row, jnp.zeros_like(gate_row))
    scale = scale.reshape(CAP, n_dp, piece).transpose(1, 0, 2).reshape(-1)

    hidden = gather_gate(mine, w_gate, w_up, cid=20)
    halves = down_scatter(hidden, w_down, scale[:, None], cid=1)

    outs = reduce_scatter_2d(halves, cid=2)
    outs = outs.reshape(n_expert * CAP, piece * local_width)

    selector = chosen_blocks.reshape(-1)[None, :] == jnp.arange(n_blocks)[:, None]
    added = jnp.dot(selector.astype(jnp.bfloat16), outs, preferred_element_type=jnp.float32)
    mixed = pieces.reshape(n_blocks, piece * local_width).astype(jnp.float32) + added
    mixed = mixed.astype(jnp.bfloat16).reshape(n_dp, local_blocks, piece, local_width)
    back = dp_exchange(mixed, gather=False, cid=3)
    return back.transpose(1, 0, 2, 3).reshape(local_tokens, local_width)


def solution(mesh):
    in_specs = (
        P("dp", None),
        P("dp", "expert"),
        P("dp", "expert"),
        P("expert", None, "dp"),
        P("expert", None, "dp"),
        P("expert", "dp", None),
        P("expert", None),
        P(),
        P(),
    )
    out_specs = P("dp", "expert")
    return jax.shard_map(body, mesh=mesh, in_specs=in_specs, out_specs=out_specs, check_vma=False)
```

```python
import functools

import jax
import jax.numpy as jnp
from jax import lax
from jax.sharding import PartitionSpec as P
from jax.experimental import pallas as pl
from jax.experimental.pallas import tpu as pltpu

BLK = 128
CAP = 4


def _exchange_kernel(n, gather, axis, x_ref, o_ref, local_sem, send_sems, recv_sems):
    me = lax.axis_index(axis)
    mesh_id = pl.DeviceIdType.MESH
    barrier = pltpu.get_barrier_semaphore()
    for k in range(1, n):
        pl.semaphore_signal(barrier, 1, device_id={axis: lax.rem(me + k, n)}, device_id_type=mesh_id)
    pl.semaphore_wait(barrier, n - 1)
    local = pltpu.make_async_copy(x_ref if gather else x_ref.at[me], o_ref.at[me], local_sem)
    local.start()
    copies = []
    for k in range(1, n):
        target = lax.rem(me + k, n)
        copy = pltpu.make_async_remote_copy(
            src_ref=x_ref if gather else x_ref.at[target],
            dst_ref=o_ref.at[me],
            send_sem=send_sems.at[k - 1],
            recv_sem=recv_sems.at[k - 1],
            device_id={axis: target},
            device_id_type=mesh_id,
        )
        copy.start()
        copies.append(copy)
    local.wait()
    for copy in copies:
        copy.wait()


def dp_exchange(x, gather, cid, axis="dp"):
    n = lax.axis_size(axis)
    shape = (n,) + x.shape if gather else x.shape
    return pl.pallas_call(
        functools.partial(_exchange_kernel, n, gather, axis),
        out_shape=jax.ShapeDtypeStruct(shape, x.dtype),
        in_specs=[pl.BlockSpec(memory_space=pl.ANY)],
        out_specs=pl.BlockSpec(memory_space=pl.ANY),
        scratch_shapes=[
            pltpu.SemaphoreType.DMA(()),
            pltpu.SemaphoreType.DMA((n - 1,)),
            pltpu.SemaphoreType.DMA((n - 1,)),
        ],
        compiler_params=pltpu.CompilerParams(collective_id=cid, has_side_effects=True),
    )(x)


def _route_kernel(strides, side, gather, *refs):
    n_in = len(strides)
    ins, outs = refs[:n_in], refs[n_in:2 * n_in]
    local_sems, send_sems, recv_sems = refs[2 * n_in:]
    me = lax.axis_index("dp")
    mesh_id = pl.DeviceIdType.MESH
    routes = []
    for r, stride in enumerate(strides):
        coord = lax.rem(me // stride, side)
        base = me - coord * stride
        for k in range(1, side):
            to = lax.rem(coord + k, side)
            routes.append((r, coord, to, base + to * stride))
    barrier = pltpu.get_barrier_semaphore()
    for _, _, _, target in routes:
        pl.semaphore_signal(barrier, 1, device_id={"dp": target}, device_id_type=mesh_id)
    pl.semaphore_wait(barrier, len(routes))
    locals_ = []
    for r in range(n_in):
        coord = lax.rem(me // strides[r], side)
        source = ins[r] if gather else ins[r].at[coord]
        local = pltpu.make_async_copy(source, outs[r].at[coord], local_sems.at[r])
        local.start()
        locals_.append(local)
    copies = []
    for i, (r, coord, to, target) in enumerate(routes):
        copy = pltpu.make_async_remote_copy(
            src_ref=ins[r] if gather else ins[r].at[to],
            dst_ref=outs[r].at[coord],
            send_sem=send_sems.at[i],
            recv_sem=recv_sems.at[i],
            device_id={"dp": target},
            device_id_type=mesh_id,
        )
        copy.start()
        copies.append(copy)
    for local in locals_:
        local.wait()
    for copy in copies:
        copy.wait()


def dp_route(xs, strides, cid, side=4, gather=False):
    n_routes = len(strides) * (side - 1)
    shapes = [((side,) + x.shape) if gather else x.shape for x in xs]
    return pl.pallas_call(
        functools.partial(_route_kernel, tuple(strides), side, gather),
        out_shape=[jax.ShapeDtypeStruct(s, x.dtype) for s, x in zip(shapes, xs)],
        in_specs=[pl.BlockSpec(memory_space=pl.ANY)] * len(xs),
        out_specs=[pl.BlockSpec(memory_space=pl.ANY)] * len(xs),
        scratch_shapes=[
            pltpu.SemaphoreType.DMA((len(xs),)),
            pltpu.SemaphoreType.DMA((n_routes,)),
            pltpu.SemaphoreType.DMA((n_routes,)),
        ],
        compiler_params=pltpu.CompilerParams(collective_id=cid, has_side_effects=True),
    )(*xs)


def _finish_kernel(side, n_expert, a_ref, b_ref, out_ref, got_a, got_b, outgoing,
                   local_sems, send_sems, recv_sems, ex_send, ex_recv):
    me = lax.axis_index("dp")
    mine_e = lax.axis_index("expert")
    mesh_id = pl.DeviceIdType.MESH
    routes = ((a_ref, got_a, side), (b_ref, got_b, 1))
    barrier = pltpu.get_barrier_semaphore()
    for _, _, stride in routes:
        coord = lax.rem(me // stride, side)
        base = me - coord * stride
        for k in range(1, side):
            peer = base + lax.rem(coord + k, side) * stride
            pl.semaphore_signal(barrier, 1, device_id={"dp": peer}, device_id_type=mesh_id)
    for k in range(1, n_expert):
        pl.semaphore_signal(
            barrier, 1, device_id={"expert": lax.rem(mine_e + k, n_expert)}, device_id_type=mesh_id
        )
    pl.semaphore_wait(barrier, 2 * (side - 1) + n_expert - 1)
    locals_, copies = [], []
    for r, (src, dst, stride) in enumerate(routes):
        coord = lax.rem(me // stride, side)
        base = me - coord * stride
        local = pltpu.make_async_copy(src.at[coord], dst.at[coord], local_sems.at[r])
        local.start()
        locals_.append(local)
        for k in range(1, side):
            to = lax.rem(coord + k, side)
            copy = pltpu.make_async_remote_copy(
                src_ref=src.at[to],
                dst_ref=dst.at[coord],
                send_sem=send_sems.at[r, k - 1],
                recv_sem=recv_sems.at[r, k - 1],
                device_id={"dp": base + to * stride},
                device_id_type=mesh_id,
            )
            copy.start()
            copies.append(copy)
    for local in locals_:
        local.wait()
    for copy in copies:
        copy.wait()
    width = outgoing.shape[-1]
    per_half = got_a.shape[-1] // width
    for h, got in enumerate((got_a, got_b)):
        total = got[0].astype(jnp.float32)
        for j in range(1, side):
            total = total + got[j].astype(jnp.float32)
        total = total.astype(outgoing.dtype)
        for j in range(per_half):
            outgoing[h * per_half + j] = total[:, j * width:(j + 1) * width]
    local = pltpu.make_async_copy(outgoing.at[mine_e], out_ref.at[mine_e], local_sems.at[2])
    local.start()
    copies = []
    for k in range(1, n_expert):
        target = lax.rem(mine_e + k, n_expert)
        copy = pltpu.make_async_remote_copy(
            src_ref=outgoing.at[target],
            dst_ref=out_ref.at[mine_e],
            send_sem=ex_send.at[k - 1],
            recv_sem=ex_recv.at[k - 1],
            device_id={"expert": target},
            device_id_type=mesh_id,
        )
        copy.start()
        copies.append(copy)
    local.wait()
    for copy in copies:
        copy.wait()


def _down_scatter_kernel(side, hidden_ref, wd_ref, scale_ref, sum_a, sum_b,
                         send_a, send_b, got_a, got_b, send_sems, recv_sems):
    me = lax.axis_index("dp")
    mesh_id = pl.DeviceIdType.MESH
    half = send_a.shape[-1]
    rows = send_a.shape[2]
    chunk = side * rows
    my_y = lax.rem(me, side)
    my_x = lax.rem(me // side, side)
    base_y = me - my_y
    base_x = me - my_x * side
    barrier = pltpu.get_barrier_semaphore()
    for k in range(1, side):
        pl.semaphore_signal(barrier, 1, device_id={"dp": base_y + lax.rem(my_y + k, side)}, device_id_type=mesh_id)
        pl.semaphore_signal(
            barrier, 1, device_id={"dp": base_x + lax.rem(my_x + k, side) * side}, device_id_type=mesh_id
        )
    pl.semaphore_wait(barrier, 2 * (side - 1))

    def to_a(k, y):
        return pltpu.make_async_remote_copy(
            src_ref=send_a.at[y], dst_ref=got_a.at[my_y], send_sem=send_sems.at[0, k - 1],
            recv_sem=recv_sems.at[0, k - 1], device_id={"dp": base_y + y}, device_id_type=mesh_id,
        )

    def to_b(k, x):
        return pltpu.make_async_remote_copy(
            src_ref=send_b.at[x], dst_ref=got_b.at[my_x], send_sem=send_sems.at[1, k - 1],
            recv_sem=recv_sems.at[1, k - 1], device_id={"dp": base_x + x * side}, device_id_type=mesh_id,
        )

    sends = []
    for k in list(range(1, side)) + [0]:
        x = lax.rem(my_x + k, side)
        at = pl.ds(pl.multiple_of(x * chunk, chunk), chunk)
        part = jnp.dot(hidden_ref[at], wd_ref[...], preferred_element_type=jnp.float32)
        part = (part * scale_ref[at]).astype(send_a.dtype)
        for y in range(side):
            send_a[y, x] = part[y * rows:(y + 1) * rows, :half]
            send_b[x, y] = part[y * rows:(y + 1) * rows, half:]
        if k:
            copy = to_b(k, x)
            copy.start()
            sends.append(copy)
    for k in range(1, side):
        copy = to_a(k, lax.rem(my_y + k, side))
        copy.start()
        sends.append(copy)
    for k in range(1, side):
        to_a(k, lax.rem(my_y + side - k, side)).wait_recv()
        to_b(k, lax.rem(my_x + side - k, side)).wait_recv()
    for x in range(side):
        total = send_a[my_y, x].astype(jnp.float32)
        for k in range(1, side):
            total = total + got_a[lax.rem(my_y + side - k, side), x].astype(jnp.float32)
        sum_a[x] = total.astype(sum_a.dtype)
    for y in range(side):
        total = send_b[my_x, y].astype(jnp.float32)
        for k in range(1, side):
            total = total + got_b[lax.rem(my_x + side - k, side), y].astype(jnp.float32)
        sum_b[y] = total.astype(sum_b.dtype)
    for copy in sends:
        copy.wait_send()


def down_scatter(hidden, w_down, scale, cid):
    side = 4
    rows = hidden.shape[0] // (side * side)
    half = w_down.shape[1] // 2
    slab = (side, side, rows, half)
    vmem = pl.BlockSpec(memory_space=pltpu.VMEM)
    return pl.pallas_call(
        functools.partial(_down_scatter_kernel, side),
        out_shape=[jax.ShapeDtypeStruct((side, rows, half), jnp.bfloat16)] * 2,
        in_specs=[vmem] * 3,
        out_specs=[vmem] * 2,
        scratch_shapes=[
            pltpu.VMEM(slab, jnp.bfloat16),
            pltpu.VMEM(slab, jnp.bfloat16),
            pltpu.VMEM(slab, jnp.bfloat16),
            pltpu.VMEM(slab, jnp.bfloat16),
            pltpu.SemaphoreType.DMA((2, side - 1)),
            pltpu.SemaphoreType.DMA((2, side - 1)),
        ],
        compiler_params=pltpu.CompilerParams(collective_id=cid, has_side_effects=True),
    )(hidden, w_down, scale)


def reduce_scatter_2d(part, cid):
    side = 4
    n_expert = lax.axis_size("expert")
    second_a, second_b = part
    rows = second_a.shape[1]
    cols = 2 * second_a.shape[2]
    width = cols // n_expert
    return pl.pallas_call(
        functools.partial(_finish_kernel, side, n_expert),
        out_shape=jax.ShapeDtypeStruct((n_expert, rows, width), second_a.dtype),
        in_specs=[pl.BlockSpec(memory_space=pl.ANY)] * 2,
        out_specs=pl.BlockSpec(memory_space=pl.ANY),
        scratch_shapes=[
            pltpu.VMEM(second_a.shape, second_a.dtype),
            pltpu.VMEM(second_b.shape, second_b.dtype),
            pltpu.VMEM((n_expert, rows, width), second_a.dtype),
            pltpu.SemaphoreType.DMA((3,)),
            pltpu.SemaphoreType.DMA((2, side - 1)),
            pltpu.SemaphoreType.DMA((2, side - 1)),
            pltpu.SemaphoreType.DMA((n_expert - 1,)),
            pltpu.SemaphoreType.DMA((n_expert - 1,)),
        ],
        compiler_params=pltpu.CompilerParams(collective_id=cid, has_side_effects=True),
    )(second_a, second_b)


def all_gather_2d(x, cid):
    side = 4
    half = x.shape[-1] // 2
    got_a, got_b = dp_route([x[..., :half], x[..., half:]], (1, side), cid, gather=True)
    got_a, got_b = dp_route([got_a, got_b], (side, 1), cid + 1, gather=True)
    n = side * side
    got_a = got_a.reshape((n,) + got_a.shape[2:])
    perm = (1, 0) + tuple(range(2, got_b.ndim))
    got_b = got_b.transpose(perm).reshape((n,) + got_b.shape[2:])
    return got_a, got_b


def _gather_gate_kernel(side, a_ref, b_ref, wg_ref, wu_ref, hidden_ref,
                        got_a, got_b, acc_g, acc_u, local_sems, send_sems, recv_sems):
    me = lax.axis_index("dp")
    mesh_id = pl.DeviceIdType.MESH
    half = a_ref.shape[-1]
    group = got_a.shape[1] * got_a.shape[2]
    rows = got_a.shape[2]
    routes = ((a_ref, got_a, side), (b_ref, got_b, 1))
    geo = []
    for _, _, stride in routes:
        coord = lax.rem(me // stride, side)
        geo.append((coord, me - coord * stride))
    barrier = pltpu.get_barrier_semaphore()
    for (coord, base), (_, _, stride) in zip(geo, routes):
        for k in range(1, side):
            peer = base + lax.rem(coord + k, side) * stride
            pl.semaphore_signal(barrier, 1, device_id={"dp": peer}, device_id_type=mesh_id)
    pl.semaphore_wait(barrier, 2 * (side - 1))

    def remote(r, k, source, to):
        src, dst, stride = routes[r]
        coord, base = geo[r]
        return pltpu.make_async_remote_copy(
            src_ref=src,
            dst_ref=dst.at[source],
            send_sem=send_sems.at[r, k - 1],
            recv_sem=recv_sems.at[r, k - 1],
            device_id={"dp": base + to * stride},
            device_id_type=mesh_id,
        )

    locals_, sends = [], []
    for r, (src, dst, stride) in enumerate(routes):
        coord, base = geo[r]
        local = pltpu.make_async_copy(src, dst.at[coord], local_sems.at[r])
        local.start()
        locals_.append(local)
        for k in range(1, side):
            copy = remote(r, k, coord, lax.rem(coord + k, side))
            copy.start()
            sends.append(copy)
    acc_g[...] = jnp.zeros_like(acc_g)
    acc_u[...] = jnp.zeros_like(acc_u)

    def add_a(source):
        block = got_a[source].reshape(group, half)
        at = pl.ds(pl.multiple_of(source * group, group), group)
        acc_g[at] += jnp.dot(block, wg_ref[:half], preferred_element_type=jnp.float32)
        acc_u[at] += jnp.dot(block, wu_ref[:half], preferred_element_type=jnp.float32)

    def add_b(source):
        block = got_b[source].reshape(group, half)
        g = jnp.dot(block, wg_ref[half:], preferred_element_type=jnp.float32)
        u = jnp.dot(block, wu_ref[half:], preferred_element_type=jnp.float32)
        for x in range(side):
            at = pl.ds(pl.multiple_of((x * side + source) * rows, rows), rows)
            acc_g[at] += g[x * rows:(x + 1) * rows]
            acc_u[at] += u[x * rows:(x + 1) * rows]

    for local in locals_:
        local.wait()
    add_a(geo[0][0])
    add_b(geo[1][0])
    for k in range(1, side):
        for r, add in ((0, add_a), (1, add_b)):
            coord, _ = geo[r]
            source = lax.rem(coord + side - k, side)
            remote(r, k, source, source).wait_recv()
            add(source)
    g = acc_g[...]
    hidden_ref[...] = (g / (1.0 + jnp.exp(-g)) * acc_u[...]).astype(hidden_ref.dtype)
    for copy in sends:
        copy.wait_send()


def gather_gate(x, w_gate, w_up, cid):
    side = 4
    n = side * side
    half = x.shape[-1] // 2
    first_a, first_b = dp_route([x[..., :half], x[..., half:]], (1, side), cid, gather=True)
    return pl.pallas_call(
        functools.partial(_gather_gate_kernel, side),
        out_shape=jax.ShapeDtypeStruct((n * x.shape[0], w_gate.shape[1]), jnp.bfloat16),
        in_specs=[pl.BlockSpec(memory_space=pl.ANY)] * 2 + [pl.BlockSpec(memory_space=pltpu.VMEM)] * 2,
        out_specs=pl.BlockSpec(memory_space=pltpu.VMEM),
        scratch_shapes=[
            pltpu.VMEM((side,) + first_a.shape, first_a.dtype),
            pltpu.VMEM((side,) + first_b.shape, first_b.dtype),
            pltpu.VMEM((n * x.shape[0], w_gate.shape[1]), jnp.float32),
            pltpu.VMEM((n * x.shape[0], w_gate.shape[1]), jnp.float32),
            pltpu.SemaphoreType.DMA((2,)),
            pltpu.SemaphoreType.DMA((2, side - 1)),
            pltpu.SemaphoreType.DMA((2, side - 1)),
        ],
        compiler_params=pltpu.CompilerParams(collective_id=cid + 1, has_side_effects=True),
    )(first_a, first_b, w_gate, w_up)


def _gather_attend_kernel(side, a_ref, b_ref, ctx_ref, res_ref, out_ref,
                          got_a, got_b, acc_a, acc_b, local_sems, send_sems, recv_sems):
    me = lax.axis_index("dp")
    mesh_id = pl.DeviceIdType.MESH
    rows = got_a.shape[2]
    bundle = side * rows
    routes = ((a_ref, got_a, side), (b_ref, got_b, 1))
    geo = []
    for _, _, stride in routes:
        coord = lax.rem(me // stride, side)
        geo.append((coord, me - coord * stride))
    barrier = pltpu.get_barrier_semaphore()
    for (coord, base), (_, _, stride) in zip(geo, routes):
        for k in range(1, side):
            peer = base + lax.rem(coord + k, side) * stride
            pl.semaphore_signal(barrier, 1, device_id={"dp": peer}, device_id_type=mesh_id)
    pl.semaphore_wait(barrier, 2 * (side - 1))

    def remote(r, k, source, to):
        src, dst, stride = routes[r]
        coord, base = geo[r]
        return pltpu.make_async_remote_copy(
            src_ref=src,
            dst_ref=dst.at[source],
            send_sem=send_sems.at[r, k - 1],
            recv_sem=recv_sems.at[r, k - 1],
            device_id={"dp": base + to * stride},
            device_id_type=mesh_id,
        )

    locals_, sends = [], []
    for r, (src, dst, stride) in enumerate(routes):
        coord, base = geo[r]
        local = pltpu.make_async_copy(src, dst.at[coord], local_sems.at[r])
        local.start()
        locals_.append(local)
        for k in range(1, side):
            copy = remote(r, k, coord, lax.rem(coord + k, side))
            copy.start()
            sends.append(copy)
    acc_a[...] = jnp.zeros_like(acc_a)
    acc_b[...] = jnp.zeros_like(acc_b)

    def add_a(source):
        block = got_a[source].reshape(bundle, got_a.shape[-1])
        at = pl.ds(pl.multiple_of(source * bundle, bundle), bundle)
        acc_a[...] += jnp.dot(ctx_ref[:, at], block, preferred_element_type=jnp.float32)

    def add_b(source):
        for x in range(side):
            at = pl.ds(pl.multiple_of((x * side + source) * rows, rows), rows)
            acc_b[...] += jnp.dot(ctx_ref[:, at], got_b[source, x], preferred_element_type=jnp.float32)

    for local in locals_:
        local.wait()
    add_a(geo[0][0])
    add_b(geo[1][0])
    for k in range(1, side):
        for r, add in ((0, add_a), (1, add_b)):
            coord, _ = geo[r]
            source = lax.rem(coord + side - k, side)
            remote(r, k, source, source).wait_recv()
            add(source)
    half = acc_a.shape[1]
    out_ref[:, :half] = (res_ref[:, :half].astype(jnp.float32) + acc_a[...]).astype(out_ref.dtype)
    out_ref[:, half:] = (res_ref[:, half:].astype(jnp.float32) + acc_b[...]).astype(out_ref.dtype)
    for copy in sends:
        copy.wait_send()


def gather_attend(w, context, residual, cid):
    side = 4
    half = w.shape[-1] // 2
    first_a, first_b = dp_route([w[..., :half], w[..., half:]], (1, side), cid, gather=True)
    vmem = pl.BlockSpec(memory_space=pltpu.VMEM)
    return pl.pallas_call(
        functools.partial(_gather_attend_kernel, side),
        out_shape=jax.ShapeDtypeStruct(residual.shape, jnp.bfloat16),
        in_specs=[pl.BlockSpec(memory_space=pl.ANY)] * 2 + [vmem] * 2,
        out_specs=vmem,
        scratch_shapes=[
            pltpu.VMEM((side,) + first_a.shape, first_a.dtype),
            pltpu.VMEM((side,) + first_b.shape, first_b.dtype),
            pltpu.VMEM((context.shape[0], half), jnp.float32),
            pltpu.VMEM((context.shape[0], half), jnp.float32),
            pltpu.SemaphoreType.DMA((2,)),
            pltpu.SemaphoreType.DMA((2, side - 1)),
            pltpu.SemaphoreType.DMA((2, side - 1)),
        ],
        compiler_params=pltpu.CompilerParams(collective_id=cid + 1, has_side_effects=True),
    )(first_a, first_b, context, residual)


def _spread_kernel(n_dp, n_expert, chosen_ref, split_ref, pieces_ref, mine_ref,
                   held, outgoing, local_sems, dp_send, dp_recv, ex_send, ex_recv):
    me = lax.axis_index("dp")
    mine_e = lax.axis_index("expert")
    mesh_id = pl.DeviceIdType.MESH
    group = split_ref.shape[1]
    barrier = pltpu.get_barrier_semaphore()
    for k in range(1, n_dp):
        pl.semaphore_signal(barrier, 1, device_id={"dp": lax.rem(me + k, n_dp)}, device_id_type=mesh_id)
    for k in range(1, n_expert):
        pl.semaphore_signal(
            barrier, 1, device_id={"expert": lax.rem(mine_e + k, n_expert)}, device_id_type=mesh_id
        )
    pl.semaphore_wait(barrier, n_dp + n_expert - 2)

    def at_source(src):
        return held.at[pl.ds(pl.multiple_of(src * group, group), group)]

    local = pltpu.make_async_copy(split_ref.at[me], at_source(me), local_sems.at[0])
    local.start()
    copies = []
    for k in range(1, n_dp):
        target = lax.rem(me + k, n_dp)
        copy = pltpu.make_async_remote_copy(
            src_ref=split_ref.at[target],
            dst_ref=at_source(me),
            send_sem=dp_send.at[k - 1],
            recv_sem=dp_recv.at[k - 1],
            device_id={"dp": target},
            device_id_type=mesh_id,
        )
        copy.start()
        copies.append(copy)
    local.wait()
    for copy in copies:
        copy.wait()
    keep = pltpu.make_async_copy(held, pieces_ref, local_sems.at[1])
    keep.start()
    for e in range(n_expert):
        for s in range(CAP):
            outgoing[e, s] = held[chosen_ref[e * CAP + s]]
    local = pltpu.make_async_copy(outgoing.at[mine_e], mine_ref.at[mine_e], local_sems.at[2])
    local.start()
    copies = []
    for k in range(1, n_expert):
        target = lax.rem(mine_e + k, n_expert)
        copy = pltpu.make_async_remote_copy(
            src_ref=outgoing.at[target],
            dst_ref=mine_ref.at[mine_e],
            send_sem=ex_send.at[k - 1],
            recv_sem=ex_recv.at[k - 1],
            device_id={"expert": target},
            device_id_type=mesh_id,
        )
        copy.start()
        copies.append(copy)
    local.wait()
    for copy in copies:
        copy.wait()
    keep.wait()


def spread_select(chosen, split, cid):
    n_dp = lax.axis_size("dp")
    n_expert = lax.axis_size("expert")
    _, group, rows, width = split.shape
    n_blocks = n_dp * group
    return pl.pallas_call(
        functools.partial(_spread_kernel, n_dp, n_expert),
        out_shape=[
            jax.ShapeDtypeStruct((n_blocks, rows, width), split.dtype),
            jax.ShapeDtypeStruct((n_expert, CAP, rows, width), split.dtype),
        ],
        in_specs=[pl.BlockSpec(memory_space=pltpu.SMEM), pl.BlockSpec(memory_space=pl.ANY)],
        out_specs=[pl.BlockSpec(memory_space=pl.ANY)] * 2,
        scratch_shapes=[
            pltpu.VMEM((n_blocks, rows, width), split.dtype),
            pltpu.VMEM((n_expert, CAP, rows, width), split.dtype),
            pltpu.SemaphoreType.DMA((3,)),
            pltpu.SemaphoreType.DMA((n_dp - 1,)),
            pltpu.SemaphoreType.DMA((n_dp - 1,)),
            pltpu.SemaphoreType.DMA((n_expert - 1,)),
            pltpu.SemaphoreType.DMA((n_expert - 1,)),
        ],
        compiler_params=pltpu.CompilerParams(collective_id=cid, has_side_effects=True),
    )(chosen, split)


def body(
    context,
    out_weight,
    residual,
    gate_weight,
    up_weight,
    down_weight,
    gate_values,
    chosen_blocks,
    block_counts,
):
    n_dp = lax.axis_size("dp")
    n_expert = lax.axis_size("expert")
    local_tokens = context.shape[0]
    local_width = residual.shape[1]
    model_width = context.shape[1]
    local_blocks = local_tokens // BLK
    n_blocks = local_blocks * n_dp
    piece = BLK // n_dp
    my_expert = lax.axis_index("expert")

    attended = gather_attend(out_weight, context, residual, cid=10)

    split = attended.reshape(local_blocks, n_dp, piece, local_width).transpose(1, 0, 2, 3)
    pieces, mine = spread_select(chosen_blocks.reshape(-1), split, cid=0)
    mine = mine.transpose(1, 2, 0, 3).reshape(CAP * piece, model_width)
    w_gate = gate_weight[0]
    w_up = up_weight[0]
    w_down = down_weight[0]
    gate_row = gate_values[0]
    my_count = lax.dynamic_index_in_dim(block_counts, my_expert, 0, keepdims=False)
    live = jnp.arange(CAP * BLK) // BLK < my_count
    scale = jnp.where(live, gate_row, jnp.zeros_like(gate_row))
    scale = scale.reshape(CAP, n_dp, piece).transpose(1, 0, 2).reshape(-1)

    hidden = gather_gate(mine, w_gate, w_up, cid=20)
    halves = down_scatter(hidden, w_down, scale[:, None], cid=1)

    outs = reduce_scatter_2d(halves, cid=2)
    outs = outs.reshape(n_expert * CAP, piece * local_width)

    selector = chosen_blocks.reshape(-1)[None, :] == jnp.arange(n_blocks)[:, None]
    added = jnp.dot(selector.astype(jnp.bfloat16), outs, preferred_element_type=jnp.float32)
    mixed = pieces.reshape(n_blocks, piece * local_width).astype(jnp.float32) + added
    mixed = mixed.astype(jnp.bfloat16).reshape(n_dp, local_blocks, piece, local_width)
    back = dp_exchange(mixed, gather=False, cid=3)
    return back.transpose(1, 0, 2, 3).reshape(local_tokens, local_width)


def solution(mesh):
    in_specs = (
        P("dp", None),
        P("dp", "expert"),
        P("dp", "expert"),
        P("expert", None, "dp"),
        P("expert", None, "dp"),
        P("expert", "dp", None),
        P("expert", None),
        P(),
        P(),
    )
    out_specs = P("dp", "expert")
    return jax.shard_map(body, mesh=mesh, in_specs=in_specs, out_specs=out_specs, check_vma=False)
```

```python
import functools

import jax
import jax.numpy as jnp
from jax import lax
from jax.sharding import PartitionSpec as P
from jax.experimental import pallas as pl
from jax.experimental.pallas import tpu as pltpu

BLK = 128
CAP = 4


def _exchange_kernel(n, gather, axis, x_ref, o_ref, local_sem, send_sems, recv_sems):
    me = lax.axis_index(axis)
    mesh_id = pl.DeviceIdType.MESH
    barrier = pltpu.get_barrier_semaphore()
    for k in range(1, n):
        pl.semaphore_signal(barrier, 1, device_id={axis: lax.rem(me + k, n)}, device_id_type=mesh_id)
    pl.semaphore_wait(barrier, n - 1)
    local = pltpu.make_async_copy(x_ref if gather else x_ref.at[me], o_ref.at[me], local_sem)
    local.start()
    copies = []
    for k in range(1, n):
        target = lax.rem(me + k, n)
        copy = pltpu.make_async_remote_copy(
            src_ref=x_ref if gather else x_ref.at[target],
            dst_ref=o_ref.at[me],
            send_sem=send_sems.at[k - 1],
            recv_sem=recv_sems.at[k - 1],
            device_id={axis: target},
            device_id_type=mesh_id,
        )
        copy.start()
        copies.append(copy)
    local.wait()
    for copy in copies:
        copy.wait()


def dp_exchange(x, gather, cid, axis="dp"):
    n = lax.axis_size(axis)
    shape = (n,) + x.shape if gather else x.shape
    return pl.pallas_call(
        functools.partial(_exchange_kernel, n, gather, axis),
        out_shape=jax.ShapeDtypeStruct(shape, x.dtype),
        in_specs=[pl.BlockSpec(memory_space=pl.ANY)],
        out_specs=pl.BlockSpec(memory_space=pl.ANY),
        scratch_shapes=[
            pltpu.SemaphoreType.DMA(()),
            pltpu.SemaphoreType.DMA((n - 1,)),
            pltpu.SemaphoreType.DMA((n - 1,)),
        ],
        compiler_params=pltpu.CompilerParams(collective_id=cid, has_side_effects=True),
    )(x)


def _route_kernel(strides, side, gather, windows, *refs):
    n_in = len(strides)
    ins, outs = refs[:n_in], refs[n_in:2 * n_in]
    local_sems, send_sems, recv_sems = refs[2 * n_in:]
    me = lax.axis_index("dp")
    mesh_id = pl.DeviceIdType.MESH

    def window(r):
        if windows is None:
            return ins[r]
        start, size = windows[r]
        return ins[r].at[:, pl.ds(start, size)]

    routes = []
    for r, stride in enumerate(strides):
        coord = lax.rem(me // stride, side)
        base = me - coord * stride
        for k in range(1, side):
            to = lax.rem(coord + k, side)
            routes.append((r, coord, to, base + to * stride))
    barrier = pltpu.get_barrier_semaphore()
    for _, _, _, target in routes:
        pl.semaphore_signal(barrier, 1, device_id={"dp": target}, device_id_type=mesh_id)
    pl.semaphore_wait(barrier, len(routes))
    locals_ = []
    for r in range(n_in):
        coord = lax.rem(me // strides[r], side)
        source = window(r) if gather else ins[r].at[coord]
        local = pltpu.make_async_copy(source, outs[r].at[coord], local_sems.at[r])
        local.start()
        locals_.append(local)
    copies = []
    for i, (r, coord, to, target) in enumerate(routes):
        copy = pltpu.make_async_remote_copy(
            src_ref=window(r) if gather else ins[r].at[to],
            dst_ref=outs[r].at[coord],
            send_sem=send_sems.at[i],
            recv_sem=recv_sems.at[i],
            device_id={"dp": target},
            device_id_type=mesh_id,
        )
        copy.start()
        copies.append(copy)
    for local in locals_:
        local.wait()
    for copy in copies:
        copy.wait()


def dp_route(xs, strides, cid, side=4, gather=False, windows=None):
    n_routes = len(strides) * (side - 1)
    if windows is not None:
        shapes = [(side, x.shape[0], size) for x, (_, size) in zip(xs, windows)]
    else:
        shapes = [((side,) + x.shape) if gather else x.shape for x in xs]
    return pl.pallas_call(
        functools.partial(_route_kernel, tuple(strides), side, gather, windows),
        out_shape=[jax.ShapeDtypeStruct(s, x.dtype) for s, x in zip(shapes, xs)],
        in_specs=[pl.BlockSpec(memory_space=pl.ANY)] * len(xs),
        out_specs=[pl.BlockSpec(memory_space=pl.ANY)] * len(xs),
        scratch_shapes=[
            pltpu.SemaphoreType.DMA((len(xs),)),
            pltpu.SemaphoreType.DMA((n_routes,)),
            pltpu.SemaphoreType.DMA((n_routes,)),
        ],
        compiler_params=pltpu.CompilerParams(collective_id=cid, has_side_effects=True),
    )(*xs)


def _finish_kernel(side, n_expert, a_ref, b_ref, out_ref, got_a, got_b, outgoing,
                   local_sems, send_sems, recv_sems, ex_send, ex_recv):
    me = lax.axis_index("dp")
    mine_e = lax.axis_index("expert")
    mesh_id = pl.DeviceIdType.MESH
    routes = ((a_ref, got_a, side), (b_ref, got_b, 1))
    barrier = pltpu.get_barrier_semaphore()
    for _, _, stride in routes:
        coord = lax.rem(me // stride, side)
        base = me - coord * stride
        for k in range(1, side):
            peer = base + lax.rem(coord + k, side) * stride
            pl.semaphore_signal(barrier, 1, device_id={"dp": peer}, device_id_type=mesh_id)
    for k in range(1, n_expert):
        pl.semaphore_signal(
            barrier, 1, device_id={"expert": lax.rem(mine_e + k, n_expert)}, device_id_type=mesh_id
        )
    pl.semaphore_wait(barrier, 2 * (side - 1) + n_expert - 1)
    locals_, copies = [], []
    for r, (src, dst, stride) in enumerate(routes):
        coord = lax.rem(me // stride, side)
        base = me - coord * stride
        local = pltpu.make_async_copy(src.at[coord], dst.at[coord], local_sems.at[r])
        local.start()
        locals_.append(local)
        for k in range(1, side):
            to = lax.rem(coord + k, side)
            copy = pltpu.make_async_remote_copy(
                src_ref=src.at[to],
                dst_ref=dst.at[coord],
                send_sem=send_sems.at[r, k - 1],
                recv_sem=recv_sems.at[r, k - 1],
                device_id={"dp": base + to * stride},
                device_id_type=mesh_id,
            )
            copy.start()
            copies.append(copy)
    for local in locals_:
        local.wait()
    for copy in copies:
        copy.wait()
    width = outgoing.shape[-1]
    per_half = got_a.shape[-1] // width
    for h, got in enumerate((got_a, got_b)):
        total = got[0].astype(jnp.float32)
        for j in range(1, side):
            total = total + got[j].astype(jnp.float32)
        total = total.astype(outgoing.dtype)
        for j in range(per_half):
            outgoing[h * per_half + j] = total[:, j * width:(j + 1) * width]
    local = pltpu.make_async_copy(outgoing.at[mine_e], out_ref.at[mine_e], local_sems.at[2])
    local.start()
    copies = []
    for k in range(1, n_expert):
        target = lax.rem(mine_e + k, n_expert)
        copy = pltpu.make_async_remote_copy(
            src_ref=outgoing.at[target],
            dst_ref=out_ref.at[mine_e],
            send_sem=ex_send.at[k - 1],
            recv_sem=ex_recv.at[k - 1],
            device_id={"expert": target},
            device_id_type=mesh_id,
        )
        copy.start()
        copies.append(copy)
    local.wait()
    for copy in copies:
        copy.wait()


def _down_scatter_kernel(side, hidden_ref, wd_ref, scale_ref, sum_a, sum_b,
                         send_a, send_b, got_a, got_b, send_sems, recv_sems):
    me = lax.axis_index("dp")
    mesh_id = pl.DeviceIdType.MESH
    half = send_a.shape[-1]
    rows = send_a.shape[2]
    chunk = side * rows
    my_y = lax.rem(me, side)
    my_x = lax.rem(me // side, side)
    base_y = me - my_y
    base_x = me - my_x * side
    barrier = pltpu.get_barrier_semaphore()
    for k in range(1, side):
        pl.semaphore_signal(barrier, 1, device_id={"dp": base_y + lax.rem(my_y + k, side)}, device_id_type=mesh_id)
        pl.semaphore_signal(
            barrier, 1, device_id={"dp": base_x + lax.rem(my_x + k, side) * side}, device_id_type=mesh_id
        )
    pl.semaphore_wait(barrier, 2 * (side - 1))

    def to_a(k, y):
        return pltpu.make_async_remote_copy(
            src_ref=send_a.at[y], dst_ref=got_a.at[my_y], send_sem=send_sems.at[0, k - 1],
            recv_sem=recv_sems.at[0, k - 1], device_id={"dp": base_y + y}, device_id_type=mesh_id,
        )

    def to_b(k, x):
        return pltpu.make_async_remote_copy(
            src_ref=send_b.at[x], dst_ref=got_b.at[my_x], send_sem=send_sems.at[1, k - 1],
            recv_sem=recv_sems.at[1, k - 1], device_id={"dp": base_x + x * side}, device_id_type=mesh_id,
        )

    sends = []
    for k in list(range(1, side)) + [0]:
        x = lax.rem(my_x + k, side)
        at = pl.ds(pl.multiple_of(x * chunk, chunk), chunk)
        part = jnp.dot(hidden_ref[at], wd_ref[...], preferred_element_type=jnp.float32)
        part = (part * scale_ref[at]).astype(send_a.dtype)
        for y in range(side):
            send_a[y, x] = part[y * rows:(y + 1) * rows, :half]
            send_b[x, y] = part[y * rows:(y + 1) * rows, half:]
        if k:
            copy = to_b(k, x)
            copy.start()
            sends.append(copy)
    for k in range(1, side):
        copy = to_a(k, lax.rem(my_y + k, side))
        copy.start()
        sends.append(copy)
    for k in range(1, side):
        to_a(k, lax.rem(my_y + side - k, side)).wait_recv()
        to_b(k, lax.rem(my_x + side - k, side)).wait_recv()
    for x in range(side):
        total = send_a[my_y, x].astype(jnp.float32)
        for k in range(1, side):
            total = total + got_a[lax.rem(my_y + side - k, side), x].astype(jnp.float32)
        sum_a[x] = total.astype(sum_a.dtype)
    for y in range(side):
        total = send_b[my_x, y].astype(jnp.float32)
        for k in range(1, side):
            total = total + got_b[lax.rem(my_x + side - k, side), y].astype(jnp.float32)
        sum_b[y] = total.astype(sum_b.dtype)
    for copy in sends:
        copy.wait_send()


def down_scatter(hidden, w_down, scale, cid):
    side = 4
    rows = hidden.shape[0] // (side * side)
    half = w_down.shape[1] // 2
    slab = (side, side, rows, half)
    vmem = pl.BlockSpec(memory_space=pltpu.VMEM)
    return pl.pallas_call(
        functools.partial(_down_scatter_kernel, side),
        out_shape=[jax.ShapeDtypeStruct((side, rows, half), jnp.bfloat16)] * 2,
        in_specs=[vmem] * 3,
        out_specs=[vmem] * 2,
        scratch_shapes=[
            pltpu.VMEM(slab, jnp.bfloat16),
            pltpu.VMEM(slab, jnp.bfloat16),
            pltpu.VMEM(slab, jnp.bfloat16),
            pltpu.VMEM(slab, jnp.bfloat16),
            pltpu.SemaphoreType.DMA((2, side - 1)),
            pltpu.SemaphoreType.DMA((2, side - 1)),
        ],
        compiler_params=pltpu.CompilerParams(collective_id=cid, has_side_effects=True),
    )(hidden, w_down, scale)


def reduce_scatter_2d(part, cid):
    side = 4
    n_expert = lax.axis_size("expert")
    second_a, second_b = part
    rows = second_a.shape[1]
    cols = 2 * second_a.shape[2]
    width = cols // n_expert
    return pl.pallas_call(
        functools.partial(_finish_kernel, side, n_expert),
        out_shape=jax.ShapeDtypeStruct((n_expert, rows, width), second_a.dtype),
        in_specs=[pl.BlockSpec(memory_space=pl.ANY)] * 2,
        out_specs=pl.BlockSpec(memory_space=pl.ANY),
        scratch_shapes=[
            pltpu.VMEM(second_a.shape, second_a.dtype),
            pltpu.VMEM(second_b.shape, second_b.dtype),
            pltpu.VMEM((n_expert, rows, width), second_a.dtype),
            pltpu.SemaphoreType.DMA((3,)),
            pltpu.SemaphoreType.DMA((2, side - 1)),
            pltpu.SemaphoreType.DMA((2, side - 1)),
            pltpu.SemaphoreType.DMA((n_expert - 1,)),
            pltpu.SemaphoreType.DMA((n_expert - 1,)),
        ],
        compiler_params=pltpu.CompilerParams(collective_id=cid, has_side_effects=True),
    )(second_a, second_b)


def all_gather_2d(x, cid):
    side = 4
    half = x.shape[-1] // 2
    got_a, got_b = dp_route([x, x], (1, side), cid, gather=True, windows=((0, half), (half, half)))
    got_a, got_b = dp_route([got_a, got_b], (side, 1), cid + 1, gather=True)
    n = side * side
    got_a = got_a.reshape((n,) + got_a.shape[2:])
    perm = (1, 0) + tuple(range(2, got_b.ndim))
    got_b = got_b.transpose(perm).reshape((n,) + got_b.shape[2:])
    return got_a, got_b


def _gather_gate_kernel(side, a_ref, b_ref, wg_ref, wu_ref, hidden_ref,
                        got_a, got_b, acc_g, acc_u, local_sems, send_sems, recv_sems):
    me = lax.axis_index("dp")
    mesh_id = pl.DeviceIdType.MESH
    half = a_ref.shape[-1]
    group = got_a.shape[1] * got_a.shape[2]
    rows = got_a.shape[2]
    routes = ((a_ref, got_a, side), (b_ref, got_b, 1))
    geo = []
    for _, _, stride in routes:
        coord = lax.rem(me // stride, side)
        geo.append((coord, me - coord * stride))
    barrier = pltpu.get_barrier_semaphore()
    for (coord, base), (_, _, stride) in zip(geo, routes):
        for k in range(1, side):
            peer = base + lax.rem(coord + k, side) * stride
            pl.semaphore_signal(barrier, 1, device_id={"dp": peer}, device_id_type=mesh_id)
    pl.semaphore_wait(barrier, 2 * (side - 1))

    def remote(r, k, source, to):
        src, dst, stride = routes[r]
        coord, base = geo[r]
        return pltpu.make_async_remote_copy(
            src_ref=src,
            dst_ref=dst.at[source],
            send_sem=send_sems.at[r, k - 1],
            recv_sem=recv_sems.at[r, k - 1],
            device_id={"dp": base + to * stride},
            device_id_type=mesh_id,
        )

    locals_, sends = [], []
    for r, (src, dst, stride) in enumerate(routes):
        coord, base = geo[r]
        local = pltpu.make_async_copy(src, dst.at[coord], local_sems.at[r])
        local.start()
        locals_.append(local)
        for k in range(1, side):
            copy = remote(r, k, coord, lax.rem(coord + k, side))
            copy.start()
            sends.append(copy)
    acc_g[...] = jnp.zeros_like(acc_g)
    acc_u[...] = jnp.zeros_like(acc_u)

    def add_a(source):
        block = got_a[source].reshape(group, half)
        at = pl.ds(pl.multiple_of(source * group, group), group)
        acc_g[at] += jnp.dot(block, wg_ref[:half], preferred_element_type=jnp.float32)
        acc_u[at] += jnp.dot(block, wu_ref[:half], preferred_element_type=jnp.float32)

    def add_b(source):
        block = got_b[source].reshape(group, half)
        g = jnp.dot(block, wg_ref[half:], preferred_element_type=jnp.float32)
        u = jnp.dot(block, wu_ref[half:], preferred_element_type=jnp.float32)
        for x in range(side):
            at = pl.ds(pl.multiple_of((x * side + source) * rows, rows), rows)
            acc_g[at] += g[x * rows:(x + 1) * rows]
            acc_u[at] += u[x * rows:(x + 1) * rows]

    for local in locals_:
        local.wait()
    add_a(geo[0][0])
    add_b(geo[1][0])
    for k in range(1, side):
        for r, add in ((0, add_a), (1, add_b)):
            coord, _ = geo[r]
            source = lax.rem(coord + side - k, side)
            remote(r, k, source, source).wait_recv()
            add(source)
    g = acc_g[...]
    hidden_ref[...] = (g / (1.0 + jnp.exp(-g)) * acc_u[...]).astype(hidden_ref.dtype)
    for copy in sends:
        copy.wait_send()


def gather_gate(x, w_gate, w_up, cid):
    side = 4
    n = side * side
    half = x.shape[-1] // 2
    first_a, first_b = dp_route([x, x], (1, side), cid, gather=True, windows=((0, half), (half, half)))
    return pl.pallas_call(
        functools.partial(_gather_gate_kernel, side),
        out_shape=jax.ShapeDtypeStruct((n * x.shape[0], w_gate.shape[1]), jnp.bfloat16),
        in_specs=[pl.BlockSpec(memory_space=pl.ANY)] * 2 + [pl.BlockSpec(memory_space=pltpu.VMEM)] * 2,
        out_specs=pl.BlockSpec(memory_space=pltpu.VMEM),
        scratch_shapes=[
            pltpu.VMEM((side,) + first_a.shape, first_a.dtype),
            pltpu.VMEM((side,) + first_b.shape, first_b.dtype),
            pltpu.VMEM((n * x.shape[0], w_gate.shape[1]), jnp.float32),
            pltpu.VMEM((n * x.shape[0], w_gate.shape[1]), jnp.float32),
            pltpu.SemaphoreType.DMA((2,)),
            pltpu.SemaphoreType.DMA((2, side - 1)),
            pltpu.SemaphoreType.DMA((2, side - 1)),
        ],
        compiler_params=pltpu.CompilerParams(collective_id=cid + 1, has_side_effects=True),
    )(first_a, first_b, w_gate, w_up)


def _gather_attend_kernel(side, a_ref, b_ref, ctx_ref, res_ref, out_ref,
                          got_a, got_b, acc_a, acc_b, local_sems, send_sems, recv_sems):
    me = lax.axis_index("dp")
    mesh_id = pl.DeviceIdType.MESH
    rows = got_a.shape[2]
    bundle = side * rows
    routes = ((a_ref, got_a, side), (b_ref, got_b, 1))
    geo = []
    for _, _, stride in routes:
        coord = lax.rem(me // stride, side)
        geo.append((coord, me - coord * stride))
    barrier = pltpu.get_barrier_semaphore()
    for (coord, base), (_, _, stride) in zip(geo, routes):
        for k in range(1, side):
            peer = base + lax.rem(coord + k, side) * stride
            pl.semaphore_signal(barrier, 1, device_id={"dp": peer}, device_id_type=mesh_id)
    pl.semaphore_wait(barrier, 2 * (side - 1))

    def remote(r, k, source, to):
        src, dst, stride = routes[r]
        coord, base = geo[r]
        return pltpu.make_async_remote_copy(
            src_ref=src,
            dst_ref=dst.at[source],
            send_sem=send_sems.at[r, k - 1],
            recv_sem=recv_sems.at[r, k - 1],
            device_id={"dp": base + to * stride},
            device_id_type=mesh_id,
        )

    locals_, sends = [], []
    for r, (src, dst, stride) in enumerate(routes):
        coord, base = geo[r]
        local = pltpu.make_async_copy(src, dst.at[coord], local_sems.at[r])
        local.start()
        locals_.append(local)
        for k in range(1, side):
            copy = remote(r, k, coord, lax.rem(coord + k, side))
            copy.start()
            sends.append(copy)
    acc_a[...] = jnp.zeros_like(acc_a)
    acc_b[...] = jnp.zeros_like(acc_b)

    def add_a(source):
        block = got_a[source].reshape(bundle, got_a.shape[-1])
        at = pl.ds(pl.multiple_of(source * bundle, bundle), bundle)
        acc_a[...] += jnp.dot(ctx_ref[:, at], block, preferred_element_type=jnp.float32)

    def add_b(source):
        for x in range(side):
            at = pl.ds(pl.multiple_of((x * side + source) * rows, rows), rows)
            acc_b[...] += jnp.dot(ctx_ref[:, at], got_b[source, x], preferred_element_type=jnp.float32)

    for local in locals_:
        local.wait()
    add_a(geo[0][0])
    add_b(geo[1][0])
    for k in range(1, side):
        for r, add in ((0, add_a), (1, add_b)):
            coord, _ = geo[r]
            source = lax.rem(coord + side - k, side)
            remote(r, k, source, source).wait_recv()
            add(source)
    half = acc_a.shape[1]
    out_ref[:, :half] = (res_ref[:, :half].astype(jnp.float32) + acc_a[...]).astype(out_ref.dtype)
    out_ref[:, half:] = (res_ref[:, half:].astype(jnp.float32) + acc_b[...]).astype(out_ref.dtype)
    for copy in sends:
        copy.wait_send()


def gather_attend(w, context, residual, cid):
    side = 4
    half = w.shape[-1] // 2
    first_a, first_b = dp_route([w, w], (1, side), cid, gather=True, windows=((0, half), (half, half)))
    vmem = pl.BlockSpec(memory_space=pltpu.VMEM)
    return pl.pallas_call(
        functools.partial(_gather_attend_kernel, side),
        out_shape=jax.ShapeDtypeStruct(residual.shape, jnp.bfloat16),
        in_specs=[pl.BlockSpec(memory_space=pl.ANY)] * 2 + [vmem] * 2,
        out_specs=vmem,
        scratch_shapes=[
            pltpu.VMEM((side,) + first_a.shape, first_a.dtype),
            pltpu.VMEM((side,) + first_b.shape, first_b.dtype),
            pltpu.VMEM((context.shape[0], half), jnp.float32),
            pltpu.VMEM((context.shape[0], half), jnp.float32),
            pltpu.SemaphoreType.DMA((2,)),
            pltpu.SemaphoreType.DMA((2, side - 1)),
            pltpu.SemaphoreType.DMA((2, side - 1)),
        ],
        compiler_params=pltpu.CompilerParams(collective_id=cid + 1, has_side_effects=True),
    )(first_a, first_b, context, residual)


def _spread_kernel(n_dp, n_expert, chosen_ref, split_ref, pieces_ref, mine_ref,
                   held, outgoing, local_sems, dp_send, dp_recv, ex_send, ex_recv):
    me = lax.axis_index("dp")
    mine_e = lax.axis_index("expert")
    mesh_id = pl.DeviceIdType.MESH
    group = split_ref.shape[1]
    barrier = pltpu.get_barrier_semaphore()
    for k in range(1, n_dp):
        pl.semaphore_signal(barrier, 1, device_id={"dp": lax.rem(me + k, n_dp)}, device_id_type=mesh_id)
    for k in range(1, n_expert):
        pl.semaphore_signal(
            barrier, 1, device_id={"expert": lax.rem(mine_e + k, n_expert)}, device_id_type=mesh_id
        )
    pl.semaphore_wait(barrier, n_dp + n_expert - 2)

    def at_source(src):
        return held.at[pl.ds(pl.multiple_of(src * group, group), group)]

    local = pltpu.make_async_copy(split_ref.at[me], at_source(me), local_sems.at[0])
    local.start()
    copies = []
    for k in range(1, n_dp):
        target = lax.rem(me + k, n_dp)
        copy = pltpu.make_async_remote_copy(
            src_ref=split_ref.at[target],
            dst_ref=at_source(me),
            send_sem=dp_send.at[k - 1],
            recv_sem=dp_recv.at[k - 1],
            device_id={"dp": target},
            device_id_type=mesh_id,
        )
        copy.start()
        copies.append(copy)
    local.wait()
    for copy in copies:
        copy.wait()
    keep = pltpu.make_async_copy(held, pieces_ref, local_sems.at[1])
    keep.start()
    for e in range(n_expert):
        for s in range(CAP):
            outgoing[e, s] = held[chosen_ref[e * CAP + s]]
    local = pltpu.make_async_copy(outgoing.at[mine_e], mine_ref.at[mine_e], local_sems.at[2])
    local.start()
    copies = []
    for k in range(1, n_expert):
        target = lax.rem(mine_e + k, n_expert)
        copy = pltpu.make_async_remote_copy(
            src_ref=outgoing.at[target],
            dst_ref=mine_ref.at[mine_e],
            send_sem=ex_send.at[k - 1],
            recv_sem=ex_recv.at[k - 1],
            device_id={"expert": target},
            device_id_type=mesh_id,
        )
        copy.start()
        copies.append(copy)
    local.wait()
    for copy in copies:
        copy.wait()
    keep.wait()


def spread_select(chosen, split, cid):
    n_dp = lax.axis_size("dp")
    n_expert = lax.axis_size("expert")
    _, group, rows, width = split.shape
    n_blocks = n_dp * group
    return pl.pallas_call(
        functools.partial(_spread_kernel, n_dp, n_expert),
        out_shape=[
            jax.ShapeDtypeStruct((n_blocks, rows, width), split.dtype),
            jax.ShapeDtypeStruct((n_expert, CAP, rows, width), split.dtype),
        ],
        in_specs=[pl.BlockSpec(memory_space=pltpu.SMEM), pl.BlockSpec(memory_space=pl.ANY)],
        out_specs=[pl.BlockSpec(memory_space=pl.ANY)] * 2,
        scratch_shapes=[
            pltpu.VMEM((n_blocks, rows, width), split.dtype),
            pltpu.VMEM((n_expert, CAP, rows, width), split.dtype),
            pltpu.SemaphoreType.DMA((3,)),
            pltpu.SemaphoreType.DMA((n_dp - 1,)),
            pltpu.SemaphoreType.DMA((n_dp - 1,)),
            pltpu.SemaphoreType.DMA((n_expert - 1,)),
            pltpu.SemaphoreType.DMA((n_expert - 1,)),
        ],
        compiler_params=pltpu.CompilerParams(collective_id=cid, has_side_effects=True),
    )(chosen, split)


def body(
    context,
    out_weight,
    residual,
    gate_weight,
    up_weight,
    down_weight,
    gate_values,
    chosen_blocks,
    block_counts,
):
    n_dp = lax.axis_size("dp")
    n_expert = lax.axis_size("expert")
    local_tokens = context.shape[0]
    local_width = residual.shape[1]
    model_width = context.shape[1]
    local_blocks = local_tokens // BLK
    n_blocks = local_blocks * n_dp
    piece = BLK // n_dp
    my_expert = lax.axis_index("expert")

    attended = gather_attend(out_weight, context, residual, cid=10)

    split = attended.reshape(local_blocks, n_dp, piece, local_width).transpose(1, 0, 2, 3)
    pieces, mine = spread_select(chosen_blocks.reshape(-1), split, cid=0)
    mine = mine.transpose(1, 2, 0, 3).reshape(CAP * piece, model_width)
    w_gate = gate_weight[0]
    w_up = up_weight[0]
    w_down = down_weight[0]
    gate_row = gate_values[0]
    my_count = lax.dynamic_index_in_dim(block_counts, my_expert, 0, keepdims=False)
    live = jnp.arange(CAP * BLK) // BLK < my_count
    scale = jnp.where(live, gate_row, jnp.zeros_like(gate_row))
    scale = scale.reshape(CAP, n_dp, piece).transpose(1, 0, 2).reshape(-1)

    hidden = gather_gate(mine, w_gate, w_up, cid=20)
    halves = down_scatter(hidden, w_down, scale[:, None], cid=1)

    outs = reduce_scatter_2d(halves, cid=2)
    outs = outs.reshape(n_expert * CAP, piece * local_width)

    selector = chosen_blocks.reshape(-1)[None, :] == jnp.arange(n_blocks)[:, None]
    added = jnp.dot(selector.astype(jnp.bfloat16), outs, preferred_element_type=jnp.float32)
    mixed = pieces.reshape(n_blocks, piece * local_width).astype(jnp.float32) + added
    mixed = mixed.astype(jnp.bfloat16).reshape(n_dp, local_blocks, piece, local_width)
    back = dp_exchange(mixed, gather=False, cid=3)
    return back.transpose(1, 0, 2, 3).reshape(local_tokens, local_width)


def solution(mesh):
    in_specs = (
        P("dp", None),
        P("dp", "expert"),
        P("dp", "expert"),
        P("expert", None, "dp"),
        P("expert", None, "dp"),
        P("expert", "dp", None),
        P("expert", None),
        P(),
        P(),
    )
    out_specs = P("dp", "expert")
    return jax.shard_map(body, mesh=mesh, in_specs=in_specs, out_specs=out_specs, check_vma=False)
```

```python
import functools

import jax
import jax.numpy as jnp
from jax import lax
from jax.sharding import PartitionSpec as P
from jax.experimental import pallas as pl
from jax.experimental.pallas import tpu as pltpu

BLK = 128
CAP = 4


def _exchange_kernel(n, gather, axis, x_ref, o_ref, local_sem, send_sems, recv_sems):
    me = lax.axis_index(axis)
    mesh_id = pl.DeviceIdType.MESH
    barrier = pltpu.get_barrier_semaphore()
    for k in range(1, n):
        pl.semaphore_signal(barrier, 1, device_id={axis: lax.rem(me + k, n)}, device_id_type=mesh_id)
    pl.semaphore_wait(barrier, n - 1)
    local = pltpu.make_async_copy(x_ref if gather else x_ref.at[me], o_ref.at[me], local_sem)
    local.start()
    copies = []
    for k in range(1, n):
        target = lax.rem(me + k, n)
        copy = pltpu.make_async_remote_copy(
            src_ref=x_ref if gather else x_ref.at[target],
            dst_ref=o_ref.at[me],
            send_sem=send_sems.at[k - 1],
            recv_sem=recv_sems.at[k - 1],
            device_id={axis: target},
            device_id_type=mesh_id,
        )
        copy.start()
        copies.append(copy)
    local.wait()
    for copy in copies:
        copy.wait()


def dp_exchange(x, gather, cid, axis="dp"):
    n = lax.axis_size(axis)
    shape = (n,) + x.shape if gather else x.shape
    return pl.pallas_call(
        functools.partial(_exchange_kernel, n, gather, axis),
        out_shape=jax.ShapeDtypeStruct(shape, x.dtype),
        in_specs=[pl.BlockSpec(memory_space=pl.ANY)],
        out_specs=pl.BlockSpec(memory_space=pl.ANY),
        scratch_shapes=[
            pltpu.SemaphoreType.DMA(()),
            pltpu.SemaphoreType.DMA((n - 1,)),
            pltpu.SemaphoreType.DMA((n - 1,)),
        ],
        compiler_params=pltpu.CompilerParams(collective_id=cid, has_side_effects=True),
    )(x)


def _route_kernel(strides, side, gather, windows, *refs):
    n_in = len(strides)
    ins, outs = refs[:n_in], refs[n_in:2 * n_in]
    local_sems, send_sems, recv_sems = refs[2 * n_in:]
    me = lax.axis_index("dp")
    mesh_id = pl.DeviceIdType.MESH

    def window(r):
        if windows is None:
            return ins[r]
        start, size = windows[r]
        return ins[r].at[:, pl.ds(start, size)]

    routes = []
    for r, stride in enumerate(strides):
        coord = lax.rem(me // stride, side)
        base = me - coord * stride
        for k in range(1, side):
            to = lax.rem(coord + k, side)
            routes.append((r, coord, to, base + to * stride))
    barrier = pltpu.get_barrier_semaphore()
    for _, _, _, target in routes:
        pl.semaphore_signal(barrier, 1, device_id={"dp": target}, device_id_type=mesh_id)
    pl.semaphore_wait(barrier, len(routes))
    locals_ = []
    for r in range(n_in):
        coord = lax.rem(me // strides[r], side)
        source = window(r) if gather else ins[r].at[coord]
        local = pltpu.make_async_copy(source, outs[r].at[coord], local_sems.at[r])
        local.start()
        locals_.append(local)
    copies = []
    for i, (r, coord, to, target) in enumerate(routes):
        copy = pltpu.make_async_remote_copy(
            src_ref=window(r) if gather else ins[r].at[to],
            dst_ref=outs[r].at[coord],
            send_sem=send_sems.at[i],
            recv_sem=recv_sems.at[i],
            device_id={"dp": target},
            device_id_type=mesh_id,
        )
        copy.start()
        copies.append(copy)
    for local in locals_:
        local.wait()
    for copy in copies:
        copy.wait()


def dp_route(xs, strides, cid, side=4, gather=False, windows=None):
    n_routes = len(strides) * (side - 1)
    if windows is not None:
        shapes = [(side, x.shape[0], size) for x, (_, size) in zip(xs, windows)]
    else:
        shapes = [((side,) + x.shape) if gather else x.shape for x in xs]
    return pl.pallas_call(
        functools.partial(_route_kernel, tuple(strides), side, gather, windows),
        out_shape=[jax.ShapeDtypeStruct(s, x.dtype) for s, x in zip(shapes, xs)],
        in_specs=[pl.BlockSpec(memory_space=pl.ANY)] * len(xs),
        out_specs=[pl.BlockSpec(memory_space=pl.ANY)] * len(xs),
        scratch_shapes=[
            pltpu.SemaphoreType.DMA((len(xs),)),
            pltpu.SemaphoreType.DMA((n_routes,)),
            pltpu.SemaphoreType.DMA((n_routes,)),
        ],
        compiler_params=pltpu.CompilerParams(collective_id=cid, has_side_effects=True),
    )(*xs)


def _finish_kernel(side, n_expert, a_ref, b_ref, out_ref, got_a, got_b, outgoing,
                   local_sems, send_sems, recv_sems, ex_send, ex_recv):
    me = lax.axis_index("dp")
    mine_e = lax.axis_index("expert")
    mesh_id = pl.DeviceIdType.MESH
    routes = ((a_ref, got_a, side), (b_ref, got_b, 1))
    barrier = pltpu.get_barrier_semaphore()
    for _, _, stride in routes:
        coord = lax.rem(me // stride, side)
        base = me - coord * stride
        for k in range(1, side):
            peer = base + lax.rem(coord + k, side) * stride
            pl.semaphore_signal(barrier, 1, device_id={"dp": peer}, device_id_type=mesh_id)
    for k in range(1, n_expert):
        pl.semaphore_signal(
            barrier, 1, device_id={"expert": lax.rem(mine_e + k, n_expert)}, device_id_type=mesh_id
        )
    pl.semaphore_wait(barrier, 2 * (side - 1) + n_expert - 1)
    locals_, copies = [], []
    for r, (src, dst, stride) in enumerate(routes):
        coord = lax.rem(me // stride, side)
        base = me - coord * stride
        local = pltpu.make_async_copy(src.at[coord], dst.at[coord], local_sems.at[r])
        local.start()
        locals_.append(local)
        for k in range(1, side):
            to = lax.rem(coord + k, side)
            copy = pltpu.make_async_remote_copy(
                src_ref=src.at[to],
                dst_ref=dst.at[coord],
                send_sem=send_sems.at[r, k - 1],
                recv_sem=recv_sems.at[r, k - 1],
                device_id={"dp": base + to * stride},
                device_id_type=mesh_id,
            )
            copy.start()
            copies.append(copy)
    for local in locals_:
        local.wait()
    for copy in copies:
        copy.wait()
    width = outgoing.shape[-1]
    per_half = got_a.shape[-1] // width
    for h, got in enumerate((got_a, got_b)):
        total = got[0].astype(jnp.float32)
        for j in range(1, side):
            total = total + got[j].astype(jnp.float32)
        total = total.astype(outgoing.dtype)
        for j in range(per_half):
            outgoing[h * per_half + j] = total[:, j * width:(j + 1) * width]
    local = pltpu.make_async_copy(outgoing.at[mine_e], out_ref.at[mine_e], local_sems.at[2])
    local.start()
    copies = []
    for k in range(1, n_expert):
        target = lax.rem(mine_e + k, n_expert)
        copy = pltpu.make_async_remote_copy(
            src_ref=outgoing.at[target],
            dst_ref=out_ref.at[mine_e],
            send_sem=ex_send.at[k - 1],
            recv_sem=ex_recv.at[k - 1],
            device_id={"expert": target},
            device_id_type=mesh_id,
        )
        copy.start()
        copies.append(copy)
    local.wait()
    for copy in copies:
        copy.wait()


def _down_scatter_kernel(side, hidden_ref, wd_ref, scale_ref, sum_a, sum_b,
                         send_a, send_b, got_a, got_b, send_sems, recv_sems):
    me = lax.axis_index("dp")
    mesh_id = pl.DeviceIdType.MESH
    half = send_a.shape[-1]
    rows = send_a.shape[2]
    chunk = side * rows
    my_y = lax.rem(me, side)
    my_x = lax.rem(me // side, side)
    base_y = me - my_y
    base_x = me - my_x * side
    barrier = pltpu.get_barrier_semaphore()
    for k in range(1, side):
        pl.semaphore_signal(barrier, 1, device_id={"dp": base_y + lax.rem(my_y + k, side)}, device_id_type=mesh_id)
        pl.semaphore_signal(
            barrier, 1, device_id={"dp": base_x + lax.rem(my_x + k, side) * side}, device_id_type=mesh_id
        )
    pl.semaphore_wait(barrier, 2 * (side - 1))

    def to_a(k, y):
        return pltpu.make_async_remote_copy(
            src_ref=send_a.at[y], dst_ref=got_a.at[my_y], send_sem=send_sems.at[0, k - 1],
            recv_sem=recv_sems.at[0, k - 1], device_id={"dp": base_y + y}, device_id_type=mesh_id,
        )

    def to_b(k, x):
        return pltpu.make_async_remote_copy(
            src_ref=send_b.at[x], dst_ref=got_b.at[my_x], send_sem=send_sems.at[1, k - 1],
            recv_sem=recv_sems.at[1, k - 1], device_id={"dp": base_x + x * side}, device_id_type=mesh_id,
        )

    sends = []
    for k in list(range(1, side)) + [0]:
        x = lax.rem(my_x + k, side)
        at = pl.ds(pl.multiple_of(x * chunk, chunk), chunk)
        part = jnp.dot(hidden_ref[at], wd_ref[...], preferred_element_type=jnp.float32)
        part = (part * scale_ref[at]).astype(send_a.dtype)
        for y in range(side):
            send_a[y, x] = part[y * rows:(y + 1) * rows, :half]
            send_b[x, y] = part[y * rows:(y + 1) * rows, half:]
        if k:
            copy = to_b(k, x)
            copy.start()
            sends.append(copy)
    for k in range(1, side):
        copy = to_a(k, lax.rem(my_y + k, side))
        copy.start()
        sends.append(copy)
    for k in range(1, side):
        to_a(k, lax.rem(my_y + side - k, side)).wait_recv()
        to_b(k, lax.rem(my_x + side - k, side)).wait_recv()
    for x in range(side):
        total = send_a[my_y, x].astype(jnp.float32)
        for k in range(1, side):
            total = total + got_a[lax.rem(my_y + side - k, side), x].astype(jnp.float32)
        sum_a[x] = total.astype(sum_a.dtype)
    for y in range(side):
        total = send_b[my_x, y].astype(jnp.float32)
        for k in range(1, side):
            total = total + got_b[lax.rem(my_x + side - k, side), y].astype(jnp.float32)
        sum_b[y] = total.astype(sum_b.dtype)
    for copy in sends:
        copy.wait_send()


def down_scatter(hidden, w_down, scale, cid):
    side = 4
    rows = hidden.shape[0] // (side * side)
    half = w_down.shape[1] // 2
    slab = (side, side, rows, half)
    vmem = pl.BlockSpec(memory_space=pltpu.VMEM)
    return pl.pallas_call(
        functools.partial(_down_scatter_kernel, side),
        out_shape=[jax.ShapeDtypeStruct((side, rows, half), jnp.bfloat16)] * 2,
        in_specs=[vmem] * 3,
        out_specs=[vmem] * 2,
        scratch_shapes=[
            pltpu.VMEM(slab, jnp.bfloat16),
            pltpu.VMEM(slab, jnp.bfloat16),
            pltpu.VMEM(slab, jnp.bfloat16),
            pltpu.VMEM(slab, jnp.bfloat16),
            pltpu.SemaphoreType.DMA((2, side - 1)),
            pltpu.SemaphoreType.DMA((2, side - 1)),
        ],
        compiler_params=pltpu.CompilerParams(collective_id=cid, has_side_effects=True),
    )(hidden, w_down, scale)


def reduce_scatter_2d(part, cid):
    side = 4
    n_expert = lax.axis_size("expert")
    second_a, second_b = part
    rows = second_a.shape[1]
    cols = 2 * second_a.shape[2]
    width = cols // n_expert
    return pl.pallas_call(
        functools.partial(_finish_kernel, side, n_expert),
        out_shape=jax.ShapeDtypeStruct((n_expert, rows, width), second_a.dtype),
        in_specs=[pl.BlockSpec(memory_space=pl.ANY)] * 2,
        out_specs=pl.BlockSpec(memory_space=pl.ANY),
        scratch_shapes=[
            pltpu.VMEM(second_a.shape, second_a.dtype),
            pltpu.VMEM(second_b.shape, second_b.dtype),
            pltpu.VMEM((n_expert, rows, width), second_a.dtype),
            pltpu.SemaphoreType.DMA((3,)),
            pltpu.SemaphoreType.DMA((2, side - 1)),
            pltpu.SemaphoreType.DMA((2, side - 1)),
            pltpu.SemaphoreType.DMA((n_expert - 1,)),
            pltpu.SemaphoreType.DMA((n_expert - 1,)),
        ],
        compiler_params=pltpu.CompilerParams(collective_id=cid, has_side_effects=True),
    )(second_a, second_b)


def all_gather_2d(x, cid):
    side = 4
    half = x.shape[-1] // 2
    got_a, got_b = dp_route([x, x], (1, side), cid, gather=True, windows=((0, half), (half, half)))
    got_a, got_b = dp_route([got_a, got_b], (side, 1), cid + 1, gather=True)
    n = side * side
    got_a = got_a.reshape((n,) + got_a.shape[2:])
    perm = (1, 0) + tuple(range(2, got_b.ndim))
    got_b = got_b.transpose(perm).reshape((n,) + got_b.shape[2:])
    return got_a, got_b


def _gather_gate_kernel(side, a_ref, b_ref, wg_ref, wu_ref, hidden_ref,
                        got_a, got_b, acc_g, acc_u, local_sems, send_sems, recv_sems):
    me = lax.axis_index("dp")
    mesh_id = pl.DeviceIdType.MESH
    half = a_ref.shape[-1]
    group = got_a.shape[1] * got_a.shape[2]
    rows = got_a.shape[2]
    routes = ((a_ref, got_a, side), (b_ref, got_b, 1))
    geo = []
    for _, _, stride in routes:
        coord = lax.rem(me // stride, side)
        geo.append((coord, me - coord * stride))
    barrier = pltpu.get_barrier_semaphore()
    for (coord, base), (_, _, stride) in zip(geo, routes):
        for k in range(1, side):
            peer = base + lax.rem(coord + k, side) * stride
            pl.semaphore_signal(barrier, 1, device_id={"dp": peer}, device_id_type=mesh_id)
    pl.semaphore_wait(barrier, 2 * (side - 1))

    def remote(r, k, source, to):
        src, dst, stride = routes[r]
        coord, base = geo[r]
        return pltpu.make_async_remote_copy(
            src_ref=src,
            dst_ref=dst.at[source],
            send_sem=send_sems.at[r, k - 1],
            recv_sem=recv_sems.at[r, k - 1],
            device_id={"dp": base + to * stride},
            device_id_type=mesh_id,
        )

    locals_, sends = [], []
    for r, (src, dst, stride) in enumerate(routes):
        coord, base = geo[r]
        local = pltpu.make_async_copy(src, dst.at[coord], local_sems.at[r])
        local.start()
        locals_.append(local)
        for k in range(1, side):
            copy = remote(r, k, coord, lax.rem(coord + k, side))
            copy.start()
            sends.append(copy)
    acc_g[...] = jnp.zeros_like(acc_g)
    acc_u[...] = jnp.zeros_like(acc_u)

    def add_a(source):
        block = got_a[source].reshape(group, half)
        at = pl.ds(pl.multiple_of(source * group, group), group)
        acc_g[at] += jnp.dot(block, wg_ref[:half], preferred_element_type=jnp.float32)
        acc_u[at] += jnp.dot(block, wu_ref[:half], preferred_element_type=jnp.float32)

    def add_b(source):
        block = got_b[source].reshape(group, half)
        g = jnp.dot(block, wg_ref[half:], preferred_element_type=jnp.float32)
        u = jnp.dot(block, wu_ref[half:], preferred_element_type=jnp.float32)
        for x in range(side):
            at = pl.ds(pl.multiple_of((x * side + source) * rows, rows), rows)
            acc_g[at] += g[x * rows:(x + 1) * rows]
            acc_u[at] += u[x * rows:(x + 1) * rows]

    for local in locals_:
        local.wait()
    add_a(geo[0][0])
    add_b(geo[1][0])
    for k in range(1, side):
        for r, add in ((0, add_a), (1, add_b)):
            coord, _ = geo[r]
            source = lax.rem(coord + side - k, side)
            remote(r, k, source, source).wait_recv()
            add(source)
    g = acc_g[...]
    hidden_ref[...] = (g / (1.0 + jnp.exp(-g)) * acc_u[...]).astype(hidden_ref.dtype)
    for copy in sends:
        copy.wait_send()


def gather_gate(x, w_gate, w_up, cid):
    side = 4
    n = side * side
    half = x.shape[-1] // 2
    first_a, first_b = dp_route([x, x], (1, side), cid, gather=True, windows=((0, half), (half, half)))
    return pl.pallas_call(
        functools.partial(_gather_gate_kernel, side),
        out_shape=jax.ShapeDtypeStruct((n * x.shape[0], w_gate.shape[1]), jnp.bfloat16),
        in_specs=[pl.BlockSpec(memory_space=pl.ANY)] * 2 + [pl.BlockSpec(memory_space=pltpu.VMEM)] * 2,
        out_specs=pl.BlockSpec(memory_space=pltpu.VMEM),
        scratch_shapes=[
            pltpu.VMEM((side,) + first_a.shape, first_a.dtype),
            pltpu.VMEM((side,) + first_b.shape, first_b.dtype),
            pltpu.VMEM((n * x.shape[0], w_gate.shape[1]), jnp.float32),
            pltpu.VMEM((n * x.shape[0], w_gate.shape[1]), jnp.float32),
            pltpu.SemaphoreType.DMA((2,)),
            pltpu.SemaphoreType.DMA((2, side - 1)),
            pltpu.SemaphoreType.DMA((2, side - 1)),
        ],
        compiler_params=pltpu.CompilerParams(collective_id=cid + 1, has_side_effects=True),
    )(first_a, first_b, w_gate, w_up)


def _gather_attend_kernel(side, a_ref, b_ref, ctx_ref, res_ref, out_ref,
                          got_a, got_b, acc_a, acc_b, local_sems, send_sems, recv_sems):
    me = lax.axis_index("dp")
    mesh_id = pl.DeviceIdType.MESH
    rows = got_a.shape[2]
    bundle = side * rows
    routes = ((a_ref, got_a, side), (b_ref, got_b, 1))
    geo = []
    for _, _, stride in routes:
        coord = lax.rem(me // stride, side)
        geo.append((coord, me - coord * stride))
    barrier = pltpu.get_barrier_semaphore()
    for (coord, base), (_, _, stride) in zip(geo, routes):
        for k in range(1, side):
            peer = base + lax.rem(coord + k, side) * stride
            pl.semaphore_signal(barrier, 1, device_id={"dp": peer}, device_id_type=mesh_id)
    pl.semaphore_wait(barrier, 2 * (side - 1))

    def remote(r, k, source, to):
        src, dst, stride = routes[r]
        coord, base = geo[r]
        return pltpu.make_async_remote_copy(
            src_ref=src,
            dst_ref=dst.at[source],
            send_sem=send_sems.at[r, k - 1],
            recv_sem=recv_sems.at[r, k - 1],
            device_id={"dp": base + to * stride},
            device_id_type=mesh_id,
        )

    locals_, sends = [], []
    for r, (src, dst, stride) in enumerate(routes):
        coord, base = geo[r]
        local = pltpu.make_async_copy(src, dst.at[coord], local_sems.at[r])
        local.start()
        locals_.append(local)
        for k in range(1, side):
            copy = remote(r, k, coord, lax.rem(coord + k, side))
            copy.start()
            sends.append(copy)
    acc_a[...] = jnp.zeros_like(acc_a)
    acc_b[...] = jnp.zeros_like(acc_b)

    def add_a(source):
        block = got_a[source].reshape(bundle, got_a.shape[-1])
        at = pl.ds(pl.multiple_of(source * bundle, bundle), bundle)
        acc_a[...] += jnp.dot(ctx_ref[:, at], block, preferred_element_type=jnp.float32)

    def add_b(source):
        for x in range(side):
            at = pl.ds(pl.multiple_of((x * side + source) * rows, rows), rows)
            acc_b[...] += jnp.dot(ctx_ref[:, at], got_b[source, x], preferred_element_type=jnp.float32)

    for local in locals_:
        local.wait()
    add_a(geo[0][0])
    add_b(geo[1][0])
    for k in range(1, side):
        for r, add in ((0, add_a), (1, add_b)):
            coord, _ = geo[r]
            source = lax.rem(coord + side - k, side)
            remote(r, k, source, source).wait_recv()
            add(source)
    half = acc_a.shape[1]
    out_ref[:, :half] = (res_ref[:, :half].astype(jnp.float32) + acc_a[...]).astype(out_ref.dtype)
    out_ref[:, half:] = (res_ref[:, half:].astype(jnp.float32) + acc_b[...]).astype(out_ref.dtype)
    for copy in sends:
        copy.wait_send()


def gather_attend(w, context, residual, cid):
    side = 4
    half = w.shape[-1] // 2
    first_a, first_b = dp_route([w, w], (1, side), cid, gather=True, windows=((0, half), (half, half)))
    vmem = pl.BlockSpec(memory_space=pltpu.VMEM)
    return pl.pallas_call(
        functools.partial(_gather_attend_kernel, side),
        out_shape=jax.ShapeDtypeStruct(residual.shape, jnp.bfloat16),
        in_specs=[pl.BlockSpec(memory_space=pl.ANY)] * 2 + [vmem] * 2,
        out_specs=vmem,
        scratch_shapes=[
            pltpu.VMEM((side,) + first_a.shape, first_a.dtype),
            pltpu.VMEM((side,) + first_b.shape, first_b.dtype),
            pltpu.VMEM((context.shape[0], half), jnp.float32),
            pltpu.VMEM((context.shape[0], half), jnp.float32),
            pltpu.SemaphoreType.DMA((2,)),
            pltpu.SemaphoreType.DMA((2, side - 1)),
            pltpu.SemaphoreType.DMA((2, side - 1)),
        ],
        compiler_params=pltpu.CompilerParams(collective_id=cid + 1, has_side_effects=True),
    )(first_a, first_b, context, residual)


def _spread_kernel(n_dp, n_expert, chosen_ref, split_ref, pieces_ref, mine_ref,
                   held, outgoing, local_sems, dp_send, dp_recv, ex_send, ex_recv):
    me = lax.axis_index("dp")
    mine_e = lax.axis_index("expert")
    mesh_id = pl.DeviceIdType.MESH
    group = split_ref.shape[1]
    barrier = pltpu.get_barrier_semaphore()
    for k in range(1, n_dp):
        pl.semaphore_signal(barrier, 1, device_id={"dp": lax.rem(me + k, n_dp)}, device_id_type=mesh_id)
    for k in range(1, n_expert):
        pl.semaphore_signal(
            barrier, 1, device_id={"expert": lax.rem(mine_e + k, n_expert)}, device_id_type=mesh_id
        )
    pl.semaphore_wait(barrier, n_dp + n_expert - 2)

    def at_source(src):
        return held.at[pl.ds(pl.multiple_of(src * group, group), group)]

    local = pltpu.make_async_copy(split_ref.at[me], at_source(me), local_sems.at[0])
    local.start()
    copies = []
    for k in range(1, n_dp):
        target = lax.rem(me + k, n_dp)
        copy = pltpu.make_async_remote_copy(
            src_ref=split_ref.at[target],
            dst_ref=at_source(me),
            send_sem=dp_send.at[k - 1],
            recv_sem=dp_recv.at[k - 1],
            device_id={"dp": target},
            device_id_type=mesh_id,
        )
        copy.start()
        copies.append(copy)
    local.wait()
    for copy in copies:
        copy.wait()
    keep = pltpu.make_async_copy(held, pieces_ref, local_sems.at[1])
    keep.start()
    rows = held.shape[1]
    width = held.shape[2]
    for e in range(n_expert):
        for s in range(CAP):
            outgoing[e, s * rows:(s + 1) * rows] = held[chosen_ref[e * CAP + s]]
    columns = pl.ds(pl.multiple_of(mine_e * width, width), width)
    local = pltpu.make_async_copy(outgoing.at[mine_e], mine_ref.at[:, columns], local_sems.at[2])
    local.start()
    copies = []
    for k in range(1, n_expert):
        target = lax.rem(mine_e + k, n_expert)
        copy = pltpu.make_async_remote_copy(
            src_ref=outgoing.at[target],
            dst_ref=mine_ref.at[:, columns],
            send_sem=ex_send.at[k - 1],
            recv_sem=ex_recv.at[k - 1],
            device_id={"expert": target},
            device_id_type=mesh_id,
        )
        copy.start()
        copies.append(copy)
    local.wait()
    for copy in copies:
        copy.wait()
    keep.wait()


def spread_select(chosen, split, cid):
    n_dp = lax.axis_size("dp")
    n_expert = lax.axis_size("expert")
    _, group, rows, width = split.shape
    n_blocks = n_dp * group
    return pl.pallas_call(
        functools.partial(_spread_kernel, n_dp, n_expert),
        out_shape=[
            jax.ShapeDtypeStruct((n_blocks, rows, width), split.dtype),
            jax.ShapeDtypeStruct((CAP * rows, n_expert * width), split.dtype),
        ],
        in_specs=[pl.BlockSpec(memory_space=pltpu.SMEM), pl.BlockSpec(memory_space=pl.ANY)],
        out_specs=[pl.BlockSpec(memory_space=pl.ANY)] * 2,
        scratch_shapes=[
            pltpu.VMEM((n_blocks, rows, width), split.dtype),
            pltpu.VMEM((n_expert, CAP * rows, width), split.dtype),
            pltpu.SemaphoreType.DMA((3,)),
            pltpu.SemaphoreType.DMA((n_dp - 1,)),
            pltpu.SemaphoreType.DMA((n_dp - 1,)),
            pltpu.SemaphoreType.DMA((n_expert - 1,)),
            pltpu.SemaphoreType.DMA((n_expert - 1,)),
        ],
        compiler_params=pltpu.CompilerParams(collective_id=cid, has_side_effects=True),
    )(chosen, split)


def body(
    context,
    out_weight,
    residual,
    gate_weight,
    up_weight,
    down_weight,
    gate_values,
    chosen_blocks,
    block_counts,
):
    n_dp = lax.axis_size("dp")
    n_expert = lax.axis_size("expert")
    local_tokens = context.shape[0]
    local_width = residual.shape[1]
    model_width = context.shape[1]
    local_blocks = local_tokens // BLK
    n_blocks = local_blocks * n_dp
    piece = BLK // n_dp
    my_expert = lax.axis_index("expert")

    attended = gather_attend(out_weight, context, residual, cid=10)

    split = attended.reshape(local_blocks, n_dp, piece, local_width).transpose(1, 0, 2, 3)
    pieces, mine = spread_select(chosen_blocks.reshape(-1), split, cid=0)
    w_gate = gate_weight[0]
    w_up = up_weight[0]
    w_down = down_weight[0]
    gate_row = gate_values[0]
    my_count = lax.dynamic_index_in_dim(block_counts, my_expert, 0, keepdims=False)
    live = jnp.arange(CAP * BLK) // BLK < my_count
    scale = jnp.where(live, gate_row, jnp.zeros_like(gate_row))
    scale = scale.reshape(CAP, n_dp, piece).transpose(1, 0, 2).reshape(-1)

    hidden = gather_gate(mine, w_gate, w_up, cid=20)
    halves = down_scatter(hidden, w_down, scale[:, None], cid=1)

    outs = reduce_scatter_2d(halves, cid=2)
    outs = outs.reshape(n_expert * CAP, piece * local_width)

    selector = chosen_blocks.reshape(-1)[None, :] == jnp.arange(n_blocks)[:, None]
    added = jnp.dot(selector.astype(jnp.bfloat16), outs, preferred_element_type=jnp.float32)
    mixed = pieces.reshape(n_blocks, piece * local_width).astype(jnp.float32) + added
    mixed = mixed.astype(jnp.bfloat16).reshape(n_dp, local_blocks, piece, local_width)
    back = dp_exchange(mixed, gather=False, cid=3)
    return back.transpose(1, 0, 2, 3).reshape(local_tokens, local_width)


def solution(mesh):
    in_specs = (
        P("dp", None),
        P("dp", "expert"),
        P("dp", "expert"),
        P("expert", None, "dp"),
        P("expert", None, "dp"),
        P("expert", "dp", None),
        P("expert", None),
        P(),
        P(),
    )
    out_specs = P("dp", "expert")
    return jax.shard_map(body, mesh=mesh, in_specs=in_specs, out_specs=out_specs, check_vma=False)
```

```python
import functools

import jax
import jax.numpy as jnp
from jax import lax
from jax.sharding import PartitionSpec as P
from jax.experimental import pallas as pl
from jax.experimental.pallas import tpu as pltpu

BLK = 128
CAP = 4


def _exchange_kernel(n, gather, axis, x_ref, o_ref, local_sem, send_sems, recv_sems):
    me = lax.axis_index(axis)
    mesh_id = pl.DeviceIdType.MESH
    barrier = pltpu.get_barrier_semaphore()
    for k in range(1, n):
        pl.semaphore_signal(barrier, 1, device_id={axis: lax.rem(me + k, n)}, device_id_type=mesh_id)
    pl.semaphore_wait(barrier, n - 1)
    local = pltpu.make_async_copy(x_ref if gather else x_ref.at[me], o_ref.at[me], local_sem)
    local.start()
    copies = []
    for k in range(1, n):
        target = lax.rem(me + k, n)
        copy = pltpu.make_async_remote_copy(
            src_ref=x_ref if gather else x_ref.at[target],
            dst_ref=o_ref.at[me],
            send_sem=send_sems.at[k - 1],
            recv_sem=recv_sems.at[k - 1],
            device_id={axis: target},
            device_id_type=mesh_id,
        )
        copy.start()
        copies.append(copy)
    local.wait()
    for copy in copies:
        copy.wait()


def dp_exchange(x, gather, cid, axis="dp"):
    n = lax.axis_size(axis)
    shape = (n,) + x.shape if gather else x.shape
    return pl.pallas_call(
        functools.partial(_exchange_kernel, n, gather, axis),
        out_shape=jax.ShapeDtypeStruct(shape, x.dtype),
        in_specs=[pl.BlockSpec(memory_space=pl.ANY)],
        out_specs=pl.BlockSpec(memory_space=pl.ANY),
        scratch_shapes=[
            pltpu.SemaphoreType.DMA(()),
            pltpu.SemaphoreType.DMA((n - 1,)),
            pltpu.SemaphoreType.DMA((n - 1,)),
        ],
        compiler_params=pltpu.CompilerParams(collective_id=cid, has_side_effects=True),
    )(x)


def _route_kernel(strides, side, gather, windows, *refs):
    n_in = len(strides)
    ins, outs = refs[:n_in], refs[n_in:2 * n_in]
    local_sems, send_sems, recv_sems = refs[2 * n_in:]
    me = lax.axis_index("dp")
    mesh_id = pl.DeviceIdType.MESH

    def window(r):
        if windows is None:
            return ins[r]
        start, size = windows[r]
        return ins[r].at[:, pl.ds(start, size)]

    routes = []
    for r, stride in enumerate(strides):
        coord = lax.rem(me // stride, side)
        base = me - coord * stride
        for k in range(1, side):
            to = lax.rem(coord + k, side)
            routes.append((r, coord, to, base + to * stride))
    barrier = pltpu.get_barrier_semaphore()
    for _, _, _, target in routes:
        pl.semaphore_signal(barrier, 1, device_id={"dp": target}, device_id_type=mesh_id)
    pl.semaphore_wait(barrier, len(routes))
    locals_ = []
    for r in range(n_in):
        coord = lax.rem(me // strides[r], side)
        source = window(r) if gather else ins[r].at[coord]
        local = pltpu.make_async_copy(source, outs[r].at[coord], local_sems.at[r])
        local.start()
        locals_.append(local)
    copies = []
    for i, (r, coord, to, target) in enumerate(routes):
        copy = pltpu.make_async_remote_copy(
            src_ref=window(r) if gather else ins[r].at[to],
            dst_ref=outs[r].at[coord],
            send_sem=send_sems.at[i],
            recv_sem=recv_sems.at[i],
            device_id={"dp": target},
            device_id_type=mesh_id,
        )
        copy.start()
        copies.append(copy)
    for local in locals_:
        local.wait()
    for copy in copies:
        copy.wait()


def dp_route(xs, strides, cid, side=4, gather=False, windows=None):
    n_routes = len(strides) * (side - 1)
    if windows is not None:
        shapes = [(side, x.shape[0], size) for x, (_, size) in zip(xs, windows)]
    else:
        shapes = [((side,) + x.shape) if gather else x.shape for x in xs]
    return pl.pallas_call(
        functools.partial(_route_kernel, tuple(strides), side, gather, windows),
        out_shape=[jax.ShapeDtypeStruct(s, x.dtype) for s, x in zip(shapes, xs)],
        in_specs=[pl.BlockSpec(memory_space=pl.ANY)] * len(xs),
        out_specs=[pl.BlockSpec(memory_space=pl.ANY)] * len(xs),
        scratch_shapes=[
            pltpu.SemaphoreType.DMA((len(xs),)),
            pltpu.SemaphoreType.DMA((n_routes,)),
            pltpu.SemaphoreType.DMA((n_routes,)),
        ],
        compiler_params=pltpu.CompilerParams(collective_id=cid, has_side_effects=True),
    )(*xs)


def _finish_kernel(side, n_expert, a_ref, b_ref, out_ref, got_a, got_b, outgoing,
                   local_sems, send_sems, recv_sems, ex_send, ex_recv):
    me = lax.axis_index("dp")
    mine_e = lax.axis_index("expert")
    mesh_id = pl.DeviceIdType.MESH
    routes = ((a_ref, got_a, side), (b_ref, got_b, 1))
    barrier = pltpu.get_barrier_semaphore()
    for _, _, stride in routes:
        coord = lax.rem(me // stride, side)
        base = me - coord * stride
        for k in range(1, side):
            peer = base + lax.rem(coord + k, side) * stride
            pl.semaphore_signal(barrier, 1, device_id={"dp": peer}, device_id_type=mesh_id)
    for k in range(1, n_expert):
        pl.semaphore_signal(
            barrier, 1, device_id={"expert": lax.rem(mine_e + k, n_expert)}, device_id_type=mesh_id
        )
    pl.semaphore_wait(barrier, 2 * (side - 1) + n_expert - 1)
    locals_, copies = [], []
    for r, (src, dst, stride) in enumerate(routes):
        coord = lax.rem(me // stride, side)
        base = me - coord * stride
        local = pltpu.make_async_copy(src.at[coord], dst.at[coord], local_sems.at[r])
        local.start()
        locals_.append(local)
        for k in range(1, side):
            to = lax.rem(coord + k, side)
            copy = pltpu.make_async_remote_copy(
                src_ref=src.at[to],
                dst_ref=dst.at[coord],
                send_sem=send_sems.at[r, k - 1],
                recv_sem=recv_sems.at[r, k - 1],
                device_id={"dp": base + to * stride},
                device_id_type=mesh_id,
            )
            copy.start()
            copies.append(copy)
    for local in locals_:
        local.wait()
    for copy in copies:
        copy.wait()
    width = outgoing.shape[-1]
    per_half = got_a.shape[-1] // width
    for h, got in enumerate((got_a, got_b)):
        total = got[0].astype(jnp.float32)
        for j in range(1, side):
            total = total + got[j].astype(jnp.float32)
        total = total.astype(outgoing.dtype)
        for j in range(per_half):
            outgoing[h * per_half + j] = total[:, j * width:(j + 1) * width]
    local = pltpu.make_async_copy(outgoing.at[mine_e], out_ref.at[mine_e], local_sems.at[2])
    local.start()
    copies = []
    for k in range(1, n_expert):
        target = lax.rem(mine_e + k, n_expert)
        copy = pltpu.make_async_remote_copy(
            src_ref=outgoing.at[target],
            dst_ref=out_ref.at[mine_e],
            send_sem=ex_send.at[k - 1],
            recv_sem=ex_recv.at[k - 1],
            device_id={"expert": target},
            device_id_type=mesh_id,
        )
        copy.start()
        copies.append(copy)
    local.wait()
    for copy in copies:
        copy.wait()


def _down_scatter_kernel(side, hidden_ref, wd_ref, scale_ref, sum_a, sum_b,
                         send_a, send_b, got_a, got_b, send_sems, recv_sems):
    me = lax.axis_index("dp")
    mesh_id = pl.DeviceIdType.MESH
    half = send_a.shape[-1]
    rows = send_a.shape[2]
    chunk = side * rows
    my_y = lax.rem(me, side)
    my_x = lax.rem(me // side, side)
    base_y = me - my_y
    base_x = me - my_x * side
    barrier = pltpu.get_barrier_semaphore()
    for k in range(1, side):
        pl.semaphore_signal(barrier, 1, device_id={"dp": base_y + lax.rem(my_y + k, side)}, device_id_type=mesh_id)
        pl.semaphore_signal(
            barrier, 1, device_id={"dp": base_x + lax.rem(my_x + k, side) * side}, device_id_type=mesh_id
        )
    pl.semaphore_wait(barrier, 2 * (side - 1))

    def to_a(k, y):
        return pltpu.make_async_remote_copy(
            src_ref=send_a.at[y], dst_ref=got_a.at[my_y], send_sem=send_sems.at[0, k - 1],
            recv_sem=recv_sems.at[0, k - 1], device_id={"dp": base_y + y}, device_id_type=mesh_id,
        )

    def to_b(k, x):
        return pltpu.make_async_remote_copy(
            src_ref=send_b.at[x], dst_ref=got_b.at[my_x], send_sem=send_sems.at[1, k - 1],
            recv_sem=recv_sems.at[1, k - 1], device_id={"dp": base_x + x * side}, device_id_type=mesh_id,
        )

    sends = []
    for k in list(range(1, side)) + [0]:
        x = lax.rem(my_x + k, side)
        at = pl.ds(pl.multiple_of(x * chunk, chunk), chunk)
        part = jnp.dot(hidden_ref[at], wd_ref[...], preferred_element_type=jnp.float32)
        part = (part * scale_ref[at]).astype(send_a.dtype)
        for y in range(side):
            send_a[y, x] = part[y * rows:(y + 1) * rows, :half]
            send_b[x, y] = part[y * rows:(y + 1) * rows, half:]
        if k:
            copy = to_b(k, x)
            copy.start()
            sends.append(copy)
    for k in range(1, side):
        copy = to_a(k, lax.rem(my_y + k, side))
        copy.start()
        sends.append(copy)
    for k in range(1, side):
        to_a(k, lax.rem(my_y + side - k, side)).wait_recv()
        to_b(k, lax.rem(my_x + side - k, side)).wait_recv()
    for x in range(side):
        total = send_a[my_y, x].astype(jnp.float32)
        for k in range(1, side):
            total = total + got_a[lax.rem(my_y + side - k, side), x].astype(jnp.float32)
        sum_a[x] = total.astype(sum_a.dtype)
    for y in range(side):
        total = send_b[my_x, y].astype(jnp.float32)
        for k in range(1, side):
            total = total + got_b[lax.rem(my_x + side - k, side), y].astype(jnp.float32)
        sum_b[y] = total.astype(sum_b.dtype)
    for copy in sends:
        copy.wait_send()


def down_scatter(hidden, w_down, scale, cid):
    side = 4
    rows = hidden.shape[0] // (side * side)
    half = w_down.shape[1] // 2
    slab = (side, side, rows, half)
    vmem = pl.BlockSpec(memory_space=pltpu.VMEM)
    return pl.pallas_call(
        functools.partial(_down_scatter_kernel, side),
        out_shape=[jax.ShapeDtypeStruct((side, rows, half), jnp.bfloat16)] * 2,
        in_specs=[vmem] * 3,
        out_specs=[vmem] * 2,
        scratch_shapes=[
            pltpu.VMEM(slab, jnp.bfloat16),
            pltpu.VMEM(slab, jnp.bfloat16),
            pltpu.VMEM(slab, jnp.bfloat16),
            pltpu.VMEM(slab, jnp.bfloat16),
            pltpu.SemaphoreType.DMA((2, side - 1)),
            pltpu.SemaphoreType.DMA((2, side - 1)),
        ],
        compiler_params=pltpu.CompilerParams(collective_id=cid, has_side_effects=True),
    )(hidden, w_down, scale)


def reduce_scatter_2d(part, cid):
    side = 4
    n_expert = lax.axis_size("expert")
    second_a, second_b = part
    rows = second_a.shape[1]
    cols = 2 * second_a.shape[2]
    width = cols // n_expert
    return pl.pallas_call(
        functools.partial(_finish_kernel, side, n_expert),
        out_shape=jax.ShapeDtypeStruct((n_expert, rows, width), second_a.dtype),
        in_specs=[pl.BlockSpec(memory_space=pl.ANY)] * 2,
        out_specs=pl.BlockSpec(memory_space=pl.ANY),
        scratch_shapes=[
            pltpu.VMEM(second_a.shape, second_a.dtype),
            pltpu.VMEM(second_b.shape, second_b.dtype),
            pltpu.VMEM((n_expert, rows, width), second_a.dtype),
            pltpu.SemaphoreType.DMA((3,)),
            pltpu.SemaphoreType.DMA((2, side - 1)),
            pltpu.SemaphoreType.DMA((2, side - 1)),
            pltpu.SemaphoreType.DMA((n_expert - 1,)),
            pltpu.SemaphoreType.DMA((n_expert - 1,)),
        ],
        compiler_params=pltpu.CompilerParams(collective_id=cid, has_side_effects=True),
    )(second_a, second_b)


def all_gather_2d(x, cid):
    side = 4
    half = x.shape[-1] // 2
    got_a, got_b = dp_route([x, x], (1, side), cid, gather=True, windows=((0, half), (half, half)))
    got_a, got_b = dp_route([got_a, got_b], (side, 1), cid + 1, gather=True)
    n = side * side
    got_a = got_a.reshape((n,) + got_a.shape[2:])
    perm = (1, 0) + tuple(range(2, got_b.ndim))
    got_b = got_b.transpose(perm).reshape((n,) + got_b.shape[2:])
    return got_a, got_b


def _gather_gate_kernel(side, a_ref, b_ref, wg_ref, wu_ref, hidden_ref,
                        got_a, got_b, acc_g, acc_u, local_sems, send_sems, recv_sems):
    me = lax.axis_index("dp")
    mesh_id = pl.DeviceIdType.MESH
    half = a_ref.shape[-1]
    group = got_a.shape[1] * got_a.shape[2]
    rows = got_a.shape[2]
    routes = ((a_ref, got_a, side), (b_ref, got_b, 1))
    geo = []
    for _, _, stride in routes:
        coord = lax.rem(me // stride, side)
        geo.append((coord, me - coord * stride))
    barrier = pltpu.get_barrier_semaphore()
    for (coord, base), (_, _, stride) in zip(geo, routes):
        for k in range(1, side):
            peer = base + lax.rem(coord + k, side) * stride
            pl.semaphore_signal(barrier, 1, device_id={"dp": peer}, device_id_type=mesh_id)
    pl.semaphore_wait(barrier, 2 * (side - 1))

    def remote(r, k, source, to):
        src, dst, stride = routes[r]
        coord, base = geo[r]
        return pltpu.make_async_remote_copy(
            src_ref=src,
            dst_ref=dst.at[source],
            send_sem=send_sems.at[r, k - 1],
            recv_sem=recv_sems.at[r, k - 1],
            device_id={"dp": base + to * stride},
            device_id_type=mesh_id,
        )

    locals_, sends = [], []
    for r, (src, dst, stride) in enumerate(routes):
        coord, base = geo[r]
        local = pltpu.make_async_copy(src, dst.at[coord], local_sems.at[r])
        local.start()
        locals_.append(local)
        for k in range(1, side):
            copy = remote(r, k, coord, lax.rem(coord + k, side))
            copy.start()
            sends.append(copy)
    acc_g[...] = jnp.zeros_like(acc_g)
    acc_u[...] = jnp.zeros_like(acc_u)

    def add_a(source):
        block = got_a[source].reshape(group, half)
        at = pl.ds(pl.multiple_of(source * group, group), group)
        acc_g[at] += jnp.dot(block, wg_ref[:half], preferred_element_type=jnp.float32)
        acc_u[at] += jnp.dot(block, wu_ref[:half], preferred_element_type=jnp.float32)

    def add_b(source):
        block = got_b[source].reshape(group, half)
        g = jnp.dot(block, wg_ref[half:], preferred_element_type=jnp.float32)
        u = jnp.dot(block, wu_ref[half:], preferred_element_type=jnp.float32)
        for x in range(side):
            at = pl.ds(pl.multiple_of((x * side + source) * rows, rows), rows)
            acc_g[at] += g[x * rows:(x + 1) * rows]
            acc_u[at] += u[x * rows:(x + 1) * rows]

    for local in locals_:
        local.wait()
    add_a(geo[0][0])
    add_b(geo[1][0])
    for k in range(1, side):
        for r, add in ((0, add_a), (1, add_b)):
            coord, _ = geo[r]
            source = lax.rem(coord + side - k, side)
            remote(r, k, source, source).wait_recv()
            add(source)
    g = acc_g[...]
    hidden_ref[...] = (g / (1.0 + jnp.exp(-g)) * acc_u[...]).astype(hidden_ref.dtype)
    for copy in sends:
        copy.wait_send()


def gather_gate(x, w_gate, w_up, cid):
    side = 4
    n = side * side
    half = x.shape[-1] // 2
    first_a, first_b = dp_route([x, x], (1, side), cid, gather=True, windows=((0, half), (half, half)))
    return pl.pallas_call(
        functools.partial(_gather_gate_kernel, side),
        out_shape=jax.ShapeDtypeStruct((n * x.shape[0], w_gate.shape[1]), jnp.bfloat16),
        in_specs=[pl.BlockSpec(memory_space=pl.ANY)] * 2 + [pl.BlockSpec(memory_space=pltpu.VMEM)] * 2,
        out_specs=pl.BlockSpec(memory_space=pltpu.VMEM),
        scratch_shapes=[
            pltpu.VMEM((side,) + first_a.shape, first_a.dtype),
            pltpu.VMEM((side,) + first_b.shape, first_b.dtype),
            pltpu.VMEM((n * x.shape[0], w_gate.shape[1]), jnp.float32),
            pltpu.VMEM((n * x.shape[0], w_gate.shape[1]), jnp.float32),
            pltpu.SemaphoreType.DMA((2,)),
            pltpu.SemaphoreType.DMA((2, side - 1)),
            pltpu.SemaphoreType.DMA((2, side - 1)),
        ],
        compiler_params=pltpu.CompilerParams(collective_id=cid + 1, has_side_effects=True),
    )(first_a, first_b, w_gate, w_up)


def _gather_attend_kernel(side, a_ref, b_ref, ctx_ref, res_ref, out_ref,
                          got_a, got_b, acc_a, acc_b, local_sems, send_sems, recv_sems):
    me = lax.axis_index("dp")
    mesh_id = pl.DeviceIdType.MESH
    rows = got_a.shape[2]
    bundle = side * rows
    routes = ((a_ref, got_a, side), (b_ref, got_b, 1))
    geo = []
    for _, _, stride in routes:
        coord = lax.rem(me // stride, side)
        geo.append((coord, me - coord * stride))
    barrier = pltpu.get_barrier_semaphore()
    for (coord, base), (_, _, stride) in zip(geo, routes):
        for k in range(1, side):
            peer = base + lax.rem(coord + k, side) * stride
            pl.semaphore_signal(barrier, 1, device_id={"dp": peer}, device_id_type=mesh_id)
    pl.semaphore_wait(barrier, 2 * (side - 1))

    def remote(r, k, source, to):
        src, dst, stride = routes[r]
        coord, base = geo[r]
        return pltpu.make_async_remote_copy(
            src_ref=src,
            dst_ref=dst.at[source],
            send_sem=send_sems.at[r, k - 1],
            recv_sem=recv_sems.at[r, k - 1],
            device_id={"dp": base + to * stride},
            device_id_type=mesh_id,
        )

    locals_, sends = [], []
    for r, (src, dst, stride) in enumerate(routes):
        coord, base = geo[r]
        local = pltpu.make_async_copy(src, dst.at[coord], local_sems.at[r])
        local.start()
        locals_.append(local)
        for k in range(1, side):
            copy = remote(r, k, coord, lax.rem(coord + k, side))
            copy.start()
            sends.append(copy)
    acc_a[...] = jnp.zeros_like(acc_a)
    acc_b[...] = jnp.zeros_like(acc_b)

    def add_a(source):
        block = got_a[source].reshape(bundle, got_a.shape[-1])
        at = pl.ds(pl.multiple_of(source * bundle, bundle), bundle)
        acc_a[...] += jnp.dot(ctx_ref[:, at], block, preferred_element_type=jnp.float32)

    def add_b(source):
        for x in range(side):
            at = pl.ds(pl.multiple_of((x * side + source) * rows, rows), rows)
            acc_b[...] += jnp.dot(ctx_ref[:, at], got_b[source, x], preferred_element_type=jnp.float32)

    for local in locals_:
        local.wait()
    add_a(geo[0][0])
    add_b(geo[1][0])
    for k in range(1, side):
        for r, add in ((0, add_a), (1, add_b)):
            coord, _ = geo[r]
            source = lax.rem(coord + side - k, side)
            remote(r, k, source, source).wait_recv()
            add(source)
    half = acc_a.shape[1]
    out_ref[:, :half] = (res_ref[:, :half].astype(jnp.float32) + acc_a[...]).astype(out_ref.dtype)
    out_ref[:, half:] = (res_ref[:, half:].astype(jnp.float32) + acc_b[...]).astype(out_ref.dtype)
    for copy in sends:
        copy.wait_send()


def gather_attend(w, context, residual, cid):
    side = 4
    half = w.shape[-1] // 2
    first_a, first_b = dp_route([w, w], (1, side), cid, gather=True, windows=((0, half), (half, half)))
    vmem = pl.BlockSpec(memory_space=pltpu.VMEM)
    return pl.pallas_call(
        functools.partial(_gather_attend_kernel, side),
        out_shape=jax.ShapeDtypeStruct(residual.shape, jnp.bfloat16),
        in_specs=[pl.BlockSpec(memory_space=pl.ANY)] * 2 + [vmem] * 2,
        out_specs=vmem,
        scratch_shapes=[
            pltpu.VMEM((side,) + first_a.shape, first_a.dtype),
            pltpu.VMEM((side,) + first_b.shape, first_b.dtype),
            pltpu.VMEM((context.shape[0], half), jnp.float32),
            pltpu.VMEM((context.shape[0], half), jnp.float32),
            pltpu.SemaphoreType.DMA((2,)),
            pltpu.SemaphoreType.DMA((2, side - 1)),
            pltpu.SemaphoreType.DMA((2, side - 1)),
        ],
        compiler_params=pltpu.CompilerParams(collective_id=cid + 1, has_side_effects=True),
    )(first_a, first_b, context, residual)


def _spread_kernel(n_dp, n_expert, chosen_ref, split_ref, pieces_ref, mine_ref,
                   held, outgoing, local_sems, dp_send, dp_recv, ex_send, ex_recv):
    me = lax.axis_index("dp")
    mine_e = lax.axis_index("expert")
    mesh_id = pl.DeviceIdType.MESH
    group = split_ref.shape[1]
    barrier = pltpu.get_barrier_semaphore()
    for k in range(1, n_dp):
        pl.semaphore_signal(barrier, 1, device_id={"dp": lax.rem(me + k, n_dp)}, device_id_type=mesh_id)
    for k in range(1, n_expert):
        pl.semaphore_signal(
            barrier, 1, device_id={"expert": lax.rem(mine_e + k, n_expert)}, device_id_type=mesh_id
        )
    pl.semaphore_wait(barrier, n_dp + n_expert - 2)

    def at_source(src):
        return held.at[pl.ds(pl.multiple_of(src * group, group), group)]

    local = pltpu.make_async_copy(split_ref.at[me], at_source(me), local_sems.at[0])
    local.start()
    copies = []
    for k in range(1, n_dp):
        target = lax.rem(me + k, n_dp)
        copy = pltpu.make_async_remote_copy(
            src_ref=split_ref.at[target],
            dst_ref=at_source(me),
            send_sem=dp_send.at[k - 1],
            recv_sem=dp_recv.at[k - 1],
            device_id={"dp": target},
            device_id_type=mesh_id,
        )
        copy.start()
        copies.append(copy)
    local.wait()
    for copy in copies:
        copy.wait()
    keep = pltpu.make_async_copy(held, pieces_ref, local_sems.at[1])
    keep.start()
    rows = held.shape[1]
    width = held.shape[2]
    for e in range(n_expert):
        for s in range(CAP):
            outgoing[e, s * rows:(s + 1) * rows] = held[chosen_ref[e * CAP + s]]
    columns = pl.ds(pl.multiple_of(mine_e * width, width), width)
    local = pltpu.make_async_copy(outgoing.at[mine_e], mine_ref.at[:, columns], local_sems.at[2])
    local.start()
    copies = []
    for k in range(1, n_expert):
        target = lax.rem(mine_e + k, n_expert)
        copy = pltpu.make_async_remote_copy(
            src_ref=outgoing.at[target],
            dst_ref=mine_ref.at[:, columns],
            send_sem=ex_send.at[k - 1],
            recv_sem=ex_recv.at[k - 1],
            device_id={"expert": target},
            device_id_type=mesh_id,
        )
        copy.start()
        copies.append(copy)
    local.wait()
    for copy in copies:
        copy.wait()
    keep.wait()


def spread_select(chosen, split, cid):
    n_dp = lax.axis_size("dp")
    n_expert = lax.axis_size("expert")
    _, group, rows, width = split.shape
    n_blocks = n_dp * group
    return pl.pallas_call(
        functools.partial(_spread_kernel, n_dp, n_expert),
        out_shape=[
            jax.ShapeDtypeStruct((n_blocks, rows, width), split.dtype),
            jax.ShapeDtypeStruct((CAP * rows, n_expert * width), split.dtype),
        ],
        in_specs=[pl.BlockSpec(memory_space=pltpu.SMEM), pl.BlockSpec(memory_space=pl.ANY)],
        out_specs=[pl.BlockSpec(memory_space=pl.ANY)] * 2,
        scratch_shapes=[
            pltpu.VMEM((n_blocks, rows, width), split.dtype),
            pltpu.VMEM((n_expert, CAP * rows, width), split.dtype),
            pltpu.SemaphoreType.DMA((3,)),
            pltpu.SemaphoreType.DMA((n_dp - 1,)),
            pltpu.SemaphoreType.DMA((n_dp - 1,)),
            pltpu.SemaphoreType.DMA((n_expert - 1,)),
            pltpu.SemaphoreType.DMA((n_expert - 1,)),
        ],
        compiler_params=pltpu.CompilerParams(collective_id=cid, has_side_effects=True),
    )(chosen, split)


def body(
    context,
    out_weight,
    residual,
    gate_weight,
    up_weight,
    down_weight,
    gate_values,
    chosen_blocks,
    block_counts,
):
    n_dp = lax.axis_size("dp")
    n_expert = lax.axis_size("expert")
    local_tokens = context.shape[0]
    local_width = residual.shape[1]
    model_width = context.shape[1]
    local_blocks = local_tokens // BLK
    n_blocks = local_blocks * n_dp
    piece = BLK // n_dp
    my_expert = lax.axis_index("expert")

    attended = gather_attend(out_weight, context, residual, cid=10)

    split = attended.reshape(local_blocks, n_dp, piece, local_width).transpose(1, 0, 2, 3)
    pieces, mine = spread_select(chosen_blocks.reshape(-1), split, cid=0)
    w_gate = gate_weight[0]
    w_up = up_weight[0]
    w_down = down_weight[0]
    gate_row = gate_values[0]
    my_count = jnp.sum(jnp.where(jnp.arange(n_expert) == my_expert, block_counts, 0))
    row_slot = (jnp.arange(CAP * BLK) // piece) % CAP
    gate_perm = gate_row.reshape(CAP, n_dp, piece).transpose(1, 0, 2).reshape(-1)
    scale = jnp.where(row_slot < my_count, gate_perm, jnp.zeros_like(gate_perm))

    hidden = gather_gate(mine, w_gate, w_up, cid=20)
    halves = down_scatter(hidden, w_down, scale[:, None], cid=1)

    outs = reduce_scatter_2d(halves, cid=2)
    outs = outs.reshape(n_expert * CAP, piece * local_width)

    selector = chosen_blocks.reshape(-1)[None, :] == jnp.arange(n_blocks)[:, None]
    added = jnp.dot(selector.astype(jnp.bfloat16), outs, preferred_element_type=jnp.float32)
    mixed = pieces.reshape(n_blocks, piece * local_width).astype(jnp.float32) + added
    mixed = mixed.astype(jnp.bfloat16).reshape(n_dp, local_blocks, piece, local_width)
    back = dp_exchange(mixed, gather=False, cid=3)
    return back.transpose(1, 0, 2, 3).reshape(local_tokens, local_width)


def solution(mesh):
    in_specs = (
        P("dp", None),
        P("dp", "expert"),
        P("dp", "expert"),
        P("expert", None, "dp"),
        P("expert", None, "dp"),
        P("expert", "dp", None),
        P("expert", None),
        P(),
        P(),
    )
    out_specs = P("dp", "expert")
    return jax.shard_map(body, mesh=mesh, in_specs=in_specs, out_specs=out_specs, check_vma=False)
```

```python
import functools

import jax
import jax.numpy as jnp
from jax import lax
from jax.sharding import PartitionSpec as P
from jax.experimental import pallas as pl
from jax.experimental.pallas import tpu as pltpu

BLK = 128
CAP = 4


def _exchange_kernel(n, gather, axis, x_ref, o_ref, local_sem, send_sems, recv_sems):
    me = lax.axis_index(axis)
    mesh_id = pl.DeviceIdType.MESH
    barrier = pltpu.get_barrier_semaphore()
    for k in range(1, n):
        pl.semaphore_signal(barrier, 1, device_id={axis: lax.rem(me + k, n)}, device_id_type=mesh_id)
    pl.semaphore_wait(barrier, n - 1)
    local = pltpu.make_async_copy(x_ref if gather else x_ref.at[me], o_ref.at[me], local_sem)
    local.start()
    copies = []
    for k in range(1, n):
        target = lax.rem(me + k, n)
        copy = pltpu.make_async_remote_copy(
            src_ref=x_ref if gather else x_ref.at[target],
            dst_ref=o_ref.at[me],
            send_sem=send_sems.at[k - 1],
            recv_sem=recv_sems.at[k - 1],
            device_id={axis: target},
            device_id_type=mesh_id,
        )
        copy.start()
        copies.append(copy)
    local.wait()
    for copy in copies:
        copy.wait()


def dp_exchange(x, gather, cid, axis="dp"):
    n = lax.axis_size(axis)
    shape = (n,) + x.shape if gather else x.shape
    return pl.pallas_call(
        functools.partial(_exchange_kernel, n, gather, axis),
        out_shape=jax.ShapeDtypeStruct(shape, x.dtype),
        in_specs=[pl.BlockSpec(memory_space=pl.ANY)],
        out_specs=pl.BlockSpec(memory_space=pl.ANY),
        scratch_shapes=[
            pltpu.SemaphoreType.DMA(()),
            pltpu.SemaphoreType.DMA((n - 1,)),
            pltpu.SemaphoreType.DMA((n - 1,)),
        ],
        compiler_params=pltpu.CompilerParams(collective_id=cid, has_side_effects=True),
    )(x)


def _route_kernel(strides, side, gather, windows, *refs):
    n_in = len(strides)
    ins, outs = refs[:n_in], refs[n_in:2 * n_in]
    local_sems, send_sems, recv_sems = refs[2 * n_in:]
    me = lax.axis_index("dp")
    mesh_id = pl.DeviceIdType.MESH

    def window(r):
        if windows is None:
            return ins[r]
        start, size = windows[r]
        return ins[r].at[:, pl.ds(start, size)]

    routes = []
    for r, stride in enumerate(strides):
        coord = lax.rem(me // stride, side)
        base = me - coord * stride
        for k in range(1, side):
            to = lax.rem(coord + k, side)
            routes.append((r, coord, to, base + to * stride))
    barrier = pltpu.get_barrier_semaphore()
    for _, _, _, target in routes:
        pl.semaphore_signal(barrier, 1, device_id={"dp": target}, device_id_type=mesh_id)
    pl.semaphore_wait(barrier, len(routes))
    locals_ = []
    for r in range(n_in):
        coord = lax.rem(me // strides[r], side)
        source = window(r) if gather else ins[r].at[coord]
        local = pltpu.make_async_copy(source, outs[r].at[coord], local_sems.at[r])
        local.start()
        locals_.append(local)
    copies = []
    for i, (r, coord, to, target) in enumerate(routes):
        copy = pltpu.make_async_remote_copy(
            src_ref=window(r) if gather else ins[r].at[to],
            dst_ref=outs[r].at[coord],
            send_sem=send_sems.at[i],
            recv_sem=recv_sems.at[i],
            device_id={"dp": target},
            device_id_type=mesh_id,
        )
        copy.start()
        copies.append(copy)
    for local in locals_:
        local.wait()
    for copy in copies:
        copy.wait()


def dp_route(xs, strides, cid, side=4, gather=False, windows=None):
    n_routes = len(strides) * (side - 1)
    if windows is not None:
        shapes = [(side, x.shape[0], size) for x, (_, size) in zip(xs, windows)]
    else:
        shapes = [((side,) + x.shape) if gather else x.shape for x in xs]
    return pl.pallas_call(
        functools.partial(_route_kernel, tuple(strides), side, gather, windows),
        out_shape=[jax.ShapeDtypeStruct(s, x.dtype) for s, x in zip(shapes, xs)],
        in_specs=[pl.BlockSpec(memory_space=pl.ANY)] * len(xs),
        out_specs=[pl.BlockSpec(memory_space=pl.ANY)] * len(xs),
        scratch_shapes=[
            pltpu.SemaphoreType.DMA((len(xs),)),
            pltpu.SemaphoreType.DMA((n_routes,)),
            pltpu.SemaphoreType.DMA((n_routes,)),
        ],
        compiler_params=pltpu.CompilerParams(collective_id=cid, has_side_effects=True),
    )(*xs)


def _finish_kernel(side, n_expert, a_ref, b_ref, out_ref, got_a, got_b, outgoing,
                   local_sems, send_sems, recv_sems, ex_send, ex_recv):
    me = lax.axis_index("dp")
    mine_e = lax.axis_index("expert")
    mesh_id = pl.DeviceIdType.MESH
    routes = ((a_ref, got_a, side), (b_ref, got_b, 1))
    barrier = pltpu.get_barrier_semaphore()
    for _, _, stride in routes:
        coord = lax.rem(me // stride, side)
        base = me - coord * stride
        for k in range(1, side):
            peer = base + lax.rem(coord + k, side) * stride
            pl.semaphore_signal(barrier, 1, device_id={"dp": peer}, device_id_type=mesh_id)
    for k in range(1, n_expert):
        pl.semaphore_signal(
            barrier, 1, device_id={"expert": lax.rem(mine_e + k, n_expert)}, device_id_type=mesh_id
        )
    pl.semaphore_wait(barrier, 2 * (side - 1) + n_expert - 1)
    locals_, copies = [], []
    for r, (src, dst, stride) in enumerate(routes):
        coord = lax.rem(me // stride, side)
        base = me - coord * stride
        local = pltpu.make_async_copy(src.at[coord], dst.at[coord], local_sems.at[r])
        local.start()
        locals_.append(local)
        for k in range(1, side):
            to = lax.rem(coord + k, side)
            copy = pltpu.make_async_remote_copy(
                src_ref=src.at[to],
                dst_ref=dst.at[coord],
                send_sem=send_sems.at[r, k - 1],
                recv_sem=recv_sems.at[r, k - 1],
                device_id={"dp": base + to * stride},
                device_id_type=mesh_id,
            )
            copy.start()
            copies.append(copy)
    for local in locals_:
        local.wait()
    for copy in copies:
        copy.wait()
    width = outgoing.shape[-1]
    per_half = got_a.shape[-1] // width
    for h, got in enumerate((got_a, got_b)):
        total = got[0].astype(jnp.float32)
        for j in range(1, side):
            total = total + got[j].astype(jnp.float32)
        total = total.astype(outgoing.dtype)
        for j in range(per_half):
            outgoing[h * per_half + j] = total[:, j * width:(j + 1) * width]
    local = pltpu.make_async_copy(outgoing.at[mine_e], out_ref.at[mine_e], local_sems.at[2])
    local.start()
    copies = []
    for k in range(1, n_expert):
        target = lax.rem(mine_e + k, n_expert)
        copy = pltpu.make_async_remote_copy(
            src_ref=outgoing.at[target],
            dst_ref=out_ref.at[mine_e],
            send_sem=ex_send.at[k - 1],
            recv_sem=ex_recv.at[k - 1],
            device_id={"expert": target},
            device_id_type=mesh_id,
        )
        copy.start()
        copies.append(copy)
    local.wait()
    for copy in copies:
        copy.wait()


def _down_scatter_kernel(side, hidden_ref, wd_ref, scale_ref, sum_a, sum_b,
                         send_a, send_b, got_a, got_b, send_sems, recv_sems):
    me = lax.axis_index("dp")
    mesh_id = pl.DeviceIdType.MESH
    half = send_a.shape[-1]
    rows = send_a.shape[2]
    chunk = side * rows
    my_y = lax.rem(me, side)
    my_x = lax.rem(me // side, side)
    base_y = me - my_y
    base_x = me - my_x * side
    barrier = pltpu.get_barrier_semaphore()
    for k in range(1, side):
        pl.semaphore_signal(barrier, 1, device_id={"dp": base_y + lax.rem(my_y + k, side)}, device_id_type=mesh_id)
        pl.semaphore_signal(
            barrier, 1, device_id={"dp": base_x + lax.rem(my_x + k, side) * side}, device_id_type=mesh_id
        )
    pl.semaphore_wait(barrier, 2 * (side - 1))

    def to_a(k, y):
        return pltpu.make_async_remote_copy(
            src_ref=send_a.at[y], dst_ref=got_a.at[my_y], send_sem=send_sems.at[0, k - 1],
            recv_sem=recv_sems.at[0, k - 1], device_id={"dp": base_y + y}, device_id_type=mesh_id,
        )

    def to_b(k, x):
        return pltpu.make_async_remote_copy(
            src_ref=send_b.at[x], dst_ref=got_b.at[my_x], send_sem=send_sems.at[1, k - 1],
            recv_sem=recv_sems.at[1, k - 1], device_id={"dp": base_x + x * side}, device_id_type=mesh_id,
        )

    sends = []
    for k in list(range(1, side)) + [0]:
        x = lax.rem(my_x + k, side)
        at = pl.ds(pl.multiple_of(x * chunk, chunk), chunk)
        part = jnp.dot(hidden_ref[at], wd_ref[...], preferred_element_type=jnp.float32)
        part = (part * scale_ref[at]).astype(send_a.dtype)
        for y in range(side):
            send_a[y, x] = part[y * rows:(y + 1) * rows, :half]
            send_b[x, y] = part[y * rows:(y + 1) * rows, half:]
        if k:
            copy = to_b(k, x)
            copy.start()
            sends.append(copy)
    for k in range(1, side):
        copy = to_a(k, lax.rem(my_y + k, side))
        copy.start()
        sends.append(copy)
    for k in range(1, side):
        to_a(k, lax.rem(my_y + side - k, side)).wait_recv()
        to_b(k, lax.rem(my_x + side - k, side)).wait_recv()
    for x in range(side):
        total = send_a[my_y, x].astype(jnp.float32)
        for k in range(1, side):
            total = total + got_a[lax.rem(my_y + side - k, side), x].astype(jnp.float32)
        sum_a[x] = total.astype(sum_a.dtype)
    for y in range(side):
        total = send_b[my_x, y].astype(jnp.float32)
        for k in range(1, side):
            total = total + got_b[lax.rem(my_x + side - k, side), y].astype(jnp.float32)
        sum_b[y] = total.astype(sum_b.dtype)
    for copy in sends:
        copy.wait_send()


def down_scatter(hidden, w_down, scale, cid):
    side = 4
    rows = hidden.shape[0] // (side * side)
    half = w_down.shape[1] // 2
    slab = (side, side, rows, half)
    vmem = pl.BlockSpec(memory_space=pltpu.VMEM)
    return pl.pallas_call(
        functools.partial(_down_scatter_kernel, side),
        out_shape=[jax.ShapeDtypeStruct((side, rows, half), jnp.bfloat16)] * 2,
        in_specs=[vmem] * 3,
        out_specs=[vmem] * 2,
        scratch_shapes=[
            pltpu.VMEM(slab, jnp.bfloat16),
            pltpu.VMEM(slab, jnp.bfloat16),
            pltpu.VMEM(slab, jnp.bfloat16),
            pltpu.VMEM(slab, jnp.bfloat16),
            pltpu.SemaphoreType.DMA((2, side - 1)),
            pltpu.SemaphoreType.DMA((2, side - 1)),
        ],
        compiler_params=pltpu.CompilerParams(collective_id=cid, has_side_effects=True),
    )(hidden, w_down, scale)


def reduce_scatter_2d(part, cid):
    side = 4
    n_expert = lax.axis_size("expert")
    second_a, second_b = part
    rows = second_a.shape[1]
    cols = 2 * second_a.shape[2]
    width = cols // n_expert
    return pl.pallas_call(
        functools.partial(_finish_kernel, side, n_expert),
        out_shape=jax.ShapeDtypeStruct((n_expert, rows, width), second_a.dtype),
        in_specs=[pl.BlockSpec(memory_space=pl.ANY)] * 2,
        out_specs=pl.BlockSpec(memory_space=pl.ANY),
        scratch_shapes=[
            pltpu.VMEM(second_a.shape, second_a.dtype),
            pltpu.VMEM(second_b.shape, second_b.dtype),
            pltpu.VMEM((n_expert, rows, width), second_a.dtype),
            pltpu.SemaphoreType.DMA((3,)),
            pltpu.SemaphoreType.DMA((2, side - 1)),
            pltpu.SemaphoreType.DMA((2, side - 1)),
            pltpu.SemaphoreType.DMA((n_expert - 1,)),
            pltpu.SemaphoreType.DMA((n_expert - 1,)),
        ],
        compiler_params=pltpu.CompilerParams(collective_id=cid, has_side_effects=True),
    )(second_a, second_b)


def all_gather_2d(x, cid):
    side = 4
    half = x.shape[-1] // 2
    got_a, got_b = dp_route([x, x], (1, side), cid, gather=True, windows=((0, half), (half, half)))
    got_a, got_b = dp_route([got_a, got_b], (side, 1), cid + 1, gather=True)
    n = side * side
    got_a = got_a.reshape((n,) + got_a.shape[2:])
    perm = (1, 0) + tuple(range(2, got_b.ndim))
    got_b = got_b.transpose(perm).reshape((n,) + got_b.shape[2:])
    return got_a, got_b


def _gather_gate_kernel(side, a_ref, b_ref, wg_ref, wu_ref, hidden_ref,
                        got_a, got_b, acc_g, acc_u, local_sems, send_sems, recv_sems):
    me = lax.axis_index("dp")
    mesh_id = pl.DeviceIdType.MESH
    half = a_ref.shape[-1]
    group = got_a.shape[1] * got_a.shape[2]
    rows = got_a.shape[2]
    routes = ((a_ref, got_a, side), (b_ref, got_b, 1))
    geo = []
    for _, _, stride in routes:
        coord = lax.rem(me // stride, side)
        geo.append((coord, me - coord * stride))
    barrier = pltpu.get_barrier_semaphore()
    for (coord, base), (_, _, stride) in zip(geo, routes):
        for k in range(1, side):
            peer = base + lax.rem(coord + k, side) * stride
            pl.semaphore_signal(barrier, 1, device_id={"dp": peer}, device_id_type=mesh_id)
    pl.semaphore_wait(barrier, 2 * (side - 1))

    def remote(r, k, source, to):
        src, dst, stride = routes[r]
        coord, base = geo[r]
        return pltpu.make_async_remote_copy(
            src_ref=src,
            dst_ref=dst.at[source],
            send_sem=send_sems.at[r, k - 1],
            recv_sem=recv_sems.at[r, k - 1],
            device_id={"dp": base + to * stride},
            device_id_type=mesh_id,
        )

    locals_, sends = [], []
    for r, (src, dst, stride) in enumerate(routes):
        coord, base = geo[r]
        local = pltpu.make_async_copy(src, dst.at[coord], local_sems.at[r])
        local.start()
        locals_.append(local)
        for k in range(1, side):
            copy = remote(r, k, coord, lax.rem(coord + k, side))
            copy.start()
            sends.append(copy)
    acc_g[...] = jnp.zeros_like(acc_g)
    acc_u[...] = jnp.zeros_like(acc_u)

    def add_a(source):
        block = got_a[source].reshape(group, half)
        at = pl.ds(pl.multiple_of(source * group, group), group)
        acc_g[at] += jnp.dot(block, wg_ref[:half], preferred_element_type=jnp.float32)
        acc_u[at] += jnp.dot(block, wu_ref[:half], preferred_element_type=jnp.float32)

    def add_b(source):
        block = got_b[source].reshape(group, half)
        g = jnp.dot(block, wg_ref[half:], preferred_element_type=jnp.float32)
        u = jnp.dot(block, wu_ref[half:], preferred_element_type=jnp.float32)
        for x in range(side):
            at = pl.ds(pl.multiple_of((x * side + source) * rows, rows), rows)
            acc_g[at] += g[x * rows:(x + 1) * rows]
            acc_u[at] += u[x * rows:(x + 1) * rows]

    for local in locals_:
        local.wait()
    add_a(geo[0][0])
    add_b(geo[1][0])
    for k in range(1, side):
        for r, add in ((0, add_a), (1, add_b)):
            coord, _ = geo[r]
            source = lax.rem(coord + side - k, side)
            remote(r, k, source, source).wait_recv()
            add(source)
    g = acc_g[...]
    hidden_ref[...] = (g / (1.0 + jnp.exp(-g)) * acc_u[...]).astype(hidden_ref.dtype)
    for copy in sends:
        copy.wait_send()


def gather_gate(x, w_gate, w_up, cid):
    side = 4
    n = side * side
    half = x.shape[-1] // 2
    first_a, first_b = dp_route([x, x], (1, side), cid, gather=True, windows=((0, half), (half, half)))
    return pl.pallas_call(
        functools.partial(_gather_gate_kernel, side),
        out_shape=jax.ShapeDtypeStruct((n * x.shape[0], w_gate.shape[1]), jnp.bfloat16),
        in_specs=[pl.BlockSpec(memory_space=pl.ANY)] * 2 + [pl.BlockSpec(memory_space=pltpu.VMEM)] * 2,
        out_specs=pl.BlockSpec(memory_space=pltpu.VMEM),
        scratch_shapes=[
            pltpu.VMEM((side,) + first_a.shape, first_a.dtype),
            pltpu.VMEM((side,) + first_b.shape, first_b.dtype),
            pltpu.VMEM((n * x.shape[0], w_gate.shape[1]), jnp.float32),
            pltpu.VMEM((n * x.shape[0], w_gate.shape[1]), jnp.float32),
            pltpu.SemaphoreType.DMA((2,)),
            pltpu.SemaphoreType.DMA((2, side - 1)),
            pltpu.SemaphoreType.DMA((2, side - 1)),
        ],
        compiler_params=pltpu.CompilerParams(collective_id=cid + 1, has_side_effects=True),
    )(first_a, first_b, w_gate, w_up)


def _gather_attend_kernel(side, a_ref, b_ref, ctx_ref, res_ref, out_ref,
                          got_a, got_b, acc_a, acc_b, local_sems, send_sems, recv_sems):
    me = lax.axis_index("dp")
    mesh_id = pl.DeviceIdType.MESH
    rows = got_a.shape[2]
    bundle = side * rows
    routes = ((a_ref, got_a, side), (b_ref, got_b, 1))
    geo = []
    for _, _, stride in routes:
        coord = lax.rem(me // stride, side)
        geo.append((coord, me - coord * stride))
    barrier = pltpu.get_barrier_semaphore()
    for (coord, base), (_, _, stride) in zip(geo, routes):
        for k in range(1, side):
            peer = base + lax.rem(coord + k, side) * stride
            pl.semaphore_signal(barrier, 1, device_id={"dp": peer}, device_id_type=mesh_id)
    pl.semaphore_wait(barrier, 2 * (side - 1))

    def remote(r, k, source, to):
        src, dst, stride = routes[r]
        coord, base = geo[r]
        return pltpu.make_async_remote_copy(
            src_ref=src,
            dst_ref=dst.at[source],
            send_sem=send_sems.at[r, k - 1],
            recv_sem=recv_sems.at[r, k - 1],
            device_id={"dp": base + to * stride},
            device_id_type=mesh_id,
        )

    locals_, sends = [], []
    for r, (src, dst, stride) in enumerate(routes):
        coord, base = geo[r]
        local = pltpu.make_async_copy(src, dst.at[coord], local_sems.at[r])
        local.start()
        locals_.append(local)
        for k in range(1, side):
            copy = remote(r, k, coord, lax.rem(coord + k, side))
            copy.start()
            sends.append(copy)
    acc_a[...] = jnp.zeros_like(acc_a)
    acc_b[...] = jnp.zeros_like(acc_b)

    def add_a(source):
        block = got_a[source].reshape(bundle, got_a.shape[-1])
        at = pl.ds(pl.multiple_of(source * bundle, bundle), bundle)
        acc_a[...] += jnp.dot(ctx_ref[:, at], block, preferred_element_type=jnp.float32)

    def add_b(source):
        for x in range(side):
            at = pl.ds(pl.multiple_of((x * side + source) * rows, rows), rows)
            acc_b[...] += jnp.dot(ctx_ref[:, at], got_b[source, x], preferred_element_type=jnp.float32)

    for local in locals_:
        local.wait()
    add_a(geo[0][0])
    add_b(geo[1][0])
    for k in range(1, side):
        for r, add in ((0, add_a), (1, add_b)):
            coord, _ = geo[r]
            source = lax.rem(coord + side - k, side)
            remote(r, k, source, source).wait_recv()
            add(source)
    half = acc_a.shape[1]
    n_pieces, n_local, piece = out_ref.shape[:3]
    for b in range(n_local):
        for k in range(n_pieces):
            at = b * n_pieces * piece + k * piece
            out_ref[k, b, :, :half] = (
                res_ref[at:at + piece, :half].astype(jnp.float32) + acc_a[at:at + piece]
            ).astype(out_ref.dtype)
            out_ref[k, b, :, half:] = (
                res_ref[at:at + piece, half:].astype(jnp.float32) + acc_b[at:at + piece]
            ).astype(out_ref.dtype)
    for copy in sends:
        copy.wait_send()


def gather_attend(w, context, residual, cid, layout):
    side = 4
    half = w.shape[-1] // 2
    first_a, first_b = dp_route([w, w], (1, side), cid, gather=True, windows=((0, half), (half, half)))
    vmem = pl.BlockSpec(memory_space=pltpu.VMEM)
    return pl.pallas_call(
        functools.partial(_gather_attend_kernel, side),
        out_shape=jax.ShapeDtypeStruct(layout, jnp.bfloat16),
        in_specs=[pl.BlockSpec(memory_space=pl.ANY)] * 2 + [vmem] * 2,
        out_specs=vmem,
        scratch_shapes=[
            pltpu.VMEM((side,) + first_a.shape, first_a.dtype),
            pltpu.VMEM((side,) + first_b.shape, first_b.dtype),
            pltpu.VMEM((context.shape[0], half), jnp.float32),
            pltpu.VMEM((context.shape[0], half), jnp.float32),
            pltpu.SemaphoreType.DMA((2,)),
            pltpu.SemaphoreType.DMA((2, side - 1)),
            pltpu.SemaphoreType.DMA((2, side - 1)),
        ],
        compiler_params=pltpu.CompilerParams(collective_id=cid + 1, has_side_effects=True),
    )(first_a, first_b, context, residual)


def _spread_kernel(n_dp, n_expert, chosen_ref, split_ref, pieces_ref, mine_ref,
                   held, outgoing, local_sems, dp_send, dp_recv, ex_send, ex_recv):
    me = lax.axis_index("dp")
    mine_e = lax.axis_index("expert")
    mesh_id = pl.DeviceIdType.MESH
    group = split_ref.shape[1]
    barrier = pltpu.get_barrier_semaphore()
    for k in range(1, n_dp):
        pl.semaphore_signal(barrier, 1, device_id={"dp": lax.rem(me + k, n_dp)}, device_id_type=mesh_id)
    for k in range(1, n_expert):
        pl.semaphore_signal(
            barrier, 1, device_id={"expert": lax.rem(mine_e + k, n_expert)}, device_id_type=mesh_id
        )
    pl.semaphore_wait(barrier, n_dp + n_expert - 2)

    def at_source(src):
        return held.at[pl.ds(pl.multiple_of(src * group, group), group)]

    local = pltpu.make_async_copy(split_ref.at[me], at_source(me), local_sems.at[0])
    local.start()
    copies = []
    for k in range(1, n_dp):
        target = lax.rem(me + k, n_dp)
        copy = pltpu.make_async_remote_copy(
            src_ref=split_ref.at[target],
            dst_ref=at_source(me),
            send_sem=dp_send.at[k - 1],
            recv_sem=dp_recv.at[k - 1],
            device_id={"dp": target},
            device_id_type=mesh_id,
        )
        copy.start()
        copies.append(copy)
    local.wait()
    for copy in copies:
        copy.wait()
    keep = pltpu.make_async_copy(held, pieces_ref, local_sems.at[1])
    keep.start()
    rows = held.shape[1]
    width = held.shape[2]
    for e in range(n_expert):
        for s in range(CAP):
            outgoing[e, s * rows:(s + 1) * rows] = held[chosen_ref[e * CAP + s]]
    columns = pl.ds(pl.multiple_of(mine_e * width, width), width)
    local = pltpu.make_async_copy(outgoing.at[mine_e], mine_ref.at[:, columns], local_sems.at[2])
    local.start()
    copies = []
    for k in range(1, n_expert):
        target = lax.rem(mine_e + k, n_expert)
        copy = pltpu.make_async_remote_copy(
            src_ref=outgoing.at[target],
            dst_ref=mine_ref.at[:, columns],
            send_sem=ex_send.at[k - 1],
            recv_sem=ex_recv.at[k - 1],
            device_id={"expert": target},
            device_id_type=mesh_id,
        )
        copy.start()
        copies.append(copy)
    local.wait()
    for copy in copies:
        copy.wait()
    keep.wait()


def spread_select(chosen, split, cid):
    n_dp = lax.axis_size("dp")
    n_expert = lax.axis_size("expert")
    _, group, rows, width = split.shape
    n_blocks = n_dp * group
    return pl.pallas_call(
        functools.partial(_spread_kernel, n_dp, n_expert),
        out_shape=[
            jax.ShapeDtypeStruct((n_blocks, rows, width), split.dtype),
            jax.ShapeDtypeStruct((CAP * rows, n_expert * width), split.dtype),
        ],
        in_specs=[pl.BlockSpec(memory_space=pltpu.SMEM), pl.BlockSpec(memory_space=pl.ANY)],
        out_specs=[pl.BlockSpec(memory_space=pl.ANY)] * 2,
        scratch_shapes=[
            pltpu.VMEM((n_blocks, rows, width), split.dtype),
            pltpu.VMEM((n_expert, CAP * rows, width), split.dtype),
            pltpu.SemaphoreType.DMA((3,)),
            pltpu.SemaphoreType.DMA((n_dp - 1,)),
            pltpu.SemaphoreType.DMA((n_dp - 1,)),
            pltpu.SemaphoreType.DMA((n_expert - 1,)),
            pltpu.SemaphoreType.DMA((n_expert - 1,)),
        ],
        compiler_params=pltpu.CompilerParams(collective_id=cid, has_side_effects=True),
    )(chosen, split)


def body(
    context,
    out_weight,
    residual,
    gate_weight,
    up_weight,
    down_weight,
    gate_values,
    chosen_blocks,
    block_counts,
):
    n_dp = lax.axis_size("dp")
    n_expert = lax.axis_size("expert")
    local_tokens = context.shape[0]
    local_width = residual.shape[1]
    model_width = context.shape[1]
    local_blocks = local_tokens // BLK
    n_blocks = local_blocks * n_dp
    piece = BLK // n_dp
    my_expert = lax.axis_index("expert")

    split = gather_attend(
        out_weight, context, residual, cid=10, layout=(n_dp, local_blocks, BLK // n_dp, local_width)
    )

    pieces, mine = spread_select(chosen_blocks.reshape(-1), split, cid=0)
    w_gate = gate_weight[0]
    w_up = up_weight[0]
    w_down = down_weight[0]
    gate_row = gate_values[0]
    my_count = jnp.sum(jnp.where(jnp.arange(n_expert) == my_expert, block_counts, 0))
    row_slot = (jnp.arange(CAP * BLK) // piece) % CAP
    gate_perm = gate_row.reshape(CAP, n_dp, piece).transpose(1, 0, 2).reshape(-1)
    scale = jnp.where(row_slot < my_count, gate_perm, jnp.zeros_like(gate_perm))

    hidden = gather_gate(mine, w_gate, w_up, cid=20)
    halves = down_scatter(hidden, w_down, scale[:, None], cid=1)

    outs = reduce_scatter_2d(halves, cid=2)
    outs = outs.reshape(n_expert * CAP, piece * local_width)

    selector = chosen_blocks.reshape(-1)[None, :] == jnp.arange(n_blocks)[:, None]
    added = jnp.dot(selector.astype(jnp.bfloat16), outs, preferred_element_type=jnp.float32)
    mixed = pieces.reshape(n_blocks, piece * local_width).astype(jnp.float32) + added
    mixed = mixed.astype(jnp.bfloat16).reshape(n_dp, local_blocks, piece, local_width)
    back = dp_exchange(mixed, gather=False, cid=3)
    return back.transpose(1, 0, 2, 3).reshape(local_tokens, local_width)


def solution(mesh):
    in_specs = (
        P("dp", None),
        P("dp", "expert"),
        P("dp", "expert"),
        P("expert", None, "dp"),
        P("expert", None, "dp"),
        P("expert", "dp", None),
        P("expert", None),
        P(),
        P(),
    )
    out_specs = P("dp", "expert")
    return jax.shard_map(body, mesh=mesh, in_specs=in_specs, out_specs=out_specs, check_vma=False)
```

```python
import functools

import jax
import jax.numpy as jnp
from jax import lax
from jax.sharding import PartitionSpec as P
from jax.experimental import pallas as pl
from jax.experimental.pallas import tpu as pltpu

BLK = 128
CAP = 4


def _exchange_kernel(n, gather, axis, x_ref, o_ref, local_sem, send_sems, recv_sems):
    me = lax.axis_index(axis)
    mesh_id = pl.DeviceIdType.MESH
    barrier = pltpu.get_barrier_semaphore()
    for k in range(1, n):
        pl.semaphore_signal(barrier, 1, device_id={axis: lax.rem(me + k, n)}, device_id_type=mesh_id)
    pl.semaphore_wait(barrier, n - 1)
    local = pltpu.make_async_copy(x_ref if gather else x_ref.at[me], o_ref.at[me], local_sem)
    local.start()
    copies = []
    for k in range(1, n):
        target = lax.rem(me + k, n)
        copy = pltpu.make_async_remote_copy(
            src_ref=x_ref if gather else x_ref.at[target],
            dst_ref=o_ref.at[me],
            send_sem=send_sems.at[k - 1],
            recv_sem=recv_sems.at[k - 1],
            device_id={axis: target},
            device_id_type=mesh_id,
        )
        copy.start()
        copies.append(copy)
    local.wait()
    for copy in copies:
        copy.wait()


def dp_exchange(x, gather, cid, axis="dp"):
    n = lax.axis_size(axis)
    shape = (n,) + x.shape if gather else x.shape
    return pl.pallas_call(
        functools.partial(_exchange_kernel, n, gather, axis),
        out_shape=jax.ShapeDtypeStruct(shape, x.dtype),
        in_specs=[pl.BlockSpec(memory_space=pl.ANY)],
        out_specs=pl.BlockSpec(memory_space=pl.ANY),
        scratch_shapes=[
            pltpu.SemaphoreType.DMA(()),
            pltpu.SemaphoreType.DMA((n - 1,)),
            pltpu.SemaphoreType.DMA((n - 1,)),
        ],
        compiler_params=pltpu.CompilerParams(collective_id=cid, has_side_effects=True),
    )(x)


def _route_kernel(strides, side, gather, windows, *refs):
    n_in = len(strides)
    ins, outs = refs[:n_in], refs[n_in:2 * n_in]
    local_sems, send_sems, recv_sems = refs[2 * n_in:]
    me = lax.axis_index("dp")
    mesh_id = pl.DeviceIdType.MESH

    def window(r):
        if windows is None:
            return ins[r]
        start, size = windows[r]
        return ins[r].at[:, pl.ds(start, size)]

    routes = []
    for r, stride in enumerate(strides):
        coord = lax.rem(me // stride, side)
        base = me - coord * stride
        for k in range(1, side):
            to = lax.rem(coord + k, side)
            routes.append((r, coord, to, base + to * stride))
    barrier = pltpu.get_barrier_semaphore()
    for _, _, _, target in routes:
        pl.semaphore_signal(barrier, 1, device_id={"dp": target}, device_id_type=mesh_id)
    pl.semaphore_wait(barrier, len(routes))
    locals_ = []
    for r in range(n_in):
        coord = lax.rem(me // strides[r], side)
        source = window(r) if gather else ins[r].at[coord]
        local = pltpu.make_async_copy(source, outs[r].at[coord], local_sems.at[r])
        local.start()
        locals_.append(local)
    copies = []
    for i, (r, coord, to, target) in enumerate(routes):
        copy = pltpu.make_async_remote_copy(
            src_ref=window(r) if gather else ins[r].at[to],
            dst_ref=outs[r].at[coord],
            send_sem=send_sems.at[i],
            recv_sem=recv_sems.at[i],
            device_id={"dp": target},
            device_id_type=mesh_id,
        )
        copy.start()
        copies.append(copy)
    for local in locals_:
        local.wait()
    for copy in copies:
        copy.wait()


def dp_route(xs, strides, cid, side=4, gather=False, windows=None):
    n_routes = len(strides) * (side - 1)
    if windows is not None:
        shapes = [(side, x.shape[0], size) for x, (_, size) in zip(xs, windows)]
    else:
        shapes = [((side,) + x.shape) if gather else x.shape for x in xs]
    return pl.pallas_call(
        functools.partial(_route_kernel, tuple(strides), side, gather, windows),
        out_shape=[jax.ShapeDtypeStruct(s, x.dtype) for s, x in zip(shapes, xs)],
        in_specs=[pl.BlockSpec(memory_space=pl.ANY)] * len(xs),
        out_specs=[pl.BlockSpec(memory_space=pl.ANY)] * len(xs),
        scratch_shapes=[
            pltpu.SemaphoreType.DMA((len(xs),)),
            pltpu.SemaphoreType.DMA((n_routes,)),
            pltpu.SemaphoreType.DMA((n_routes,)),
        ],
        compiler_params=pltpu.CompilerParams(collective_id=cid, has_side_effects=True),
    )(*xs)


def _finish_kernel(side, n_expert, a_ref, b_ref, out_ref, got_a, got_b, outgoing,
                   local_sems, send_sems, recv_sems, ex_send, ex_recv):
    me = lax.axis_index("dp")
    mine_e = lax.axis_index("expert")
    mesh_id = pl.DeviceIdType.MESH
    routes = ((a_ref, got_a, side), (b_ref, got_b, 1))
    barrier = pltpu.get_barrier_semaphore()
    for _, _, stride in routes:
        coord = lax.rem(me // stride, side)
        base = me - coord * stride
        for k in range(1, side):
            peer = base + lax.rem(coord + k, side) * stride
            pl.semaphore_signal(barrier, 1, device_id={"dp": peer}, device_id_type=mesh_id)
    for k in range(1, n_expert):
        pl.semaphore_signal(
            barrier, 1, device_id={"expert": lax.rem(mine_e + k, n_expert)}, device_id_type=mesh_id
        )
    pl.semaphore_wait(barrier, 2 * (side - 1) + n_expert - 1)
    locals_, copies = [], []
    for r, (src, dst, stride) in enumerate(routes):
        coord = lax.rem(me // stride, side)
        base = me - coord * stride
        local = pltpu.make_async_copy(src.at[coord], dst.at[coord], local_sems.at[r])
        local.start()
        locals_.append(local)
        for k in range(1, side):
            to = lax.rem(coord + k, side)
            copy = pltpu.make_async_remote_copy(
                src_ref=src.at[to],
                dst_ref=dst.at[coord],
                send_sem=send_sems.at[r, k - 1],
                recv_sem=recv_sems.at[r, k - 1],
                device_id={"dp": base + to * stride},
                device_id_type=mesh_id,
            )
            copy.start()
            copies.append(copy)
    for local in locals_:
        local.wait()
    for copy in copies:
        copy.wait()
    width = outgoing.shape[-1]
    per_half = got_a.shape[-1] // width
    for h, got in enumerate((got_a, got_b)):
        total = got[0].astype(jnp.float32)
        for j in range(1, side):
            total = total + got[j].astype(jnp.float32)
        total = total.astype(outgoing.dtype)
        for j in range(per_half):
            outgoing[h * per_half + j] = total[:, j * width:(j + 1) * width]
    local = pltpu.make_async_copy(outgoing.at[mine_e], out_ref.at[mine_e], local_sems.at[2])
    local.start()
    copies = []
    for k in range(1, n_expert):
        target = lax.rem(mine_e + k, n_expert)
        copy = pltpu.make_async_remote_copy(
            src_ref=outgoing.at[target],
            dst_ref=out_ref.at[mine_e],
            send_sem=ex_send.at[k - 1],
            recv_sem=ex_recv.at[k - 1],
            device_id={"expert": target},
            device_id_type=mesh_id,
        )
        copy.start()
        copies.append(copy)
    local.wait()
    for copy in copies:
        copy.wait()


def _down_scatter_kernel(side, hidden_ref, wd_ref, scale_ref, sum_a, sum_b,
                         send_a, send_b, got_a, got_b, send_sems, recv_sems):
    me = lax.axis_index("dp")
    mesh_id = pl.DeviceIdType.MESH
    half = send_a.shape[-1]
    rows = send_a.shape[2]
    chunk = side * rows
    my_y = lax.rem(me, side)
    my_x = lax.rem(me // side, side)
    base_y = me - my_y
    base_x = me - my_x * side
    barrier = pltpu.get_barrier_semaphore()
    for k in range(1, side):
        pl.semaphore_signal(barrier, 1, device_id={"dp": base_y + lax.rem(my_y + k, side)}, device_id_type=mesh_id)
        pl.semaphore_signal(
            barrier, 1, device_id={"dp": base_x + lax.rem(my_x + k, side) * side}, device_id_type=mesh_id
        )
    pl.semaphore_wait(barrier, 2 * (side - 1))

    def to_a(k, y):
        return pltpu.make_async_remote_copy(
            src_ref=send_a.at[y], dst_ref=got_a.at[my_y], send_sem=send_sems.at[0, k - 1],
            recv_sem=recv_sems.at[0, k - 1], device_id={"dp": base_y + y}, device_id_type=mesh_id,
        )

    def to_b(k, x):
        return pltpu.make_async_remote_copy(
            src_ref=send_b.at[x], dst_ref=got_b.at[my_x], send_sem=send_sems.at[1, k - 1],
            recv_sem=recv_sems.at[1, k - 1], device_id={"dp": base_x + x * side}, device_id_type=mesh_id,
        )

    sends = []
    for k in list(range(1, side)) + [0]:
        x = lax.rem(my_x + k, side)
        at = pl.ds(pl.multiple_of(x * chunk, chunk), chunk)
        part = jnp.dot(hidden_ref[at], wd_ref[...], preferred_element_type=jnp.float32)
        part = (part * scale_ref[at]).astype(send_a.dtype)
        for y in range(side):
            send_a[y, x] = part[y * rows:(y + 1) * rows, :half]
            send_b[x, y] = part[y * rows:(y + 1) * rows, half:]
        if k:
            copy = to_b(k, x)
            copy.start()
            sends.append(copy)
    for k in range(1, side):
        copy = to_a(k, lax.rem(my_y + k, side))
        copy.start()
        sends.append(copy)
    for k in range(1, side):
        to_a(k, lax.rem(my_y + side - k, side)).wait_recv()
        to_b(k, lax.rem(my_x + side - k, side)).wait_recv()
    for x in range(side):
        total = send_a[my_y, x].astype(jnp.float32)
        for k in range(1, side):
            total = total + got_a[lax.rem(my_y + side - k, side), x].astype(jnp.float32)
        sum_a[x] = total.astype(sum_a.dtype)
    for y in range(side):
        total = send_b[my_x, y].astype(jnp.float32)
        for k in range(1, side):
            total = total + got_b[lax.rem(my_x + side - k, side), y].astype(jnp.float32)
        sum_b[y] = total.astype(sum_b.dtype)
    for copy in sends:
        copy.wait_send()


def down_scatter(hidden, w_down, scale, cid):
    side = 4
    rows = hidden.shape[0] // (side * side)
    half = w_down.shape[1] // 2
    slab = (side, side, rows, half)
    vmem = pl.BlockSpec(memory_space=pltpu.VMEM)
    return pl.pallas_call(
        functools.partial(_down_scatter_kernel, side),
        out_shape=[jax.ShapeDtypeStruct((side, rows, half), jnp.bfloat16)] * 2,
        in_specs=[vmem] * 3,
        out_specs=[vmem] * 2,
        scratch_shapes=[
            pltpu.VMEM(slab, jnp.bfloat16),
            pltpu.VMEM(slab, jnp.bfloat16),
            pltpu.VMEM(slab, jnp.bfloat16),
            pltpu.VMEM(slab, jnp.bfloat16),
            pltpu.SemaphoreType.DMA((2, side - 1)),
            pltpu.SemaphoreType.DMA((2, side - 1)),
        ],
        compiler_params=pltpu.CompilerParams(collective_id=cid, has_side_effects=True),
    )(hidden, w_down, scale)


def reduce_scatter_2d(part, cid):
    side = 4
    n_expert = lax.axis_size("expert")
    second_a, second_b = part
    rows = second_a.shape[1]
    cols = 2 * second_a.shape[2]
    width = cols // n_expert
    return pl.pallas_call(
        functools.partial(_finish_kernel, side, n_expert),
        out_shape=jax.ShapeDtypeStruct((n_expert, rows, width), second_a.dtype),
        in_specs=[pl.BlockSpec(memory_space=pl.ANY)] * 2,
        out_specs=pl.BlockSpec(memory_space=pl.ANY),
        scratch_shapes=[
            pltpu.VMEM(second_a.shape, second_a.dtype),
            pltpu.VMEM(second_b.shape, second_b.dtype),
            pltpu.VMEM((n_expert, rows, width), second_a.dtype),
            pltpu.SemaphoreType.DMA((3,)),
            pltpu.SemaphoreType.DMA((2, side - 1)),
            pltpu.SemaphoreType.DMA((2, side - 1)),
            pltpu.SemaphoreType.DMA((n_expert - 1,)),
            pltpu.SemaphoreType.DMA((n_expert - 1,)),
        ],
        compiler_params=pltpu.CompilerParams(collective_id=cid, has_side_effects=True),
    )(second_a, second_b)


def all_gather_2d(x, cid):
    side = 4
    half = x.shape[-1] // 2
    got_a, got_b = dp_route([x, x], (1, side), cid, gather=True, windows=((0, half), (half, half)))
    got_a, got_b = dp_route([got_a, got_b], (side, 1), cid + 1, gather=True)
    n = side * side
    got_a = got_a.reshape((n,) + got_a.shape[2:])
    perm = (1, 0) + tuple(range(2, got_b.ndim))
    got_b = got_b.transpose(perm).reshape((n,) + got_b.shape[2:])
    return got_a, got_b


def _gather_gate_kernel(side, a_ref, b_ref, wg_ref, wu_ref, hidden_ref,
                        got_a, got_b, acc_g, acc_u, local_sems, send_sems, recv_sems):
    me = lax.axis_index("dp")
    mesh_id = pl.DeviceIdType.MESH
    half = a_ref.shape[-1]
    group = got_a.shape[1] * got_a.shape[2]
    rows = got_a.shape[2]
    routes = ((a_ref, got_a, side), (b_ref, got_b, 1))
    geo = []
    for _, _, stride in routes:
        coord = lax.rem(me // stride, side)
        geo.append((coord, me - coord * stride))
    barrier = pltpu.get_barrier_semaphore()
    for (coord, base), (_, _, stride) in zip(geo, routes):
        for k in range(1, side):
            peer = base + lax.rem(coord + k, side) * stride
            pl.semaphore_signal(barrier, 1, device_id={"dp": peer}, device_id_type=mesh_id)
    pl.semaphore_wait(barrier, 2 * (side - 1))

    def remote(r, k, source, to):
        src, dst, stride = routes[r]
        coord, base = geo[r]
        return pltpu.make_async_remote_copy(
            src_ref=src,
            dst_ref=dst.at[source],
            send_sem=send_sems.at[r, k - 1],
            recv_sem=recv_sems.at[r, k - 1],
            device_id={"dp": base + to * stride},
            device_id_type=mesh_id,
        )

    locals_, sends = [], []
    for r, (src, dst, stride) in enumerate(routes):
        coord, base = geo[r]
        local = pltpu.make_async_copy(src, dst.at[coord], local_sems.at[r])
        local.start()
        locals_.append(local)
        for k in range(1, side):
            copy = remote(r, k, coord, lax.rem(coord + k, side))
            copy.start()
            sends.append(copy)
    acc_g[...] = jnp.zeros_like(acc_g)
    acc_u[...] = jnp.zeros_like(acc_u)

    def add_a(source):
        block = got_a[source].reshape(group, half)
        at = pl.ds(pl.multiple_of(source * group, group), group)
        acc_g[at] += jnp.dot(block, wg_ref[:half], preferred_element_type=jnp.float32)
        acc_u[at] += jnp.dot(block, wu_ref[:half], preferred_element_type=jnp.float32)

    def add_b(source):
        block = got_b[source].reshape(group, half)
        g = jnp.dot(block, wg_ref[half:], preferred_element_type=jnp.float32)
        u = jnp.dot(block, wu_ref[half:], preferred_element_type=jnp.float32)
        for x in range(side):
            at = pl.ds(pl.multiple_of((x * side + source) * rows, rows), rows)
            acc_g[at] += g[x * rows:(x + 1) * rows]
            acc_u[at] += u[x * rows:(x + 1) * rows]

    for local in locals_:
        local.wait()
    add_a(geo[0][0])
    add_b(geo[1][0])
    for k in range(1, side):
        for r, add in ((0, add_a), (1, add_b)):
            coord, _ = geo[r]
            source = lax.rem(coord + side - k, side)
            remote(r, k, source, source).wait_recv()
            add(source)
    g = acc_g[...]
    hidden_ref[...] = (g / (1.0 + jnp.exp(-g)) * acc_u[...]).astype(hidden_ref.dtype)
    for copy in sends:
        copy.wait_send()


def gather_gate(x, w_gate, w_up, cid):
    side = 4
    n = side * side
    half = x.shape[-1] // 2
    first_a, first_b = dp_route([x, x], (1, side), cid, gather=True, windows=((0, half), (half, half)))
    return pl.pallas_call(
        functools.partial(_gather_gate_kernel, side),
        out_shape=jax.ShapeDtypeStruct((n * x.shape[0], w_gate.shape[1]), jnp.bfloat16),
        in_specs=[pl.BlockSpec(memory_space=pl.ANY)] * 2 + [pl.BlockSpec(memory_space=pltpu.VMEM)] * 2,
        out_specs=pl.BlockSpec(memory_space=pltpu.VMEM),
        scratch_shapes=[
            pltpu.VMEM((side,) + first_a.shape, first_a.dtype),
            pltpu.VMEM((side,) + first_b.shape, first_b.dtype),
            pltpu.VMEM((n * x.shape[0], w_gate.shape[1]), jnp.float32),
            pltpu.VMEM((n * x.shape[0], w_gate.shape[1]), jnp.float32),
            pltpu.SemaphoreType.DMA((2,)),
            pltpu.SemaphoreType.DMA((2, side - 1)),
            pltpu.SemaphoreType.DMA((2, side - 1)),
        ],
        compiler_params=pltpu.CompilerParams(collective_id=cid + 1, has_side_effects=True),
    )(first_a, first_b, w_gate, w_up)


def _gather_attend_kernel(side, a_ref, b_ref, ctx_ref, res_ref, out_ref,
                          got_a, got_b, acc_a, acc_b, local_sems, send_sems, recv_sems):
    me = lax.axis_index("dp")
    mesh_id = pl.DeviceIdType.MESH
    rows = got_a.shape[2]
    bundle = side * rows
    routes = ((a_ref, got_a, side), (b_ref, got_b, 1))
    geo = []
    for _, _, stride in routes:
        coord = lax.rem(me // stride, side)
        geo.append((coord, me - coord * stride))
    barrier = pltpu.get_barrier_semaphore()
    for (coord, base), (_, _, stride) in zip(geo, routes):
        for k in range(1, side):
            peer = base + lax.rem(coord + k, side) * stride
            pl.semaphore_signal(barrier, 1, device_id={"dp": peer}, device_id_type=mesh_id)
    pl.semaphore_wait(barrier, 2 * (side - 1))

    def remote(r, k, source, to):
        src, dst, stride = routes[r]
        coord, base = geo[r]
        return pltpu.make_async_remote_copy(
            src_ref=src,
            dst_ref=dst.at[source],
            send_sem=send_sems.at[r, k - 1],
            recv_sem=recv_sems.at[r, k - 1],
            device_id={"dp": base + to * stride},
            device_id_type=mesh_id,
        )

    locals_, sends = [], []
    for r, (src, dst, stride) in enumerate(routes):
        coord, base = geo[r]
        local = pltpu.make_async_copy(src, dst.at[coord], local_sems.at[r])
        local.start()
        locals_.append(local)
        for k in range(1, side):
            copy = remote(r, k, coord, lax.rem(coord + k, side))
            copy.start()
            sends.append(copy)
    acc_a[...] = jnp.zeros_like(acc_a)
    acc_b[...] = jnp.zeros_like(acc_b)

    def add_a(source):
        block = got_a[source].reshape(bundle, got_a.shape[-1])
        at = pl.ds(pl.multiple_of(source * bundle, bundle), bundle)
        acc_a[...] += jnp.dot(ctx_ref[:, at], block, preferred_element_type=jnp.float32)

    def add_b(source):
        for x in range(side):
            at = pl.ds(pl.multiple_of((x * side + source) * rows, rows), rows)
            acc_b[...] += jnp.dot(ctx_ref[:, at], got_b[source, x], preferred_element_type=jnp.float32)

    for local in locals_:
        local.wait()
    add_a(geo[0][0])
    add_b(geo[1][0])
    for k in range(1, side):
        for r, add in ((0, add_a), (1, add_b)):
            coord, _ = geo[r]
            source = lax.rem(coord + side - k, side)
            remote(r, k, source, source).wait_recv()
            add(source)
    half = acc_a.shape[1]
    n_pieces, n_local, piece = out_ref.shape[:3]
    for b in range(n_local):
        for k in range(n_pieces):
            at = b * n_pieces * piece + k * piece
            out_ref[k, b, :, :half] = (
                res_ref[at:at + piece, :half].astype(jnp.float32) + acc_a[at:at + piece]
            ).astype(out_ref.dtype)
            out_ref[k, b, :, half:] = (
                res_ref[at:at + piece, half:].astype(jnp.float32) + acc_b[at:at + piece]
            ).astype(out_ref.dtype)
    for copy in sends:
        copy.wait_send()


def gather_attend(w, context, residual, cid, layout):
    side = 4
    half = w.shape[-1] // 2
    first_a, first_b = dp_route([w, w], (1, side), cid, gather=True, windows=((0, half), (half, half)))
    vmem = pl.BlockSpec(memory_space=pltpu.VMEM)
    return pl.pallas_call(
        functools.partial(_gather_attend_kernel, side),
        out_shape=jax.ShapeDtypeStruct(layout, jnp.bfloat16),
        in_specs=[pl.BlockSpec(memory_space=pl.ANY)] * 2 + [vmem] * 2,
        out_specs=vmem,
        scratch_shapes=[
            pltpu.VMEM((side,) + first_a.shape, first_a.dtype),
            pltpu.VMEM((side,) + first_b.shape, first_b.dtype),
            pltpu.VMEM((context.shape[0], half), jnp.float32),
            pltpu.VMEM((context.shape[0], half), jnp.float32),
            pltpu.SemaphoreType.DMA((2,)),
            pltpu.SemaphoreType.DMA((2, side - 1)),
            pltpu.SemaphoreType.DMA((2, side - 1)),
        ],
        compiler_params=pltpu.CompilerParams(collective_id=cid + 1, has_side_effects=True),
    )(first_a, first_b, context, residual)


def _spread_kernel(n_dp, n_expert, chosen_ref, split_ref, pieces_ref, mine_ref,
                   held, outgoing, local_sems, dp_send, dp_recv, ex_send, ex_recv):
    me = lax.axis_index("dp")
    mine_e = lax.axis_index("expert")
    mesh_id = pl.DeviceIdType.MESH
    group = split_ref.shape[1]
    barrier = pltpu.get_barrier_semaphore()
    for k in range(1, n_dp):
        pl.semaphore_signal(barrier, 1, device_id={"dp": lax.rem(me + k, n_dp)}, device_id_type=mesh_id)
    for k in range(1, n_expert):
        pl.semaphore_signal(
            barrier, 1, device_id={"expert": lax.rem(mine_e + k, n_expert)}, device_id_type=mesh_id
        )
    pl.semaphore_wait(barrier, n_dp + n_expert - 2)

    def at_source(src):
        return held.at[pl.ds(pl.multiple_of(src * group, group), group)]

    local = pltpu.make_async_copy(split_ref.at[me], at_source(me), local_sems.at[0])
    local.start()
    copies = []
    for k in range(1, n_dp):
        target = lax.rem(me + k, n_dp)
        copy = pltpu.make_async_remote_copy(
            src_ref=split_ref.at[target],
            dst_ref=at_source(me),
            send_sem=dp_send.at[k - 1],
            recv_sem=dp_recv.at[k - 1],
            device_id={"dp": target},
            device_id_type=mesh_id,
        )
        copy.start()
        copies.append(copy)
    local.wait()
    for copy in copies:
        copy.wait()
    keep = pltpu.make_async_copy(held, pieces_ref, local_sems.at[1])
    keep.start()
    rows = held.shape[1]
    width = held.shape[2]
    for e in range(n_expert):
        for s in range(CAP):
            outgoing[e, s * rows:(s + 1) * rows] = held[chosen_ref[e * CAP + s]]
    columns = pl.ds(pl.multiple_of(mine_e * width, width), width)
    local = pltpu.make_async_copy(outgoing.at[mine_e], mine_ref.at[:, columns], local_sems.at[2])
    local.start()
    copies = []
    for k in range(1, n_expert):
        target = lax.rem(mine_e + k, n_expert)
        copy = pltpu.make_async_remote_copy(
            src_ref=outgoing.at[target],
            dst_ref=mine_ref.at[:, columns],
            send_sem=ex_send.at[k - 1],
            recv_sem=ex_recv.at[k - 1],
            device_id={"expert": target},
            device_id_type=mesh_id,
        )
        copy.start()
        copies.append(copy)
    local.wait()
    for copy in copies:
        copy.wait()
    keep.wait()


def spread_select(chosen, split, cid):
    n_dp = lax.axis_size("dp")
    n_expert = lax.axis_size("expert")
    _, group, rows, width = split.shape
    n_blocks = n_dp * group
    return pl.pallas_call(
        functools.partial(_spread_kernel, n_dp, n_expert),
        out_shape=[
            jax.ShapeDtypeStruct((n_blocks, rows, width), split.dtype),
            jax.ShapeDtypeStruct((CAP * rows, n_expert * width), split.dtype),
        ],
        in_specs=[pl.BlockSpec(memory_space=pltpu.SMEM), pl.BlockSpec(memory_space=pl.ANY)],
        out_specs=[pl.BlockSpec(memory_space=pl.ANY)] * 2,
        scratch_shapes=[
            pltpu.VMEM((n_blocks, rows, width), split.dtype),
            pltpu.VMEM((n_expert, CAP * rows, width), split.dtype),
            pltpu.SemaphoreType.DMA((3,)),
            pltpu.SemaphoreType.DMA((n_dp - 1,)),
            pltpu.SemaphoreType.DMA((n_dp - 1,)),
            pltpu.SemaphoreType.DMA((n_expert - 1,)),
            pltpu.SemaphoreType.DMA((n_expert - 1,)),
        ],
        compiler_params=pltpu.CompilerParams(collective_id=cid, has_side_effects=True),
    )(chosen, split)


def body(
    context,
    out_weight,
    residual,
    gate_weight,
    up_weight,
    down_weight,
    gate_values,
    chosen_blocks,
    block_counts,
):
    n_dp = lax.axis_size("dp")
    n_expert = lax.axis_size("expert")
    local_tokens = context.shape[0]
    local_width = residual.shape[1]
    model_width = context.shape[1]
    local_blocks = local_tokens // BLK
    n_blocks = local_blocks * n_dp
    piece = BLK // n_dp
    my_expert = lax.axis_index("expert")

    split = gather_attend(
        out_weight, context, residual, cid=10, layout=(n_dp, local_blocks, BLK // n_dp, local_width)
    )

    pieces, mine = spread_select(chosen_blocks.reshape(-1), split, cid=0)
    w_gate = gate_weight[0]
    w_up = up_weight[0]
    w_down = down_weight[0]
    gate_row = gate_values[0]
    my_count = jnp.sum(jnp.where(jnp.arange(n_expert) == my_expert, block_counts, 0))
    row_slot = (jnp.arange(CAP * BLK) // piece) % CAP
    gate_perm = gate_row.reshape(CAP, n_dp, piece).transpose(1, 0, 2).reshape(-1)
    scale = jnp.where(row_slot < my_count, gate_perm, jnp.zeros_like(gate_perm))

    hidden = gather_gate(mine, w_gate, w_up, cid=20)
    halves = down_scatter(hidden, w_down, scale[:, None], cid=1)

    outs = reduce_scatter_2d(halves, cid=2)
    outs = outs.reshape(n_expert, CAP, piece, local_width)

    selector = chosen_blocks[None, :, :] == jnp.arange(n_blocks)[:, None, None]
    added = jnp.einsum(
        "bes,esrf->brf", selector.astype(jnp.bfloat16), outs, preferred_element_type=jnp.float32
    )
    mixed = pieces.astype(jnp.float32) + added
    mixed = mixed.astype(jnp.bfloat16).reshape(n_dp, local_blocks, piece, local_width)
    back = dp_exchange(mixed, gather=False, cid=3)
    return back.transpose(1, 0, 2, 3).reshape(local_tokens, local_width)


def solution(mesh):
    in_specs = (
        P("dp", None),
        P("dp", "expert"),
        P("dp", "expert"),
        P("expert", None, "dp"),
        P("expert", None, "dp"),
        P("expert", "dp", None),
        P("expert", None),
        P(),
        P(),
    )
    out_specs = P("dp", "expert")
    return jax.shard_map(body, mesh=mesh, in_specs=in_specs, out_specs=out_specs, check_vma=False)
```

```python
import functools

import jax
import jax.numpy as jnp
from jax import lax
from jax.sharding import PartitionSpec as P
from jax.experimental import pallas as pl
from jax.experimental.pallas import tpu as pltpu

BLK = 128
CAP = 4


def _exchange_kernel(n, gather, axis, x_ref, o_ref, local_sem, send_sems, recv_sems):
    me = lax.axis_index(axis)
    mesh_id = pl.DeviceIdType.MESH
    barrier = pltpu.get_barrier_semaphore()
    for k in range(1, n):
        pl.semaphore_signal(barrier, 1, device_id={axis: lax.rem(me + k, n)}, device_id_type=mesh_id)
    pl.semaphore_wait(barrier, n - 1)
    local = pltpu.make_async_copy(x_ref if gather else x_ref.at[me], o_ref.at[me], local_sem)
    local.start()
    copies = []
    for k in range(1, n):
        target = lax.rem(me + k, n)
        copy = pltpu.make_async_remote_copy(
            src_ref=x_ref if gather else x_ref.at[target],
            dst_ref=o_ref.at[me],
            send_sem=send_sems.at[k - 1],
            recv_sem=recv_sems.at[k - 1],
            device_id={axis: target},
            device_id_type=mesh_id,
        )
        copy.start()
        copies.append(copy)
    local.wait()
    for copy in copies:
        copy.wait()


def dp_exchange(x, gather, cid, axis="dp"):
    n = lax.axis_size(axis)
    shape = (n,) + x.shape if gather else x.shape
    return pl.pallas_call(
        functools.partial(_exchange_kernel, n, gather, axis),
        out_shape=jax.ShapeDtypeStruct(shape, x.dtype),
        in_specs=[pl.BlockSpec(memory_space=pl.ANY)],
        out_specs=pl.BlockSpec(memory_space=pl.ANY),
        scratch_shapes=[
            pltpu.SemaphoreType.DMA(()),
            pltpu.SemaphoreType.DMA((n - 1,)),
            pltpu.SemaphoreType.DMA((n - 1,)),
        ],
        compiler_params=pltpu.CompilerParams(collective_id=cid, has_side_effects=True),
    )(x)


def _route_kernel(strides, side, gather, windows, *refs):
    n_in = len(strides)
    ins, outs = refs[:n_in], refs[n_in:2 * n_in]
    local_sems, send_sems, recv_sems = refs[2 * n_in:]
    me = lax.axis_index("dp")
    mesh_id = pl.DeviceIdType.MESH

    def window(r):
        if windows is None:
            return ins[r]
        start, size = windows[r]
        return ins[r].at[:, pl.ds(start, size)]

    routes = []
    for r, stride in enumerate(strides):
        coord = lax.rem(me // stride, side)
        base = me - coord * stride
        for k in range(1, side):
            to = lax.rem(coord + k, side)
            routes.append((r, coord, to, base + to * stride))
    barrier = pltpu.get_barrier_semaphore()
    for _, _, _, target in routes:
        pl.semaphore_signal(barrier, 1, device_id={"dp": target}, device_id_type=mesh_id)
    pl.semaphore_wait(barrier, len(routes))
    locals_ = []
    for r in range(n_in):
        coord = lax.rem(me // strides[r], side)
        source = window(r) if gather else ins[r].at[coord]
        local = pltpu.make_async_copy(source, outs[r].at[coord], local_sems.at[r])
        local.start()
        locals_.append(local)
    copies = []
    for i, (r, coord, to, target) in enumerate(routes):
        copy = pltpu.make_async_remote_copy(
            src_ref=window(r) if gather else ins[r].at[to],
            dst_ref=outs[r].at[coord],
            send_sem=send_sems.at[i],
            recv_sem=recv_sems.at[i],
            device_id={"dp": target},
            device_id_type=mesh_id,
        )
        copy.start()
        copies.append(copy)
    for local in locals_:
        local.wait()
    for copy in copies:
        copy.wait()


def dp_route(xs, strides, cid, side=4, gather=False, windows=None):
    n_routes = len(strides) * (side - 1)
    if windows is not None:
        shapes = [(side, x.shape[0], size) for x, (_, size) in zip(xs, windows)]
    else:
        shapes = [((side,) + x.shape) if gather else x.shape for x in xs]
    return pl.pallas_call(
        functools.partial(_route_kernel, tuple(strides), side, gather, windows),
        out_shape=[jax.ShapeDtypeStruct(s, x.dtype) for s, x in zip(shapes, xs)],
        in_specs=[pl.BlockSpec(memory_space=pl.ANY)] * len(xs),
        out_specs=[pl.BlockSpec(memory_space=pl.ANY)] * len(xs),
        scratch_shapes=[
            pltpu.SemaphoreType.DMA((len(xs),)),
            pltpu.SemaphoreType.DMA((n_routes,)),
            pltpu.SemaphoreType.DMA((n_routes,)),
        ],
        compiler_params=pltpu.CompilerParams(collective_id=cid, has_side_effects=True),
    )(*xs)


def _finish_kernel(side, n_expert, a_ref, b_ref, out_ref, got_a, got_b, outgoing,
                   local_sems, send_sems, recv_sems, ex_send, ex_recv):
    me = lax.axis_index("dp")
    mine_e = lax.axis_index("expert")
    mesh_id = pl.DeviceIdType.MESH
    routes = ((a_ref, got_a, side), (b_ref, got_b, 1))
    barrier = pltpu.get_barrier_semaphore()
    for _, _, stride in routes:
        coord = lax.rem(me // stride, side)
        base = me - coord * stride
        for k in range(1, side):
            peer = base + lax.rem(coord + k, side) * stride
            pl.semaphore_signal(barrier, 1, device_id={"dp": peer}, device_id_type=mesh_id)
    for k in range(1, n_expert):
        pl.semaphore_signal(
            barrier, 1, device_id={"expert": lax.rem(mine_e + k, n_expert)}, device_id_type=mesh_id
        )
    pl.semaphore_wait(barrier, 2 * (side - 1) + n_expert - 1)
    locals_, copies = [], []
    for r, (src, dst, stride) in enumerate(routes):
        coord = lax.rem(me // stride, side)
        base = me - coord * stride
        local = pltpu.make_async_copy(src.at[coord], dst.at[coord], local_sems.at[r])
        local.start()
        locals_.append(local)
        for k in range(1, side):
            to = lax.rem(coord + k, side)
            copy = pltpu.make_async_remote_copy(
                src_ref=src.at[to],
                dst_ref=dst.at[coord],
                send_sem=send_sems.at[r, k - 1],
                recv_sem=recv_sems.at[r, k - 1],
                device_id={"dp": base + to * stride},
                device_id_type=mesh_id,
            )
            copy.start()
            copies.append(copy)
    for local in locals_:
        local.wait()
    for copy in copies:
        copy.wait()
    width = outgoing.shape[-1]
    per_half = got_a.shape[-1] // width
    for h, got in enumerate((got_a, got_b)):
        total = got[0].astype(jnp.float32)
        for j in range(1, side):
            total = total + got[j].astype(jnp.float32)
        total = total.astype(outgoing.dtype)
        for j in range(per_half):
            outgoing[h * per_half + j] = total[:, j * width:(j + 1) * width]
    local = pltpu.make_async_copy(outgoing.at[mine_e], out_ref.at[mine_e], local_sems.at[2])
    local.start()
    copies = []
    for k in range(1, n_expert):
        target = lax.rem(mine_e + k, n_expert)
        copy = pltpu.make_async_remote_copy(
            src_ref=outgoing.at[target],
            dst_ref=out_ref.at[mine_e],
            send_sem=ex_send.at[k - 1],
            recv_sem=ex_recv.at[k - 1],
            device_id={"expert": target},
            device_id_type=mesh_id,
        )
        copy.start()
        copies.append(copy)
    local.wait()
    for copy in copies:
        copy.wait()


def _down_scatter_kernel(side, hidden_ref, wd_ref, scale_ref, sum_a, sum_b,
                         send_a, send_b, got_a, got_b, send_sems, recv_sems):
    me = lax.axis_index("dp")
    mesh_id = pl.DeviceIdType.MESH
    half = send_a.shape[-1]
    rows = send_a.shape[2]
    chunk = side * rows
    my_y = lax.rem(me, side)
    my_x = lax.rem(me // side, side)
    base_y = me - my_y
    base_x = me - my_x * side
    barrier = pltpu.get_barrier_semaphore()
    for k in range(1, side):
        pl.semaphore_signal(barrier, 1, device_id={"dp": base_y + lax.rem(my_y + k, side)}, device_id_type=mesh_id)
        pl.semaphore_signal(
            barrier, 1, device_id={"dp": base_x + lax.rem(my_x + k, side) * side}, device_id_type=mesh_id
        )
    pl.semaphore_wait(barrier, 2 * (side - 1))

    def to_a(k, y):
        return pltpu.make_async_remote_copy(
            src_ref=send_a.at[y], dst_ref=got_a.at[my_y], send_sem=send_sems.at[0, k - 1],
            recv_sem=recv_sems.at[0, k - 1], device_id={"dp": base_y + y}, device_id_type=mesh_id,
        )

    def to_b(k, x):
        return pltpu.make_async_remote_copy(
            src_ref=send_b.at[x], dst_ref=got_b.at[my_x], send_sem=send_sems.at[1, k - 1],
            recv_sem=recv_sems.at[1, k - 1], device_id={"dp": base_x + x * side}, device_id_type=mesh_id,
        )

    sends = []
    for k in list(range(1, side)) + [0]:
        x = lax.rem(my_x + k, side)
        at = pl.ds(pl.multiple_of(x * chunk, chunk), chunk)
        part = jnp.dot(hidden_ref[at], wd_ref[...], preferred_element_type=jnp.float32)
        part = (part * scale_ref[at]).astype(send_a.dtype)
        for y in range(side):
            send_a[y, x] = part[y * rows:(y + 1) * rows, :half]
            send_b[x, y] = part[y * rows:(y + 1) * rows, half:]
        if k:
            copy = to_b(k, x)
            copy.start()
            sends.append(copy)
    for k in range(1, side):
        copy = to_a(k, lax.rem(my_y + k, side))
        copy.start()
        sends.append(copy)
    for k in range(1, side):
        to_a(k, lax.rem(my_y + side - k, side)).wait_recv()
        to_b(k, lax.rem(my_x + side - k, side)).wait_recv()
    for x in range(side):
        total = send_a[my_y, x].astype(jnp.float32)
        for k in range(1, side):
            total = total + got_a[lax.rem(my_y + side - k, side), x].astype(jnp.float32)
        sum_a[x] = total.astype(sum_a.dtype)
    for y in range(side):
        total = send_b[my_x, y].astype(jnp.float32)
        for k in range(1, side):
            total = total + got_b[lax.rem(my_x + side - k, side), y].astype(jnp.float32)
        sum_b[y] = total.astype(sum_b.dtype)
    for copy in sends:
        copy.wait_send()


def down_scatter(hidden, w_down, scale, cid):
    side = 4
    rows = hidden.shape[0] // (side * side)
    half = w_down.shape[1] // 2
    slab = (side, side, rows, half)
    vmem = pl.BlockSpec(memory_space=pltpu.VMEM)
    return pl.pallas_call(
        functools.partial(_down_scatter_kernel, side),
        out_shape=[jax.ShapeDtypeStruct((side, rows, half), jnp.bfloat16)] * 2,
        in_specs=[vmem] * 3,
        out_specs=[vmem] * 2,
        scratch_shapes=[
            pltpu.VMEM(slab, jnp.bfloat16),
            pltpu.VMEM(slab, jnp.bfloat16),
            pltpu.VMEM(slab, jnp.bfloat16),
            pltpu.VMEM(slab, jnp.bfloat16),
            pltpu.SemaphoreType.DMA((2, side - 1)),
            pltpu.SemaphoreType.DMA((2, side - 1)),
        ],
        compiler_params=pltpu.CompilerParams(collective_id=cid, has_side_effects=True),
    )(hidden, w_down, scale)


def reduce_scatter_2d(part, cid):
    side = 4
    n_expert = lax.axis_size("expert")
    second_a, second_b = part
    rows = second_a.shape[1]
    cols = 2 * second_a.shape[2]
    width = cols // n_expert
    return pl.pallas_call(
        functools.partial(_finish_kernel, side, n_expert),
        out_shape=jax.ShapeDtypeStruct((n_expert, rows, width), second_a.dtype),
        in_specs=[pl.BlockSpec(memory_space=pl.ANY)] * 2,
        out_specs=pl.BlockSpec(memory_space=pl.ANY),
        scratch_shapes=[
            pltpu.VMEM(second_a.shape, second_a.dtype),
            pltpu.VMEM(second_b.shape, second_b.dtype),
            pltpu.VMEM((n_expert, rows, width), second_a.dtype),
            pltpu.SemaphoreType.DMA((3,)),
            pltpu.SemaphoreType.DMA((2, side - 1)),
            pltpu.SemaphoreType.DMA((2, side - 1)),
            pltpu.SemaphoreType.DMA((n_expert - 1,)),
            pltpu.SemaphoreType.DMA((n_expert - 1,)),
        ],
        compiler_params=pltpu.CompilerParams(collective_id=cid, has_side_effects=True),
    )(second_a, second_b)


def all_gather_2d(x, cid):
    side = 4
    half = x.shape[-1] // 2
    got_a, got_b = dp_route([x, x], (1, side), cid, gather=True, windows=((0, half), (half, half)))
    got_a, got_b = dp_route([got_a, got_b], (side, 1), cid + 1, gather=True)
    n = side * side
    got_a = got_a.reshape((n,) + got_a.shape[2:])
    perm = (1, 0) + tuple(range(2, got_b.ndim))
    got_b = got_b.transpose(perm).reshape((n,) + got_b.shape[2:])
    return got_a, got_b


def _gather_gate_kernel(side, a_ref, b_ref, wg_ref, wu_ref, hidden_ref,
                        got_a, got_b, acc_g, acc_u, local_sems, send_sems, recv_sems):
    me = lax.axis_index("dp")
    mesh_id = pl.DeviceIdType.MESH
    half = a_ref.shape[-1]
    group = got_a.shape[1] * got_a.shape[2]
    rows = got_a.shape[2]
    routes = ((a_ref, got_a, side), (b_ref, got_b, 1))
    geo = []
    for _, _, stride in routes:
        coord = lax.rem(me // stride, side)
        geo.append((coord, me - coord * stride))
    barrier = pltpu.get_barrier_semaphore()
    for (coord, base), (_, _, stride) in zip(geo, routes):
        for k in range(1, side):
            peer = base + lax.rem(coord + k, side) * stride
            pl.semaphore_signal(barrier, 1, device_id={"dp": peer}, device_id_type=mesh_id)
    pl.semaphore_wait(barrier, 2 * (side - 1))

    def remote(r, k, source, to):
        src, dst, stride = routes[r]
        coord, base = geo[r]
        return pltpu.make_async_remote_copy(
            src_ref=src,
            dst_ref=dst.at[source],
            send_sem=send_sems.at[r, k - 1],
            recv_sem=recv_sems.at[r, k - 1],
            device_id={"dp": base + to * stride},
            device_id_type=mesh_id,
        )

    locals_, sends = [], []
    for r, (src, dst, stride) in enumerate(routes):
        coord, base = geo[r]
        local = pltpu.make_async_copy(src, dst.at[coord], local_sems.at[r])
        local.start()
        locals_.append(local)
        for k in range(1, side):
            copy = remote(r, k, coord, lax.rem(coord + k, side))
            copy.start()
            sends.append(copy)
    acc_g[...] = jnp.zeros_like(acc_g)
    acc_u[...] = jnp.zeros_like(acc_u)

    def add_a(source):
        block = got_a[source].reshape(group, half)
        at = pl.ds(pl.multiple_of(source * group, group), group)
        acc_g[at] += jnp.dot(block, wg_ref[:half], preferred_element_type=jnp.float32)
        acc_u[at] += jnp.dot(block, wu_ref[:half], preferred_element_type=jnp.float32)

    def add_b(source):
        block = got_b[source].reshape(group, half)
        g = jnp.dot(block, wg_ref[half:], preferred_element_type=jnp.float32)
        u = jnp.dot(block, wu_ref[half:], preferred_element_type=jnp.float32)
        for x in range(side):
            at = pl.ds(pl.multiple_of((x * side + source) * rows, rows), rows)
            acc_g[at] += g[x * rows:(x + 1) * rows]
            acc_u[at] += u[x * rows:(x + 1) * rows]

    for local in locals_:
        local.wait()
    add_a(geo[0][0])
    add_b(geo[1][0])
    for k in range(1, side):
        for r, add in ((0, add_a), (1, add_b)):
            coord, _ = geo[r]
            source = lax.rem(coord + side - k, side)
            remote(r, k, source, source).wait_recv()
            add(source)
    g = acc_g[...]
    hidden_ref[...] = (g / (1.0 + jnp.exp(-g)) * acc_u[...]).astype(hidden_ref.dtype)
    for copy in sends:
        copy.wait_send()


def gather_gate(x, w_gate, w_up, cid):
    side = 4
    n = side * side
    half = x.shape[-1] // 2
    first_a, first_b = dp_route([x, x], (1, side), cid, gather=True, windows=((0, half), (half, half)))
    return pl.pallas_call(
        functools.partial(_gather_gate_kernel, side),
        out_shape=jax.ShapeDtypeStruct((n * x.shape[0], w_gate.shape[1]), jnp.bfloat16),
        in_specs=[pl.BlockSpec(memory_space=pl.ANY)] * 2 + [pl.BlockSpec(memory_space=pltpu.VMEM)] * 2,
        out_specs=pl.BlockSpec(memory_space=pltpu.VMEM),
        scratch_shapes=[
            pltpu.VMEM((side,) + first_a.shape, first_a.dtype),
            pltpu.VMEM((side,) + first_b.shape, first_b.dtype),
            pltpu.VMEM((n * x.shape[0], w_gate.shape[1]), jnp.float32),
            pltpu.VMEM((n * x.shape[0], w_gate.shape[1]), jnp.float32),
            pltpu.SemaphoreType.DMA((2,)),
            pltpu.SemaphoreType.DMA((2, side - 1)),
            pltpu.SemaphoreType.DMA((2, side - 1)),
        ],
        compiler_params=pltpu.CompilerParams(collective_id=cid + 1, has_side_effects=True),
    )(first_a, first_b, w_gate, w_up)


def _gather_attend_kernel(side, a_ref, b_ref, ctx_ref, res_ref, out_ref,
                          got_a, got_b, acc_a, acc_b, local_sems, send_sems, recv_sems):
    me = lax.axis_index("dp")
    mesh_id = pl.DeviceIdType.MESH
    rows = got_a.shape[2]
    bundle = side * rows
    routes = ((a_ref, got_a, side), (b_ref, got_b, 1))
    geo = []
    for _, _, stride in routes:
        coord = lax.rem(me // stride, side)
        geo.append((coord, me - coord * stride))
    barrier = pltpu.get_barrier_semaphore()
    for (coord, base), (_, _, stride) in zip(geo, routes):
        for k in range(1, side):
            peer = base + lax.rem(coord + k, side) * stride
            pl.semaphore_signal(barrier, 1, device_id={"dp": peer}, device_id_type=mesh_id)
    pl.semaphore_wait(barrier, 2 * (side - 1))

    def remote(r, k, source, to):
        src, dst, stride = routes[r]
        coord, base = geo[r]
        return pltpu.make_async_remote_copy(
            src_ref=src,
            dst_ref=dst.at[source],
            send_sem=send_sems.at[r, k - 1],
            recv_sem=recv_sems.at[r, k - 1],
            device_id={"dp": base + to * stride},
            device_id_type=mesh_id,
        )

    locals_, sends = [], []
    for r, (src, dst, stride) in enumerate(routes):
        coord, base = geo[r]
        local = pltpu.make_async_copy(src, dst.at[coord], local_sems.at[r])
        local.start()
        locals_.append(local)
        for k in range(1, side):
            copy = remote(r, k, coord, lax.rem(coord + k, side))
            copy.start()
            sends.append(copy)
    acc_a[...] = jnp.zeros_like(acc_a)
    acc_b[...] = jnp.zeros_like(acc_b)

    def add_a(source):
        block = got_a[source].reshape(bundle, got_a.shape[-1])
        at = pl.ds(pl.multiple_of(source * bundle, bundle), bundle)
        acc_a[...] += jnp.dot(ctx_ref[:, at], block, preferred_element_type=jnp.float32)

    def add_b(source):
        for x in range(side):
            at = pl.ds(pl.multiple_of((x * side + source) * rows, rows), rows)
            acc_b[...] += jnp.dot(ctx_ref[:, at], got_b[source, x], preferred_element_type=jnp.float32)

    for local in locals_:
        local.wait()
    add_a(geo[0][0])
    add_b(geo[1][0])
    for k in range(1, side):
        for r, add in ((0, add_a), (1, add_b)):
            coord, _ = geo[r]
            source = lax.rem(coord + side - k, side)
            remote(r, k, source, source).wait_recv()
            add(source)
    half = acc_a.shape[1]
    n_pieces, n_local, piece = out_ref.shape[:3]
    for b in range(n_local):
        for k in range(n_pieces):
            at = b * n_pieces * piece + k * piece
            out_ref[k, b, :, :half] = (
                res_ref[at:at + piece, :half].astype(jnp.float32) + acc_a[at:at + piece]
            ).astype(out_ref.dtype)
            out_ref[k, b, :, half:] = (
                res_ref[at:at + piece, half:].astype(jnp.float32) + acc_b[at:at + piece]
            ).astype(out_ref.dtype)
    for copy in sends:
        copy.wait_send()


def gather_attend(w, context, residual, cid, layout):
    side = 4
    half = w.shape[-1] // 2
    first_a, first_b = dp_route([w, w], (1, side), cid, gather=True, windows=((0, half), (half, half)))
    vmem = pl.BlockSpec(memory_space=pltpu.VMEM)
    return pl.pallas_call(
        functools.partial(_gather_attend_kernel, side),
        out_shape=jax.ShapeDtypeStruct(layout, jnp.bfloat16),
        in_specs=[pl.BlockSpec(memory_space=pl.ANY)] * 2 + [vmem] * 2,
        out_specs=vmem,
        scratch_shapes=[
            pltpu.VMEM((side,) + first_a.shape, first_a.dtype),
            pltpu.VMEM((side,) + first_b.shape, first_b.dtype),
            pltpu.VMEM((context.shape[0], half), jnp.float32),
            pltpu.VMEM((context.shape[0], half), jnp.float32),
            pltpu.SemaphoreType.DMA((2,)),
            pltpu.SemaphoreType.DMA((2, side - 1)),
            pltpu.SemaphoreType.DMA((2, side - 1)),
        ],
        compiler_params=pltpu.CompilerParams(collective_id=cid + 1, has_side_effects=True),
    )(first_a, first_b, context, residual)


def _spread_kernel(n_dp, n_expert, chosen_ref, split_ref, pieces_ref, mine_ref,
                   held, outgoing, local_sems, dp_send, dp_recv, ex_send, ex_recv):
    me = lax.axis_index("dp")
    mine_e = lax.axis_index("expert")
    mesh_id = pl.DeviceIdType.MESH
    group = split_ref.shape[1]
    barrier = pltpu.get_barrier_semaphore()
    for k in range(1, n_dp):
        pl.semaphore_signal(barrier, 1, device_id={"dp": lax.rem(me + k, n_dp)}, device_id_type=mesh_id)
    for k in range(1, n_expert):
        pl.semaphore_signal(
            barrier, 1, device_id={"expert": lax.rem(mine_e + k, n_expert)}, device_id_type=mesh_id
        )
    pl.semaphore_wait(barrier, n_dp + n_expert - 2)

    def at_source(src):
        return held.at[pl.ds(pl.multiple_of(src * group, group), group)]

    local = pltpu.make_async_copy(split_ref.at[me], at_source(me), local_sems.at[0])
    local.start()
    copies = []
    for k in range(1, n_dp):
        target = lax.rem(me + k, n_dp)
        copy = pltpu.make_async_remote_copy(
            src_ref=split_ref.at[target],
            dst_ref=at_source(me),
            send_sem=dp_send.at[k - 1],
            recv_sem=dp_recv.at[k - 1],
            device_id={"dp": target},
            device_id_type=mesh_id,
        )
        copy.start()
        copies.append(copy)
    local.wait()
    for copy in copies:
        copy.wait()
    keep = pltpu.make_async_copy(held, pieces_ref, local_sems.at[1])
    keep.start()
    rows = held.shape[1]
    width = held.shape[2]
    for e in range(n_expert):
        for s in range(CAP):
            outgoing[e, s * rows:(s + 1) * rows] = held[chosen_ref[e, s]]
    columns = pl.ds(pl.multiple_of(mine_e * width, width), width)
    local = pltpu.make_async_copy(outgoing.at[mine_e], mine_ref.at[:, columns], local_sems.at[2])
    local.start()
    copies = []
    for k in range(1, n_expert):
        target = lax.rem(mine_e + k, n_expert)
        copy = pltpu.make_async_remote_copy(
            src_ref=outgoing.at[target],
            dst_ref=mine_ref.at[:, columns],
            send_sem=ex_send.at[k - 1],
            recv_sem=ex_recv.at[k - 1],
            device_id={"expert": target},
            device_id_type=mesh_id,
        )
        copy.start()
        copies.append(copy)
    local.wait()
    for copy in copies:
        copy.wait()
    keep.wait()


def spread_select(chosen, split, cid):
    n_dp = lax.axis_size("dp")
    n_expert = lax.axis_size("expert")
    _, group, rows, width = split.shape
    n_blocks = n_dp * group
    return pl.pallas_call(
        functools.partial(_spread_kernel, n_dp, n_expert),
        out_shape=[
            jax.ShapeDtypeStruct((n_blocks, rows, width), split.dtype),
            jax.ShapeDtypeStruct((CAP * rows, n_expert * width), split.dtype),
        ],
        in_specs=[pl.BlockSpec(memory_space=pltpu.SMEM), pl.BlockSpec(memory_space=pl.ANY)],
        out_specs=[pl.BlockSpec(memory_space=pl.ANY)] * 2,
        scratch_shapes=[
            pltpu.VMEM((n_blocks, rows, width), split.dtype),
            pltpu.VMEM((n_expert, CAP * rows, width), split.dtype),
            pltpu.SemaphoreType.DMA((3,)),
            pltpu.SemaphoreType.DMA((n_dp - 1,)),
            pltpu.SemaphoreType.DMA((n_dp - 1,)),
            pltpu.SemaphoreType.DMA((n_expert - 1,)),
            pltpu.SemaphoreType.DMA((n_expert - 1,)),
        ],
        compiler_params=pltpu.CompilerParams(collective_id=cid, has_side_effects=True),
    )(chosen, split)


def body(
    context,
    out_weight,
    residual,
    gate_weight,
    up_weight,
    down_weight,
    gate_values,
    chosen_blocks,
    block_counts,
):
    n_dp = lax.axis_size("dp")
    n_expert = lax.axis_size("expert")
    local_tokens = context.shape[0]
    local_width = residual.shape[1]
    model_width = context.shape[1]
    local_blocks = local_tokens // BLK
    n_blocks = local_blocks * n_dp
    piece = BLK // n_dp
    my_expert = lax.axis_index("expert")

    split = gather_attend(
        out_weight, context, residual, cid=10, layout=(n_dp, local_blocks, BLK // n_dp, local_width)
    )

    pieces, mine = spread_select(chosen_blocks, split, cid=0)
    w_gate = gate_weight[0]
    w_up = up_weight[0]
    w_down = down_weight[0]
    gate_row = gate_values[0]
    my_count = jnp.sum(jnp.where(jnp.arange(n_expert) == my_expert, block_counts, 0))
    row_slot = (jnp.arange(CAP * BLK) // piece) % CAP
    gate_perm = gate_row.reshape(CAP, n_dp, piece).transpose(1, 0, 2).reshape(-1)
    scale = jnp.where(row_slot < my_count, gate_perm, jnp.zeros_like(gate_perm))

    hidden = gather_gate(mine, w_gate, w_up, cid=20)
    halves = down_scatter(hidden, w_down, scale[:, None], cid=1)

    outs = reduce_scatter_2d(halves, cid=2)
    outs = outs.reshape(n_expert * CAP, piece * local_width)

    selector = chosen_blocks.reshape(-1)[None, :] == jnp.arange(n_blocks)[:, None]
    added = jnp.dot(selector.astype(jnp.bfloat16), outs, preferred_element_type=jnp.float32)
    mixed = pieces.reshape(n_blocks, piece * local_width).astype(jnp.float32) + added
    mixed = mixed.astype(jnp.bfloat16).reshape(n_dp, local_blocks, piece, local_width)
    back = dp_exchange(mixed, gather=False, cid=3)
    return back.transpose(1, 0, 2, 3).reshape(local_tokens, local_width)


def solution(mesh):
    in_specs = (
        P("dp", None),
        P("dp", "expert"),
        P("dp", "expert"),
        P("expert", None, "dp"),
        P("expert", None, "dp"),
        P("expert", "dp", None),
        P("expert", None),
        P(),
        P(),
    )
    out_specs = P("dp", "expert")
    return jax.shard_map(body, mesh=mesh, in_specs=in_specs, out_specs=out_specs, check_vma=False)
```

```python
import functools

import jax
import jax.numpy as jnp
from jax import lax
from jax.sharding import PartitionSpec as P
from jax.experimental import pallas as pl
from jax.experimental.pallas import tpu as pltpu

BLK = 128
CAP = 4


def _exchange_kernel(n, gather, axis, x_ref, o_ref, local_sem, send_sems, recv_sems):
    me = lax.axis_index(axis)
    mesh_id = pl.DeviceIdType.MESH
    barrier = pltpu.get_barrier_semaphore()
    for k in range(1, n):
        pl.semaphore_signal(barrier, 1, device_id={axis: lax.rem(me + k, n)}, device_id_type=mesh_id)
    pl.semaphore_wait(barrier, n - 1)
    local = pltpu.make_async_copy(x_ref if gather else x_ref.at[me], o_ref.at[me], local_sem)
    local.start()
    copies = []
    for k in range(1, n):
        target = lax.rem(me + k, n)
        copy = pltpu.make_async_remote_copy(
            src_ref=x_ref if gather else x_ref.at[target],
            dst_ref=o_ref.at[me],
            send_sem=send_sems.at[k - 1],
            recv_sem=recv_sems.at[k - 1],
            device_id={axis: target},
            device_id_type=mesh_id,
        )
        copy.start()
        copies.append(copy)
    local.wait()
    for copy in copies:
        copy.wait()


def dp_exchange(x, gather, cid, axis="dp"):
    n = lax.axis_size(axis)
    shape = (n,) + x.shape if gather else x.shape
    return pl.pallas_call(
        functools.partial(_exchange_kernel, n, gather, axis),
        out_shape=jax.ShapeDtypeStruct(shape, x.dtype),
        in_specs=[pl.BlockSpec(memory_space=pl.ANY)],
        out_specs=pl.BlockSpec(memory_space=pl.ANY),
        scratch_shapes=[
            pltpu.SemaphoreType.DMA(()),
            pltpu.SemaphoreType.DMA((n - 1,)),
            pltpu.SemaphoreType.DMA((n - 1,)),
        ],
        compiler_params=pltpu.CompilerParams(collective_id=cid, has_side_effects=True),
    )(x)


def _route_kernel(strides, side, gather, windows, *refs):
    n_in = len(strides)
    ins, outs = refs[:n_in], refs[n_in:2 * n_in]
    local_sems, send_sems, recv_sems = refs[2 * n_in:]
    me = lax.axis_index("dp")
    mesh_id = pl.DeviceIdType.MESH

    def window(r):
        if windows is None:
            return ins[r]
        start, size = windows[r]
        return ins[r].at[:, pl.ds(start, size)]

    routes = []
    for r, stride in enumerate(strides):
        coord = lax.rem(me // stride, side)
        base = me - coord * stride
        for k in range(1, side):
            to = lax.rem(coord + k, side)
            routes.append((r, coord, to, base + to * stride))
    barrier = pltpu.get_barrier_semaphore()
    for _, _, _, target in routes:
        pl.semaphore_signal(barrier, 1, device_id={"dp": target}, device_id_type=mesh_id)
    pl.semaphore_wait(barrier, len(routes))
    locals_ = []
    for r in range(n_in):
        coord = lax.rem(me // strides[r], side)
        source = window(r) if gather else ins[r].at[coord]
        local = pltpu.make_async_copy(source, outs[r].at[coord], local_sems.at[r])
        local.start()
        locals_.append(local)
    copies = []
    for i, (r, coord, to, target) in enumerate(routes):
        copy = pltpu.make_async_remote_copy(
            src_ref=window(r) if gather else ins[r].at[to],
            dst_ref=outs[r].at[coord],
            send_sem=send_sems.at[i],
            recv_sem=recv_sems.at[i],
            device_id={"dp": target},
            device_id_type=mesh_id,
        )
        copy.start()
        copies.append(copy)
    for local in locals_:
        local.wait()
    for copy in copies:
        copy.wait()


def dp_route(xs, strides, cid, side=4, gather=False, windows=None):
    n_routes = len(strides) * (side - 1)
    if windows is not None:
        shapes = [(side, x.shape[0], size) for x, (_, size) in zip(xs, windows)]
    else:
        shapes = [((side,) + x.shape) if gather else x.shape for x in xs]
    return pl.pallas_call(
        functools.partial(_route_kernel, tuple(strides), side, gather, windows),
        out_shape=[jax.ShapeDtypeStruct(s, x.dtype) for s, x in zip(shapes, xs)],
        in_specs=[pl.BlockSpec(memory_space=pl.ANY)] * len(xs),
        out_specs=[pl.BlockSpec(memory_space=pl.ANY)] * len(xs),
        scratch_shapes=[
            pltpu.SemaphoreType.DMA((len(xs),)),
            pltpu.SemaphoreType.DMA((n_routes,)),
            pltpu.SemaphoreType.DMA((n_routes,)),
        ],
        compiler_params=pltpu.CompilerParams(collective_id=cid, has_side_effects=True),
    )(*xs)


def _finish_kernel(side, n_expert, a_ref, b_ref, out_ref, got_a, got_b, outgoing,
                   local_sems, send_sems, recv_sems, ex_send, ex_recv):
    me = lax.axis_index("dp")
    mine_e = lax.axis_index("expert")
    mesh_id = pl.DeviceIdType.MESH
    routes = ((a_ref, got_a, side), (b_ref, got_b, 1))
    barrier = pltpu.get_barrier_semaphore()
    for _, _, stride in routes:
        coord = lax.rem(me // stride, side)
        base = me - coord * stride
        for k in range(1, side):
            peer = base + lax.rem(coord + k, side) * stride
            pl.semaphore_signal(barrier, 1, device_id={"dp": peer}, device_id_type=mesh_id)
    for k in range(1, n_expert):
        pl.semaphore_signal(
            barrier, 1, device_id={"expert": lax.rem(mine_e + k, n_expert)}, device_id_type=mesh_id
        )
    pl.semaphore_wait(barrier, 2 * (side - 1) + n_expert - 1)
    locals_, copies = [], []
    for r, (src, dst, stride) in enumerate(routes):
        coord = lax.rem(me // stride, side)
        base = me - coord * stride
        local = pltpu.make_async_copy(src.at[coord], dst.at[coord], local_sems.at[r])
        local.start()
        locals_.append(local)
        for k in range(1, side):
            to = lax.rem(coord + k, side)
            copy = pltpu.make_async_remote_copy(
                src_ref=src.at[to],
                dst_ref=dst.at[coord],
                send_sem=send_sems.at[r, k - 1],
                recv_sem=recv_sems.at[r, k - 1],
                device_id={"dp": base + to * stride},
                device_id_type=mesh_id,
            )
            copy.start()
            copies.append(copy)
    for local in locals_:
        local.wait()
    for copy in copies:
        copy.wait()
    width = outgoing.shape[-1]
    per_half = got_a.shape[-1] // width
    for h, got in enumerate((got_a, got_b)):
        total = got[0].astype(jnp.float32)
        for j in range(1, side):
            total = total + got[j].astype(jnp.float32)
        total = total.astype(outgoing.dtype)
        for j in range(per_half):
            outgoing[h * per_half + j] = total[:, j * width:(j + 1) * width]
    local = pltpu.make_async_copy(outgoing.at[mine_e], out_ref.at[mine_e], local_sems.at[2])
    local.start()
    copies = []
    for k in range(1, n_expert):
        target = lax.rem(mine_e + k, n_expert)
        copy = pltpu.make_async_remote_copy(
            src_ref=outgoing.at[target],
            dst_ref=out_ref.at[mine_e],
            send_sem=ex_send.at[k - 1],
            recv_sem=ex_recv.at[k - 1],
            device_id={"expert": target},
            device_id_type=mesh_id,
        )
        copy.start()
        copies.append(copy)
    local.wait()
    for copy in copies:
        copy.wait()


def _down_scatter_kernel(side, counts_ref, hidden_ref, wd_ref, scale_ref, sum_a, sum_b,
                         send_a, send_b, got_a, got_b, send_sems, recv_sems):
    me = lax.axis_index("dp")
    mesh_id = pl.DeviceIdType.MESH
    half = send_a.shape[-1]
    rows = send_a.shape[2]
    chunk = side * rows
    my_y = lax.rem(me, side)
    my_x = lax.rem(me // side, side)
    base_y = me - my_y
    base_x = me - my_x * side
    barrier = pltpu.get_barrier_semaphore()
    for k in range(1, side):
        pl.semaphore_signal(barrier, 1, device_id={"dp": base_y + lax.rem(my_y + k, side)}, device_id_type=mesh_id)
        pl.semaphore_signal(
            barrier, 1, device_id={"dp": base_x + lax.rem(my_x + k, side) * side}, device_id_type=mesh_id
        )
    pl.semaphore_wait(barrier, 2 * (side - 1))

    def to_a(k, y):
        return pltpu.make_async_remote_copy(
            src_ref=send_a.at[y], dst_ref=got_a.at[my_y], send_sem=send_sems.at[0, k - 1],
            recv_sem=recv_sems.at[0, k - 1], device_id={"dp": base_y + y}, device_id_type=mesh_id,
        )

    def to_b(k, x):
        return pltpu.make_async_remote_copy(
            src_ref=send_b.at[x], dst_ref=got_b.at[my_x], send_sem=send_sems.at[1, k - 1],
            recv_sem=recv_sems.at[1, k - 1], device_id={"dp": base_x + x * side}, device_id_type=mesh_id,
        )

    count = counts_ref[lax.axis_index("expert")]
    rows_per_slot = rows // CAP
    sends = []
    for k in list(range(1, side)) + [0]:
        x = lax.rem(my_x + k, side)
        at = pl.ds(pl.multiple_of(x * chunk, chunk), chunk)
        part = jnp.dot(hidden_ref[at], wd_ref[...], preferred_element_type=jnp.float32)
        slot = lax.rem(lax.broadcasted_iota(jnp.int32, (chunk, 1), 0) // rows_per_slot, CAP)
        live = jnp.where(slot < count, scale_ref[at], 0.0)
        part = (part * live).astype(send_a.dtype)
        for y in range(side):
            send_a[y, x] = part[y * rows:(y + 1) * rows, :half]
            send_b[x, y] = part[y * rows:(y + 1) * rows, half:]
        if k:
            copy = to_b(k, x)
            copy.start()
            sends.append(copy)
    for k in range(1, side):
        copy = to_a(k, lax.rem(my_y + k, side))
        copy.start()
        sends.append(copy)
    for k in range(1, side):
        to_a(k, lax.rem(my_y + side - k, side)).wait_recv()
        to_b(k, lax.rem(my_x + side - k, side)).wait_recv()
    for x in range(side):
        total = send_a[my_y, x].astype(jnp.float32)
        for k in range(1, side):
            total = total + got_a[lax.rem(my_y + side - k, side), x].astype(jnp.float32)
        sum_a[x] = total.astype(sum_a.dtype)
    for y in range(side):
        total = send_b[my_x, y].astype(jnp.float32)
        for k in range(1, side):
            total = total + got_b[lax.rem(my_x + side - k, side), y].astype(jnp.float32)
        sum_b[y] = total.astype(sum_b.dtype)
    for copy in sends:
        copy.wait_send()


def down_scatter(counts, hidden, w_down, scale, cid):
    side = 4
    rows = hidden.shape[0] // (side * side)
    half = w_down.shape[1] // 2
    slab = (side, side, rows, half)
    vmem = pl.BlockSpec(memory_space=pltpu.VMEM)
    return pl.pallas_call(
        functools.partial(_down_scatter_kernel, side),
        out_shape=[jax.ShapeDtypeStruct((side, rows, half), jnp.bfloat16)] * 2,
        in_specs=[pl.BlockSpec(memory_space=pltpu.SMEM)] + [vmem] * 3,
        out_specs=[vmem] * 2,
        scratch_shapes=[
            pltpu.VMEM(slab, jnp.bfloat16),
            pltpu.VMEM(slab, jnp.bfloat16),
            pltpu.VMEM(slab, jnp.bfloat16),
            pltpu.VMEM(slab, jnp.bfloat16),
            pltpu.SemaphoreType.DMA((2, side - 1)),
            pltpu.SemaphoreType.DMA((2, side - 1)),
        ],
        compiler_params=pltpu.CompilerParams(collective_id=cid, has_side_effects=True),
    )(counts, hidden, w_down, scale)


def reduce_scatter_2d(part, cid):
    side = 4
    n_expert = lax.axis_size("expert")
    second_a, second_b = part
    rows = second_a.shape[1]
    cols = 2 * second_a.shape[2]
    width = cols // n_expert
    return pl.pallas_call(
        functools.partial(_finish_kernel, side, n_expert),
        out_shape=jax.ShapeDtypeStruct((n_expert, rows, width), second_a.dtype),
        in_specs=[pl.BlockSpec(memory_space=pl.ANY)] * 2,
        out_specs=pl.BlockSpec(memory_space=pl.ANY),
        scratch_shapes=[
            pltpu.VMEM(second_a.shape, second_a.dtype),
            pltpu.VMEM(second_b.shape, second_b.dtype),
            pltpu.VMEM((n_expert, rows, width), second_a.dtype),
            pltpu.SemaphoreType.DMA((3,)),
            pltpu.SemaphoreType.DMA((2, side - 1)),
            pltpu.SemaphoreType.DMA((2, side - 1)),
            pltpu.SemaphoreType.DMA((n_expert - 1,)),
            pltpu.SemaphoreType.DMA((n_expert - 1,)),
        ],
        compiler_params=pltpu.CompilerParams(collective_id=cid, has_side_effects=True),
    )(second_a, second_b)


def all_gather_2d(x, cid):
    side = 4
    half = x.shape[-1] // 2
    got_a, got_b = dp_route([x, x], (1, side), cid, gather=True, windows=((0, half), (half, half)))
    got_a, got_b = dp_route([got_a, got_b], (side, 1), cid + 1, gather=True)
    n = side * side
    got_a = got_a.reshape((n,) + got_a.shape[2:])
    perm = (1, 0) + tuple(range(2, got_b.ndim))
    got_b = got_b.transpose(perm).reshape((n,) + got_b.shape[2:])
    return got_a, got_b


def _gather_gate_kernel(side, a_ref, b_ref, wg_ref, wu_ref, hidden_ref,
                        got_a, got_b, acc_g, acc_u, local_sems, send_sems, recv_sems):
    me = lax.axis_index("dp")
    mesh_id = pl.DeviceIdType.MESH
    half = a_ref.shape[-1]
    group = got_a.shape[1] * got_a.shape[2]
    rows = got_a.shape[2]
    routes = ((a_ref, got_a, side), (b_ref, got_b, 1))
    geo = []
    for _, _, stride in routes:
        coord = lax.rem(me // stride, side)
        geo.append((coord, me - coord * stride))
    barrier = pltpu.get_barrier_semaphore()
    for (coord, base), (_, _, stride) in zip(geo, routes):
        for k in range(1, side):
            peer = base + lax.rem(coord + k, side) * stride
            pl.semaphore_signal(barrier, 1, device_id={"dp": peer}, device_id_type=mesh_id)
    pl.semaphore_wait(barrier, 2 * (side - 1))

    def remote(r, k, source, to):
        src, dst, stride = routes[r]
        coord, base = geo[r]
        return pltpu.make_async_remote_copy(
            src_ref=src,
            dst_ref=dst.at[source],
            send_sem=send_sems.at[r, k - 1],
            recv_sem=recv_sems.at[r, k - 1],
            device_id={"dp": base + to * stride},
            device_id_type=mesh_id,
        )

    locals_, sends = [], []
    for r, (src, dst, stride) in enumerate(routes):
        coord, base = geo[r]
        local = pltpu.make_async_copy(src, dst.at[coord], local_sems.at[r])
        local.start()
        locals_.append(local)
        for k in range(1, side):
            copy = remote(r, k, coord, lax.rem(coord + k, side))
            copy.start()
            sends.append(copy)
    acc_g[...] = jnp.zeros_like(acc_g)
    acc_u[...] = jnp.zeros_like(acc_u)

    def add_a(source):
        block = got_a[source].reshape(group, half)
        at = pl.ds(pl.multiple_of(source * group, group), group)
        acc_g[at] += jnp.dot(block, wg_ref[:half], preferred_element_type=jnp.float32)
        acc_u[at] += jnp.dot(block, wu_ref[:half], preferred_element_type=jnp.float32)

    def add_b(source):
        block = got_b[source].reshape(group, half)
        g = jnp.dot(block, wg_ref[half:], preferred_element_type=jnp.float32)
        u = jnp.dot(block, wu_ref[half:], preferred_element_type=jnp.float32)
        for x in range(side):
            at = pl.ds(pl.multiple_of((x * side + source) * rows, rows), rows)
            acc_g[at] += g[x * rows:(x + 1) * rows]
            acc_u[at] += u[x * rows:(x + 1) * rows]

    for local in locals_:
        local.wait()
    add_a(geo[0][0])
    add_b(geo[1][0])
    for k in range(1, side):
        for r, add in ((0, add_a), (1, add_b)):
            coord, _ = geo[r]
            source = lax.rem(coord + side - k, side)
            remote(r, k, source, source).wait_recv()
            add(source)
    g = acc_g[...]
    hidden_ref[...] = (g / (1.0 + jnp.exp(-g)) * acc_u[...]).astype(hidden_ref.dtype)
    for copy in sends:
        copy.wait_send()


def gather_gate(x, w_gate, w_up, cid):
    side = 4
    n = side * side
    half = x.shape[-1] // 2
    first_a, first_b = dp_route([x, x], (1, side), cid, gather=True, windows=((0, half), (half, half)))
    return pl.pallas_call(
        functools.partial(_gather_gate_kernel, side),
        out_shape=jax.ShapeDtypeStruct((n * x.shape[0], w_gate.shape[1]), jnp.bfloat16),
        in_specs=[pl.BlockSpec(memory_space=pl.ANY)] * 2 + [pl.BlockSpec(memory_space=pltpu.VMEM)] * 2,
        out_specs=pl.BlockSpec(memory_space=pltpu.VMEM),
        scratch_shapes=[
            pltpu.VMEM((side,) + first_a.shape, first_a.dtype),
            pltpu.VMEM((side,) + first_b.shape, first_b.dtype),
            pltpu.VMEM((n * x.shape[0], w_gate.shape[1]), jnp.float32),
            pltpu.VMEM((n * x.shape[0], w_gate.shape[1]), jnp.float32),
            pltpu.SemaphoreType.DMA((2,)),
            pltpu.SemaphoreType.DMA((2, side - 1)),
            pltpu.SemaphoreType.DMA((2, side - 1)),
        ],
        compiler_params=pltpu.CompilerParams(collective_id=cid + 1, has_side_effects=True),
    )(first_a, first_b, w_gate, w_up)


def _gather_attend_kernel(side, a_ref, b_ref, ctx_ref, res_ref, out_ref,
                          got_a, got_b, acc_a, acc_b, local_sems, send_sems, recv_sems):
    me = lax.axis_index("dp")
    mesh_id = pl.DeviceIdType.MESH
    rows = got_a.shape[2]
    bundle = side * rows
    routes = ((a_ref, got_a, side), (b_ref, got_b, 1))
    geo = []
    for _, _, stride in routes:
        coord = lax.rem(me // stride, side)
        geo.append((coord, me - coord * stride))
    barrier = pltpu.get_barrier_semaphore()
    for (coord, base), (_, _, stride) in zip(geo, routes):
        for k in range(1, side):
            peer = base + lax.rem(coord + k, side) * stride
            pl.semaphore_signal(barrier, 1, device_id={"dp": peer}, device_id_type=mesh_id)
    pl.semaphore_wait(barrier, 2 * (side - 1))

    def remote(r, k, source, to):
        src, dst, stride = routes[r]
        coord, base = geo[r]
        return pltpu.make_async_remote_copy(
            src_ref=src,
            dst_ref=dst.at[source],
            send_sem=send_sems.at[r, k - 1],
            recv_sem=recv_sems.at[r, k - 1],
            device_id={"dp": base + to * stride},
            device_id_type=mesh_id,
        )

    locals_, sends = [], []
    for r, (src, dst, stride) in enumerate(routes):
        coord, base = geo[r]
        local = pltpu.make_async_copy(src, dst.at[coord], local_sems.at[r])
        local.start()
        locals_.append(local)
        for k in range(1, side):
            copy = remote(r, k, coord, lax.rem(coord + k, side))
            copy.start()
            sends.append(copy)
    acc_a[...] = jnp.zeros_like(acc_a)
    acc_b[...] = jnp.zeros_like(acc_b)

    def add_a(source):
        block = got_a[source].reshape(bundle, got_a.shape[-1])
        at = pl.ds(pl.multiple_of(source * bundle, bundle), bundle)
        acc_a[...] += jnp.dot(ctx_ref[:, at], block, preferred_element_type=jnp.float32)

    def add_b(source):
        for x in range(side):
            at = pl.ds(pl.multiple_of((x * side + source) * rows, rows), rows)
            acc_b[...] += jnp.dot(ctx_ref[:, at], got_b[source, x], preferred_element_type=jnp.float32)

    for local in locals_:
        local.wait()
    add_a(geo[0][0])
    add_b(geo[1][0])
    for k in range(1, side):
        for r, add in ((0, add_a), (1, add_b)):
            coord, _ = geo[r]
            source = lax.rem(coord + side - k, side)
            remote(r, k, source, source).wait_recv()
            add(source)
    half = acc_a.shape[1]
    n_pieces, n_local, piece = out_ref.shape[:3]
    for b in range(n_local):
        for k in range(n_pieces):
            at = b * n_pieces * piece + k * piece
            out_ref[k, b, :, :half] = (
                res_ref[at:at + piece, :half].astype(jnp.float32) + acc_a[at:at + piece]
            ).astype(out_ref.dtype)
            out_ref[k, b, :, half:] = (
                res_ref[at:at + piece, half:].astype(jnp.float32) + acc_b[at:at + piece]
            ).astype(out_ref.dtype)
    for copy in sends:
        copy.wait_send()


def gather_attend(w, context, residual, cid, layout):
    side = 4
    half = w.shape[-1] // 2
    first_a, first_b = dp_route([w, w], (1, side), cid, gather=True, windows=((0, half), (half, half)))
    vmem = pl.BlockSpec(memory_space=pltpu.VMEM)
    return pl.pallas_call(
        functools.partial(_gather_attend_kernel, side),
        out_shape=jax.ShapeDtypeStruct(layout, jnp.bfloat16),
        in_specs=[pl.BlockSpec(memory_space=pl.ANY)] * 2 + [vmem] * 2,
        out_specs=vmem,
        scratch_shapes=[
            pltpu.VMEM((side,) + first_a.shape, first_a.dtype),
            pltpu.VMEM((side,) + first_b.shape, first_b.dtype),
            pltpu.VMEM((context.shape[0], half), jnp.float32),
            pltpu.VMEM((context.shape[0], half), jnp.float32),
            pltpu.SemaphoreType.DMA((2,)),
            pltpu.SemaphoreType.DMA((2, side - 1)),
            pltpu.SemaphoreType.DMA((2, side - 1)),
        ],
        compiler_params=pltpu.CompilerParams(collective_id=cid + 1, has_side_effects=True),
    )(first_a, first_b, context, residual)


def _spread_kernel(n_dp, n_expert, chosen_ref, split_ref, pieces_ref, mine_ref,
                   held, outgoing, local_sems, dp_send, dp_recv, ex_send, ex_recv):
    me = lax.axis_index("dp")
    mine_e = lax.axis_index("expert")
    mesh_id = pl.DeviceIdType.MESH
    group = split_ref.shape[1]
    barrier = pltpu.get_barrier_semaphore()
    for k in range(1, n_dp):
        pl.semaphore_signal(barrier, 1, device_id={"dp": lax.rem(me + k, n_dp)}, device_id_type=mesh_id)
    for k in range(1, n_expert):
        pl.semaphore_signal(
            barrier, 1, device_id={"expert": lax.rem(mine_e + k, n_expert)}, device_id_type=mesh_id
        )
    pl.semaphore_wait(barrier, n_dp + n_expert - 2)

    def at_source(src):
        return held.at[pl.ds(pl.multiple_of(src * group, group), group)]

    local = pltpu.make_async_copy(split_ref.at[me], at_source(me), local_sems.at[0])
    local.start()
    copies = []
    for k in range(1, n_dp):
        target = lax.rem(me + k, n_dp)
        copy = pltpu.make_async_remote_copy(
            src_ref=split_ref.at[target],
            dst_ref=at_source(me),
            send_sem=dp_send.at[k - 1],
            recv_sem=dp_recv.at[k - 1],
            device_id={"dp": target},
            device_id_type=mesh_id,
        )
        copy.start()
        copies.append(copy)
    local.wait()
    for copy in copies:
        copy.wait()
    keep = pltpu.make_async_copy(held, pieces_ref, local_sems.at[1])
    keep.start()
    rows = held.shape[1]
    width = held.shape[2]
    for e in range(n_expert):
        for s in range(CAP):
            outgoing[e, s * rows:(s + 1) * rows] = held[chosen_ref[e * CAP + s]]
    columns = pl.ds(pl.multiple_of(mine_e * width, width), width)
    local = pltpu.make_async_copy(outgoing.at[mine_e], mine_ref.at[:, columns], local_sems.at[2])
    local.start()
    copies = []
    for k in range(1, n_expert):
        target = lax.rem(mine_e + k, n_expert)
        copy = pltpu.make_async_remote_copy(
            src_ref=outgoing.at[target],
            dst_ref=mine_ref.at[:, columns],
            send_sem=ex_send.at[k - 1],
            recv_sem=ex_recv.at[k - 1],
            device_id={"expert": target},
            device_id_type=mesh_id,
        )
        copy.start()
        copies.append(copy)
    local.wait()
    for copy in copies:
        copy.wait()
    keep.wait()


def spread_select(chosen, split, cid):
    n_dp = lax.axis_size("dp")
    n_expert = lax.axis_size("expert")
    _, group, rows, width = split.shape
    n_blocks = n_dp * group
    return pl.pallas_call(
        functools.partial(_spread_kernel, n_dp, n_expert),
        out_shape=[
            jax.ShapeDtypeStruct((n_blocks, rows, width), split.dtype),
            jax.ShapeDtypeStruct((CAP * rows, n_expert * width), split.dtype),
        ],
        in_specs=[pl.BlockSpec(memory_space=pltpu.SMEM), pl.BlockSpec(memory_space=pl.ANY)],
        out_specs=[pl.BlockSpec(memory_space=pl.ANY)] * 2,
        scratch_shapes=[
            pltpu.VMEM((n_blocks, rows, width), split.dtype),
            pltpu.VMEM((n_expert, CAP * rows, width), split.dtype),
            pltpu.SemaphoreType.DMA((3,)),
            pltpu.SemaphoreType.DMA((n_dp - 1,)),
            pltpu.SemaphoreType.DMA((n_dp - 1,)),
            pltpu.SemaphoreType.DMA((n_expert - 1,)),
            pltpu.SemaphoreType.DMA((n_expert - 1,)),
        ],
        compiler_params=pltpu.CompilerParams(collective_id=cid, has_side_effects=True),
    )(chosen, split)


def body(
    context,
    out_weight,
    residual,
    gate_weight,
    up_weight,
    down_weight,
    gate_values,
    chosen_blocks,
    block_counts,
):
    n_dp = lax.axis_size("dp")
    n_expert = lax.axis_size("expert")
    local_tokens = context.shape[0]
    local_width = residual.shape[1]
    model_width = context.shape[1]
    local_blocks = local_tokens // BLK
    n_blocks = local_blocks * n_dp
    piece = BLK // n_dp
    my_expert = lax.axis_index("expert")

    split = gather_attend(
        out_weight, context, residual, cid=10, layout=(n_dp, local_blocks, BLK // n_dp, local_width)
    )

    pieces, mine = spread_select(chosen_blocks.reshape(-1), split, cid=0)
    w_gate = gate_weight[0]
    w_up = up_weight[0]
    w_down = down_weight[0]
    gate_row = gate_values[0]
    scale = gate_row.reshape(CAP, n_dp, piece).transpose(1, 0, 2).reshape(-1)

    hidden = gather_gate(mine, w_gate, w_up, cid=20)
    halves = down_scatter(block_counts, hidden, w_down, scale[:, None], cid=1)

    outs = reduce_scatter_2d(halves, cid=2)
    outs = outs.reshape(n_expert * CAP, piece * local_width)

    selector = chosen_blocks.reshape(-1)[None, :] == jnp.arange(n_blocks)[:, None]
    added = jnp.dot(selector.astype(jnp.bfloat16), outs, preferred_element_type=jnp.float32)
    mixed = pieces.reshape(n_blocks, piece * local_width).astype(jnp.float32) + added
    mixed = mixed.astype(jnp.bfloat16).reshape(n_dp, local_blocks, piece, local_width)
    back = dp_exchange(mixed, gather=False, cid=3)
    return back.transpose(1, 0, 2, 3).reshape(local_tokens, local_width)


def solution(mesh):
    in_specs = (
        P("dp", None),
        P("dp", "expert"),
        P("dp", "expert"),
        P("expert", None, "dp"),
        P("expert", None, "dp"),
        P("expert", "dp", None),
        P("expert", None),
        P(),
        P(),
    )
    out_specs = P("dp", "expert")
    return jax.shard_map(body, mesh=mesh, in_specs=in_specs, out_specs=out_specs, check_vma=False)
```
